512 devices in a mesh: slab: 32 (over x, z), mode: 16 (over y, core).
Axes of the slice: x: 4, y: 8, z: 8, core: 2. Of those that a mesh axis runs over, the one named last changes fastest.
Arguments:
- design: float32 [64, 128, 128], P('slab', 'mode'), may hold values from 0.03 to 1
- mode_shapes: float32 [16, 3, 64, 128, 128], P('mode', None, 'slab'), may hold values from -2.4 to 2.4
- eigenvalues: float32 [16], P('mode'), may hold values from 0.5 to 2
Outputs:
- sensitivity: float32 [64, 128, 128], P('slab', 'mode')
- new_design: float32 [64, 128, 128], P('slab', 'mode')
The draws below stay inside these ranges and needn't reach their ends.
All inputs are finite; a program needn't handle non-finite values.
Results may differ from the reference program's by a relative error of at most 0.0003.
Values sent between devices are 32-bit elements; how exact they have to be, the bound alone decides.
No kernel may reach another device: no remote copies, remote signals or barrier semaphores. Data moves between devices by JAX's collectives and lax.ppermute only.
A program may use at most 64 MiB of HBM per device.

```python
import math
import jax
import jax.numpy as jnp
import numpy as np
from jax import lax

NY = 128
NZ = 128
FR = 3
BISECT = 12
MODES = 16
NX = 64


def draw_design(key, part):
    across = jnp.arange(NX, dtype=jnp.float32) / NX
    along_rows = jnp.arange(NY, dtype=jnp.float32) / NY
    trend = 0.33 + 0.335 * (across[:, None, None] + along_rows[None, :, None])
    rough = jax.random.uniform(key, (NX, NY, NZ), jnp.float32, 0.1, 1.0)
    return trend * rough


def shard_levels(own_key, dims, cuts, least, top_value):
    level, own = 1.0, jax.random.fold_in(own_key, 6)
    for axis_at, parts in cuts:
        heights = jnp.exp(jax.random.uniform(jax.random.fold_in(own, axis_at), (parts,), jnp.float32, least / len(cuts), top_value / len(cuts)))
        level = level * jnp.repeat(heights, dims[axis_at] // parts).reshape([-1 if axis == axis_at else 1 for axis in range(len(dims))])
    return level


def gaussian(rng, dims, scale, reach, shards=(), kind=jnp.bfloat16):
    level = shard_levels(rng, dims, shards, -0.22, 0.18) if shards else 1.0
    values = jax.random.normal(rng, dims, jnp.float32) * scale * level
    return jnp.minimum(jnp.maximum(values, -reach), reach).astype(kind)


def setup_inputs(seed: int = 0) -> dict:
    streams_of = jax.random.split(jax.random.key(seed), 4)
    return {
        "design": draw_design(jax.random.fold_in(streams_of[3], 71), 0),
        "mode_shapes": gaussian(streams_of[1], (MODES, 3, NX, NY, NZ), 0.3, 2.4, ((0, 16), (2, 32)), jnp.float32),
        "eigenvalues": jnp.clip(jnp.exp(math.log(2.0) - 1.3862944 * jax.random.uniform(streams_of[2], (MODES,), jnp.float32) ** shard_levels(streams_of[2], (MODES,), ((0, 16),), -0.2, 0.2)), 0.5, 2.0),
    }


KS_SHARP = 2.0
PENALTY = 3.0
FLOOR_MODULUS = 0.001
MOVE_LIMIT = 0.2
POISSON = 0.3
LEVEL_LOW = -14.0
LEVEL_HIGH = 14.0

def element_tables():
    lame_first = POISSON / ((1.0 + POISSON) * (1.0 - 2.0 * POISSON))
    shear_modulus = 0.5 / (1.0 + POISSON)
    elastic = np.zeros((6, 6))
    elastic[:3, :3] = lame_first
    for i in range(3):
        elastic[i, i] += 2.0 * shear_modulus
        elastic[i + 3, i + 3] = shear_modulus
    corner_signs = np.array([[a, b, c] for a in (0, 1) for b in (0, 1) for c in (0, 1)]) * 2.0 - 1.0
    gauss_points = [-1.0 / np.sqrt(3.0), 1.0 / np.sqrt(3.0)]
    stiffness = np.zeros((24, 24))
    mass_matrix = np.zeros((24, 24))
    for first in gauss_points:
        for second in gauss_points:
            for third in gauss_points:
                sample = np.array([first, second, third])
                factors = 1.0 + corner_signs * sample
                shape_values = np.prod(factors, axis=1) / 8.0
                gradients = np.zeros((8, 3))
                for d in range(3):
                    others = [e for e in range(3) if e != d]
                    gradients[:, d] = corner_signs[:, d] * factors[:, others[0]] * factors[:, others[1]] / 4.0
                strain = np.zeros((6, 24))
                shape_rows = np.zeros((3, 24))
                for n in range(8):
                    strain[0, 3 * n] = gradients[n, 0]
                    strain[1, 3 * n + 1] = gradients[n, 1]
                    strain[2, 3 * n + 2] = gradients[n, 2]
                    strain[3, 3 * n] = gradients[n, 1]
                    strain[3, 3 * n + 1] = gradients[n, 0]
                    strain[4, 3 * n + 1] = gradients[n, 2]
                    strain[4, 3 * n + 2] = gradients[n, 1]
                    strain[5, 3 * n] = gradients[n, 2]
                    strain[5, 3 * n + 2] = gradients[n, 0]
                    for i in range(3):
                        shape_rows[i, 3 * n + i] = shape_values[n]
                stiffness += strain.T @ elastic @ strain / 8.0
                mass_matrix += shape_rows.T @ shape_rows / 8.0
    return np.concatenate([stiffness, mass_matrix], 0)

def tent_valid(values, along):
    margin = FR - 1
    length = values.shape[along] - 2 * margin
    summed = None
    for offset in range(-margin, margin + 1):
        shifted = (FR - abs(offset)) * lax.slice_in_dim(values, margin + offset, margin + offset + length, axis=along)
        summed = shifted if summed is None else summed + shifted
    return summed

def tent_padded(values, along):
    margin = FR - 1
    widths = [(0, 0)] * values.ndim
    widths[along] = (margin, margin)
    return tent_valid(jnp.pad(values, widths), along)

def smooth(values):
    return tent_padded(tent_padded(tent_padded(values, 2), 0), 1)

def update(design, sensitivity, measure, level):
    factor = jnp.sqrt(jnp.maximum(sensitivity, 0.0) / (jnp.exp(level) * measure))
    return jnp.clip(design * factor, jnp.maximum(design - MOVE_LIMIT, 0.0), jnp.minimum(design + MOVE_LIMIT, 1.0))

def element_forms(node_values, tables):
    padded = jnp.pad(node_values, ((0, 0), (0, 1), (0, 1), (0, 1)))

    def one_layer(position):
        planes = lax.dynamic_slice_in_dim(padded, position, 2, 1)
        corners = []
        for a in (0, 1):
            for b in (0, 1):
                for c in (0, 1):
                    corners.append(planes[:, a, b:b + NY, c:c + NZ])
        stacked = jnp.stack(corners, 0).reshape(24, NY * NZ)
        product = jnp.dot(tables, stacked, precision=lax.Precision.HIGHEST)
        stiff_form = lax.optimization_barrier(jnp.sum(product[:24] * stacked, 0)).reshape(NY, NZ)
        mass_form = lax.optimization_barrier(jnp.sum(product[24:] * stacked, 0)).reshape(NY, NZ)
        return (stiff_form, mass_form)
    return lax.map(one_layer, jnp.arange(NX, dtype=jnp.int32))

def reference(design, mode_shapes, eigenvalues):
    tables = jnp.asarray(element_tables(), jnp.float32)
    span = smooth(jnp.ones_like(design))
    density = smooth(design) / span
    target = jnp.sum(density)
    weights = jnp.exp(-KS_SHARP * eigenvalues)
    summed_weight = jnp.sum(weights)
    slope = PENALTY * (1.0 - FLOOR_MODULUS) * density * density

    def add_mode(number, partial_value):
        stiff_form, mass_form = element_forms(mode_shapes[number], tables)
        return partial_value + weights[number] * (slope * stiff_form - eigenvalues[number] * mass_form)
    partial_value = lax.fori_loop(0, MODES, add_mode, jnp.zeros_like(design))
    gradient = partial_value / summed_weight
    sensitivity = smooth(gradient / span)
    measure = smooth(1.0 / span)

    def halve(count, bounds):
        lower, upper = bounds
        middle = (lower + upper) * 0.5
        volume = jnp.sum(update(design, sensitivity, measure, middle) * measure)
        above = volume > target
        return (jnp.where(above, middle, lower), jnp.where(above, upper, middle))
    start = (jnp.asarray(LEVEL_LOW, jnp.float32), jnp.asarray(LEVEL_HIGH, jnp.float32))
    lower, upper = lax.fori_loop(0, BISECT, halve, start)
    new_design = update(design, sensitivity, measure, (lower + upper) * 0.5)
    return (sensitivity, new_design)
```

```python
import functools

import jax
import jax.numpy as jnp
import numpy as np
from jax import lax
from jax.experimental import pallas as pl
from jax.experimental.pallas import tpu as pltpu
from jax.sharding import PartitionSpec as P

FR = 3
KS_SHARP = 2.0
PENALTY = 3.0
FLOOR_MODULUS = 0.001
MOVE_LIMIT = 0.2
POISSON = 0.3
LEVEL_LOW = -14.0
LEVEL_HIGH = 14.0
FAN = 64
COARSE = (LEVEL_HIGH - LEVEL_LOW) / FAN
FINE = COARSE / FAN
SUB, LANE = 8, 128
F32 = jnp.float32
VMEM = pl.BlockSpec(memory_space=pltpu.VMEM)
SMEM = pl.BlockSpec(memory_space=pltpu.SMEM)


def tent_1d(values):
    padded = np.pad(values, FR - 1)
    n = len(values)
    return sum((FR - abs(o)) * padded[FR - 1 + o : FR - 1 + o + n] for o in range(1 - FR, FR))


def edge_tables(n):
    span = tent_1d(np.ones(n))
    return 1.0 / span, tent_1d(1.0 / span)


def along(position, n, table):
    middle = float(table[n // 2])
    value = jnp.where(position >= 0, F32(middle), F32(0.0))
    for k in range(2 * (FR - 1)):
        if abs(table[k] - middle) > 1e-12:
            value = jnp.where((position == k) | (position == n - 1 - k), F32(table[k]), value)
    return value


def iota(shape, axis):
    return lax.broadcasted_iota(jnp.int32, shape, axis)


def tent_lanes(v):
    lanes = iota(v.shape, v.ndim - 1)
    axis = v.ndim - 1
    total = 3.0 * v
    for o in (1, 2):
        above = jnp.where(lanes < LANE - o, pltpu.roll(v, LANE - o, axis), 0.0)
        below = jnp.where(lanes >= o, pltpu.roll(v, o, axis), 0.0)
        total = total + float(FR - o) * (above + below)
    return total


def forms(load, eigen, store, pairs, tiles):
    lame = POISSON / ((1.0 + POISSON) * (1.0 - 2.0 * POISSON))
    shear = 0.5 / (1.0 + POISSON)
    rows = tiles * SUB
    lanes = iota((rows, LANE), 1)
    for c in range(3):
        for a in (0, 1):
            u = load(c, a)
            up = jnp.where(lanes < LANE - 1, pltpu.roll(u, LANE - 1, 1), 0.0)
            pairs[c, a, 0, :rows] = up + u
            pairs[c, a, 1, :rows] = up - u
            pairs[c, a, :, rows:] = jnp.zeros((2, SUB, LANE), F32)
    eigen_v = jnp.full((SUB, LANE), eigen, F32)
    weight = jnp.exp(-KS_SHARP * eigen_v)
    eigen_weight = weight * eigen_v
    normal = lame + 2.0 * shear
    ms, md = 0.25, 1.0 / 12.0
    m0, m1, m2, m3 = ms**3, ms * ms * md, ms * md * md, md**3

    def tile(r, _):
        base = pl.multiple_of(r * SUB, SUB)
        coef = {}
        for c in range(3):
            planes = []
            for a in (0, 1):
                here = {}
                for z in (0, 1):
                    p0 = pairs[c, a, z, pl.ds(base, SUB)]
                    p1 = pairs[c, a, z, pl.ds(base + 1, SUB)]
                    here[0, z] = p1 + p0
                    here[1, z] = p1 - p0
                planes.append(here)
            for y in (0, 1):
                for z in (0, 1):
                    coef[c, 0, y, z] = planes[1][y, z] + planes[0][y, z]
                    coef[c, 1, y, z] = planes[1][y, z] - planes[0][y, z]
        groups = [None] * 6
        for c in range(3):
            for x in (0, 1):
                for y in (0, 1):
                    for z in (0, 1):
                        d = (x, y, z)
                        n = x + y + z
                        g = {0: 0, 1: 1 if d[c] else 2, 2: 3 if d[c] else 4, 3: 5}[n]
                        v = coef[c, x, y, z]
                        groups[g] = v * v if groups[g] is None else groups[g] + v * v
        mass = m0 * groups[0] + m1 * (groups[1] + groups[2]) + m2 * (groups[3] + groups[4]) + m3 * groups[5]
        stiff = (
            (12.0 * m1 * normal) * groups[1]
            + (12.0 * m1 * shear) * groups[2]
            + (12.0 * m2 * (normal + shear)) * groups[3]
            + (12.0 * m2 * 2.0 * shear) * groups[4]
            + (12.0 * m3 * (normal + 2.0 * shear)) * groups[5]
        )
        for third in (0, 1):
            along_sum = across_sum = None
            for i, j, k in ((0, 1, 2), (0, 2, 1), (1, 2, 0)):

                def at(c, di, dj):
                    d = [0, 0, 0]
                    d[i], d[j], d[k] = di, dj, third
                    return coef[c, d[0], d[1], d[2]]

                t = at(i, 1, 0) * at(j, 0, 1)
                s = at(i, 0, 1) * at(j, 1, 0)
                along_sum = t if along_sum is None else along_sum + t
                across_sum = s if across_sum is None else across_sum + s
            m = (ms, md)[third] * 0.25
            stiff = stiff + (2.0 * lame * m) * along_sum + (2.0 * shear * m) * across_sum
        store(r, weight * stiff, eigen_weight * mass)
        return 0

    lax.fori_loop(0, tiles, tile, 0, unroll=2)
    return weight


def first_layer(modes, eigen, design, out, pairs):
    def store(r, stiff, mass):
        out[r, 0] = stiff
        out[r, 1] = mass

    tiles = out.shape[0]
    weight = forms(lambda c, a: modes[0, c, a], eigen[0], store, pairs, tiles)
    for r in range(tiles):
        out[r, 2] = design[0]
        out[r, 3] = design[1]
        out[r, 4] = weight


def second_layer(modes, plane, eigen, out, pairs):
    def store(r, stiff, mass):
        out[r, 0] = stiff
        out[r, 1] = mass

    def load(c, a):
        return plane[0, c] if a else modes[0, c, 1]

    forms(load, eigen[0], store, pairs, out.shape[0])


def own_sums(got, sums, rows_out, padded, *, mode):
    tiles = got.shape[0]
    m = lax.axis_index(mode)
    for k, at in enumerate((0, 1, 4)):
        total = got[0, at]
        for r in range(1, tiles):
            total = total + got[r, at]
        sums[k] = total
    for l in (0, 1):
        padded[l, :SUB] = jnp.zeros((SUB, LANE), F32)
        padded[l, (tiles + 1) * SUB :] = jnp.zeros((SUB, LANE), F32)
        for r in range(tiles):
            padded[l, (r + 1) * SUB : (r + 2) * SUB] = got[r, 2 + l]
    for l in (0, 1):
        total = None
        for o in range(1 - FR, FR):
            t = float(FR - abs(o)) * padded[l, pl.ds(m * SUB + SUB + o, SUB)]
            total = t if total is None else total + t
        rows_out[l] = tent_lanes(total)


def across_x(own, before, after):
    first = before[0] + 2.0 * before[1] + 3.0 * own[0] + 2.0 * own[1] + after[0]
    second = before[1] + 2.0 * own[0] + 3.0 * own[1] + 2.0 * after[0] + after[1]
    return first, second


def own_gradient(got, sums, rows, before, after, out, *, slab, mode, sizes):
    total_x, total_y, total_z = sizes
    tiles = got.shape[0]
    s, m = lax.axis_index(slab), lax.axis_index(mode)
    later = []
    for at in (0, 1):
        total = got[0, at]
        for r in range(1, tiles):
            total = total + got[r, at]
        later.append(total)
    stiff = (sums[0], later[0])
    mass = (sums[1], later[1])
    inverse_yz = along(m * SUB + iota((SUB, LANE), 0), total_y, edge_tables(total_y)[0]) * along(
        iota((SUB, LANE), 1), total_z, edge_tables(total_z)[0]
    )
    filtered = across_x(rows, before, after)
    inverse_weight = 1.0 / sums[2]
    for l in (0, 1):
        x = jnp.full((SUB, LANE), 2 * s + l, jnp.int32)
        inverse = inverse_yz * along(x, total_x, edge_tables(total_x)[0])
        density = filtered[l] * inverse
        slope = (PENALTY * (1.0 - FLOOR_MODULUS)) * density * density
        out[l] = tent_lanes((slope * stiff[l] - mass[l]) * inverse_weight * inverse)


def gradient_copies(own, before, after, out):
    pair = across_x(own, before, after)
    for r in range(out.shape[0]):
        out[r, 0] = pair[0]
        out[r, 1] = pair[1]


def measure_xz(slab, total_x, total_z):
    s = lax.axis_index(slab)
    z = along(iota((SUB, LANE), 1), total_z, edge_tables(total_z)[1])
    return [
        z * along(jnp.full((SUB, LANE), 2 * s + l, jnp.int32), total_x, edge_tables(total_x)[1])
        for l in (0, 1)
    ]


def volumes(levels, gain, least, most, parts):
    count = gain.shape[0]
    for start in range(0, len(levels), 8):
        chunk = levels[start : start + 8]

        def body(v, totals):
            g, lo, hi = gain[v], least[v], most[v]
            return tuple(
                t + jnp.minimum(jnp.maximum(g * q, lo), hi) for t, q in zip(totals, chunk)
            )

        zeros = tuple(jnp.zeros((SUB, LANE), F32) for _ in chunk)
        totals = lax.fori_loop(0, count, body, zeros, unroll=4)
        for i, t in enumerate(totals):
            parts[start + i : start + i + 1] = jnp.sum(t, axis=0, keepdims=True)


def lane_totals(parts):
    column = jnp.sum(parts[...], axis=1, keepdims=True)
    shape = (FAN, LANE)
    spread = jnp.where(iota(shape, 0) == iota(shape, 1), jnp.broadcast_to(column, shape), 0.0)
    return jnp.sum(spread, axis=0, keepdims=True)


def first_round(got, early, gain, least, most, own, out, padded, parts, *, slab, mode, sizes):
    total_x, total_y, total_z = sizes
    tiles = got.shape[0]
    m = lax.axis_index(mode)
    for l in (0, 1):
        padded[l, :SUB] = jnp.zeros((SUB, LANE), F32)
        padded[l, (tiles + 1) * SUB :] = jnp.zeros((SUB, LANE), F32)
        for r in range(tiles):
            padded[l, (r + 1) * SUB : (r + 2) * SUB] = got[r, l]
    xz = measure_xz(slab, total_x, total_z)
    goal = jnp.zeros((SUB, LANE), F32)
    for l in (0, 1):
        for r in range(tiles):
            total = None
            for o in range(1 - FR, FR):
                start = (r + 1) * SUB + o
                t = float(FR - abs(o)) * padded[l, start : start + SUB]
                total = t if total is None else total + t
            measure = xz[l] * along(r * SUB + iota((SUB, LANE), 0), total_y, edge_tables(total_y)[1])
            design = early[r, 2 + l]
            at = l * tiles + r
            gain[at] = design * jnp.sqrt(jnp.maximum(total, 0.0) * measure)
            least[at] = jnp.maximum(design - MOVE_LIMIT, 0.0) * measure
            most[at] = jnp.minimum(design + MOVE_LIMIT, 1.0) * measure
            goal = goal + design * measure
        total = None
        for o in range(1 - FR, FR):
            t = float(FR - abs(o)) * padded[l, pl.ds(m * SUB + SUB + o, SUB)]
            total = t if total is None else total + t
        own[l] = total
    levels = [float(np.exp(-0.5 * (LEVEL_LOW + COARSE * (i + 1)))) for i in range(FAN - 1)]
    volumes(levels, gain, least, most, parts)
    parts[FAN - 1 : FAN] = jnp.sum(goal, axis=0, keepdims=True)
    row = lane_totals(parts)
    for k in range(out.shape[0]):
        out[k] = row


def added(got):
    total = got[0]
    for k in range(1, got.shape[0]):
        total = total + got[k]
    return total


def at_lane(row, k):
    return jnp.sum(jnp.where(iota(row.shape, 1) == k, row, 0.0), axis=1, keepdims=True)


def cells_above(row, goal):
    above = (row > goal) & (iota(row.shape, 1) < FAN - 1)
    return jnp.sum(jnp.where(above, 1.0, 0.0), axis=1, keepdims=True)


def second_round(got, gain, least, most, out, state, parts):
    row = added(got)
    goal = at_lane(row, FAN - 1)
    low = LEVEL_LOW + COARSE * cells_above(row, goal)
    state[0:1] = jnp.broadcast_to(low, (1, LANE))
    state[1:2] = jnp.broadcast_to(goal, (1, LANE))
    scale = jnp.exp(-0.5 * jnp.broadcast_to(low, (SUB, LANE)))
    levels = [scale * float(np.exp(-0.5 * FINE * (i + 1))) for i in range(FAN - 1)]
    volumes(levels, gain, least, most, parts)
    parts[FAN - 1 : FAN] = jnp.zeros((1, LANE), F32)
    row = lane_totals(parts)
    for k in range(out.shape[0]):
        out[k] = row


def last_update(got, state, own, design, sens_out, out, *, slab, mode, sizes):
    total_x, total_y, total_z = sizes
    m = lax.axis_index(mode)
    row = added(got)
    goal = state[1:2, 0:1]
    level = state[0:1, 0:1] + FINE * (cells_above(row, goal) + 0.5)
    scale = jnp.exp(jnp.broadcast_to(level, (SUB, LANE)))
    y = along(m * SUB + iota((SUB, LANE), 0), total_y, edge_tables(total_y)[1])
    xz = measure_xz(slab, total_x, total_z)
    for l in (0, 1):
        d, s = design[l], own[l]
        factor = jnp.sqrt(jnp.maximum(s, 0.0) / (scale * (xz[l] * y)))
        least = jnp.maximum(d - MOVE_LIMIT, 0.0)
        most = jnp.minimum(d + MOVE_LIMIT, 1.0)
        out[l] = jnp.minimum(jnp.maximum(d * factor, least), most)
        sens_out[l] = s


def call(kernel, outs, operands, specs=None, scratch=(), flops=1000, name=None):
    outs = [jax.ShapeDtypeStruct(o, F32) for o in outs]
    size = sum(4 * int(np.prod(o.shape)) for o in (*outs, *operands))
    single = len(outs) == 1
    return pl.pallas_call(
        kernel,
        out_shape=outs[0] if single else outs,
        in_specs=specs or [VMEM] * len(operands),
        out_specs=VMEM if single else [VMEM] * len(outs),
        scratch_shapes=[pltpu.VMEM(s, F32) for s in scratch],
        cost_estimate=pl.CostEstimate(flops=flops, bytes_accessed=size, transcendentals=0),
        name=name,
    )(*operands)


def neighbours(value, axis):
    count = lax.axis_size(axis)
    up = [(i, i + 1) for i in range(count - 1)]
    down = [(j, i) for i, j in up]
    return lax.ppermute(value, axis, up), lax.ppermute(value, axis, down)


def exchange(value, axis):
    return lax.all_to_all(value, axis, 0, 0, tiled=True)


def local(design, mode_shapes, eigenvalues):
    slab, mode = "slab", "mode"
    slabs, modes = lax.axis_size(slab), lax.axis_size(mode)
    _, _, _, total_y, total_z = mode_shapes.shape
    sizes = (2 * slabs, total_y, total_z)
    pairs = (3, 2, 2, total_y + SUB, LANE)
    block = (2, SUB, LANE)
    padded = (2, total_y + 2 * SUB, LANE)
    place = dict(slab=slab, mode=mode, sizes=sizes)

    down = [(i + 1, i) for i in range(slabs - 1)]
    plane = lax.ppermute(mode_shapes[:, :, 0], slab, down)
    early = call(
        first_layer,
        [(modes, 5, SUB, LANE)],
        [mode_shapes, eigenvalues, design],
        specs=[VMEM, SMEM, VMEM],
        scratch=[pairs],
        flops=5_000_000,
        name="first_layer",
    )
    early = exchange(early, mode)
    late = call(
        second_layer,
        [(modes, 2, SUB, LANE)],
        [mode_shapes, plane, eigenvalues],
        specs=[VMEM, VMEM, SMEM],
        scratch=[pairs],
        flops=5_000_000,
        name="second_layer",
    )
    late = exchange(late, mode)
    sums, rows = call(
        functools.partial(own_sums, mode=mode),
        [(3, SUB, LANE), block],
        [early],
        scratch=[padded],
        name="own_sums",
    )
    before, after = neighbours(rows, slab)
    gradient = call(
        functools.partial(own_gradient, **place),
        [block],
        [late, sums, rows, before, after],
        name="own_gradient",
    )
    before, after = neighbours(gradient, slab)
    copies = call(gradient_copies, [(modes, *block)], [gradient, before, after], name="copies")
    whole = exchange(copies, mode)
    vectors = 2 * modes
    gain, least, most, own, sent = call(
        functools.partial(first_round, **place),
        [(vectors, SUB, LANE)] * 3 + [block, (slabs, 1, LANE)],
        [whole, early],
        scratch=[padded, (FAN, LANE)],
        name="first_round",
    )
    got = exchange(sent, slab)
    sent, state = call(
        second_round,
        [(slabs, 1, LANE), (SUB, LANE)],
        [got, gain, least, most],
        scratch=[(FAN, LANE)],
        name="second_round",
    )
    got = exchange(sent, slab)
    return call(
        functools.partial(last_update, **place),
        [block, block],
        [got, state, own, design],
        name="last_update",
    )


def solution(mesh):
    in_specs = (P("slab", "mode", None), P("mode", None, "slab", None, None), P("mode"))
    out_specs = (P("slab", "mode", None), P("slab", "mode", None))

    def step(design, mode_shapes, eigenvalues):
        return tuple(local(design, mode_shapes, eigenvalues))

    return jax.shard_map(step, mesh=mesh, in_specs=in_specs, out_specs=out_specs, check_vma=False)
```

```python
import functools

import jax
import jax.numpy as jnp
import numpy as np
from jax import lax
from jax.experimental import pallas as pl
from jax.experimental.pallas import tpu as pltpu
from jax.sharding import PartitionSpec as P


FR = 3
KS_SHARP = 2.0
PENALTY = 3.0
FLOOR_MODULUS = 0.001
MOVE_LIMIT = 0.2
POISSON = 0.3
LEVEL_LOW = -14.0
LEVEL_HIGH = 14.0
FAN = 64
COARSE = (LEVEL_HIGH - LEVEL_LOW) / FAN
FINE = COARSE / FAN
SUB, LANE = 8, 128
GRANT = 8 * 1024 * 1024
F32 = jnp.float32
VMEM = pl.BlockSpec(memory_space=pltpu.VMEM)
SMEM = pl.BlockSpec(memory_space=pltpu.SMEM)


def tent_1d(values):
    padded = np.pad(values, FR - 1)
    n = len(values)
    return sum((FR - abs(o)) * padded[FR - 1 + o : FR - 1 + o + n] for o in range(1 - FR, FR))


def edge_tables(n):
    span = tent_1d(np.ones(n))
    return 1.0 / span, tent_1d(1.0 / span)


def along(position, n, table):
    middle = float(table[n // 2])
    value = jnp.where(position >= 0, F32(middle), F32(0.0))
    for k in range(2 * (FR - 1)):
        if abs(table[k] - middle) > 1e-12:
            value = jnp.where((position == k) | (position == n - 1 - k), F32(table[k]), value)
    return value


def iota(shape, axis):
    return lax.broadcasted_iota(jnp.int32, shape, axis)


def tent_lanes(v):
    lanes = iota(v.shape, v.ndim - 1)
    axis = v.ndim - 1
    total = 3.0 * v
    for o in (1, 2):
        above = jnp.where(lanes < LANE - o, pltpu.roll(v, LANE - o, axis), 0.0)
        below = jnp.where(lanes >= o, pltpu.roll(v, o, axis), 0.0)
        total = total + float(FR - o) * (above + below)
    return total


def forms(load, eigen, store, pairs, tiles):
    lame = POISSON / ((1.0 + POISSON) * (1.0 - 2.0 * POISSON))
    shear = 0.5 / (1.0 + POISSON)
    rows = tiles * SUB
    lanes = iota((rows, LANE), 1)
    for c in range(3):
        for a in (0, 1):
            u = load(c, a)
            up = jnp.where(lanes < LANE - 1, pltpu.roll(u, LANE - 1, 1), 0.0)
            pairs[c, a, 0, :rows] = up + u
            pairs[c, a, 1, :rows] = up - u
            pairs[c, a, :, rows:] = jnp.zeros((2, SUB, LANE), F32)
    eigen_v = jnp.full((SUB, LANE), eigen, F32)
    weight = jnp.exp(-KS_SHARP * eigen_v)
    eigen_weight = weight * eigen_v
    normal = lame + 2.0 * shear
    ms, md = 0.25, 1.0 / 12.0
    m0, m1, m2, m3 = ms**3, ms * ms * md, ms * md * md, md**3

    def tile(r, _):
        base = pl.multiple_of(r * SUB, SUB)
        coef = {}
        for c in range(3):
            planes = []
            for a in (0, 1):
                here = {}
                for z in (0, 1):
                    p0 = pairs[c, a, z, pl.ds(base, SUB)]
                    p1 = pairs[c, a, z, pl.ds(base + 1, SUB)]
                    here[0, z] = p1 + p0
                    here[1, z] = p1 - p0
                planes.append(here)
            for y in (0, 1):
                for z in (0, 1):
                    coef[c, 0, y, z] = planes[1][y, z] + planes[0][y, z]
                    coef[c, 1, y, z] = planes[1][y, z] - planes[0][y, z]
        groups = [None] * 6
        for c in range(3):
            for x in (0, 1):
                for y in (0, 1):
                    for z in (0, 1):
                        d = (x, y, z)
                        n = x + y + z
                        g = {0: 0, 1: 1 if d[c] else 2, 2: 3 if d[c] else 4, 3: 5}[n]
                        v = coef[c, x, y, z]
                        groups[g] = v * v if groups[g] is None else groups[g] + v * v
        mass = m0 * groups[0] + m1 * (groups[1] + groups[2]) + m2 * (groups[3] + groups[4]) + m3 * groups[5]
        stiff = (
            (12.0 * m1 * normal) * groups[1]
            + (12.0 * m1 * shear) * groups[2]
            + (12.0 * m2 * (normal + shear)) * groups[3]
            + (12.0 * m2 * 2.0 * shear) * groups[4]
            + (12.0 * m3 * (normal + 2.0 * shear)) * groups[5]
        )
        for third in (0, 1):
            along_sum = across_sum = None
            for i, j, k in ((0, 1, 2), (0, 2, 1), (1, 2, 0)):

                def at(c, di, dj):
                    d = [0, 0, 0]
                    d[i], d[j], d[k] = di, dj, third
                    return coef[c, d[0], d[1], d[2]]

                t = at(i, 1, 0) * at(j, 0, 1)
                s = at(i, 0, 1) * at(j, 1, 0)
                along_sum = t if along_sum is None else along_sum + t
                across_sum = s if across_sum is None else across_sum + s
            m = (ms, md)[third] * 0.25
            stiff = stiff + (2.0 * lame * m) * along_sum + (2.0 * shear * m) * across_sum
        store(r, weight * stiff, eigen_weight * mass)
        return 0

    lax.fori_loop(0, tiles, tile, 0, unroll=2)
    return weight


def first_layer(modes, eigen, design, out, pairs):
    def store(r, stiff, mass):
        out[r, 0] = stiff
        out[r, 1] = mass

    tiles = out.shape[0]
    weight = forms(lambda c, a: modes[0, c, a], eigen[0], store, pairs, tiles)
    for r in range(tiles):
        out[r, 2] = design[0]
        out[r, 3] = design[1]
        out[r, 4] = weight


def shifted_rows(v, o):
    rows = iota(v.shape, 0)
    moved = pltpu.roll(v, (-o) % SUB, 0)
    return jnp.where((rows + o >= 0) & (rows + o < SUB), moved, 0.0)


def edge_rows(first, second):
    zero = jnp.zeros((4, LANE), F32)
    up, down = [], []
    for f in (first, second):
        up += [2.0 * f[7:8] + f[6:7], f[7:8]]
        down += [f[0:1], 2.0 * f[0:1] + f[1:2]]
    return jnp.concatenate([*up, zero], 0), jnp.concatenate([zero, *down], 0)


def second_layer(modes, plane, eigen, design, before, after, out, rows, pairs, *, mode):
    def store(r, stiff, mass):
        out[r, 0] = stiff
        out[r, 1] = mass

    def load(c, a):
        return plane[0, c] if a else modes[0, c, 1]

    m = lax.axis_index(mode)
    tiles = out.shape[0]
    pair = across_x(design, before, after)
    up, down = edge_rows(*pair)
    for l in (0, 1):
        rows[l] = pair[l]
    for r in range(tiles):
        to_next = jnp.where(m + 1 == r, F32(1.0), F32(0.0))
        to_last = jnp.where(m - 1 == r, F32(1.0), F32(0.0))
        out[r, 2] = up * to_next + down * to_last
    forms(load, eigen[0], store, pairs, tiles)


def across_x(own, before, after):
    first = before[0] + 2.0 * before[1] + 3.0 * own[0] + 2.0 * own[1] + after[0]
    second = before[1] + 2.0 * own[0] + 3.0 * own[1] + 2.0 * after[0] + after[1]
    return first, second


def over_modes(got, at):
    total = got[0, at]
    for r in range(1, got.shape[0]):
        total = total + got[r, at]
    return total


def own_gradient(early, late, rows, out, *, slab, mode, sizes):
    total_x, total_y, total_z = sizes
    s, m = lax.axis_index(slab), lax.axis_index(mode)
    stiff = (over_modes(early, 0), over_modes(late, 0))
    mass = (over_modes(early, 1), over_modes(late, 1))
    inverse_weight = 1.0 / over_modes(early, 4)
    edges = over_modes(late, 2)
    inverse_yz = along(m * SUB + iota((SUB, LANE), 0), total_y, edge_tables(total_y)[0]) * along(
        iota((SUB, LANE), 1), total_z, edge_tables(total_z)[0]
    )
    for l in (0, 1):
        own = rows[l]
        near = jnp.concatenate(
            [edges[2 * l : 2 * l + 2], jnp.zeros((4, LANE), F32), edges[4 + 2 * l : 6 + 2 * l]], 0
        )
        filtered = near
        for o in range(1 - FR, FR):
            filtered = filtered + float(FR - abs(o)) * (shifted_rows(own, o) if o else own)
        x = jnp.full((SUB, LANE), 2 * s + l, jnp.int32)
        inverse = inverse_yz * along(x, total_x, edge_tables(total_x)[0])
        density = tent_lanes(filtered) * inverse
        slope = (PENALTY * (1.0 - FLOOR_MODULUS)) * density * density
        out[l] = tent_lanes((slope * stiff[l] - mass[l]) * inverse_weight * inverse)


def gradient_copies(own, before, after, out):
    pair = across_x(own, before, after)
    for r in range(out.shape[0]):
        out[r, 0] = pair[0]
        out[r, 1] = pair[1]


def measure_xz(slab, total_x, total_z):
    s = lax.axis_index(slab)
    z = along(iota((SUB, LANE), 1), total_z, edge_tables(total_z)[1])
    return [
        z * along(jnp.full((SUB, LANE), 2 * s + l, jnp.int32), total_x, edge_tables(total_x)[1])
        for l in (0, 1)
    ]


def volumes(levels, gain, least, most, parts):
    count = gain.shape[0]
    for start in range(0, len(levels), 8):
        chunk = levels[start : start + 8]

        def body(v, totals):
            g, lo, hi = gain[v], least[v], most[v]
            return tuple(
                t + jnp.minimum(jnp.maximum(g * q, lo), hi) for t, q in zip(totals, chunk)
            )

        zeros = tuple(jnp.zeros((SUB, LANE), F32) for _ in chunk)
        totals = lax.fori_loop(0, count, body, zeros, unroll=4)
        for i, t in enumerate(totals):
            parts[start + i : start + i + 1] = jnp.sum(t, axis=0, keepdims=True)


def lane_totals(parts):
    column = jnp.sum(parts[...], axis=1, keepdims=True)
    shape = (FAN, LANE)
    spread = jnp.where(iota(shape, 0) == iota(shape, 1), jnp.broadcast_to(column, shape), 0.0)
    return jnp.sum(spread, axis=0, keepdims=True)


def first_round(got, early, gain, least, most, own, out, padded, parts, *, slab, mode, sizes):
    total_x, total_y, total_z = sizes
    tiles = got.shape[0]
    m = lax.axis_index(mode)
    for l in (0, 1):
        padded[l, :SUB] = jnp.zeros((SUB, LANE), F32)
        padded[l, (tiles + 1) * SUB :] = jnp.zeros((SUB, LANE), F32)
        for r in range(tiles):
            padded[l, (r + 1) * SUB : (r + 2) * SUB] = got[r, l]
    xz = measure_xz(slab, total_x, total_z)
    goal = jnp.zeros((SUB, LANE), F32)
    for l in (0, 1):
        for r in range(tiles):
            total = None
            for o in range(1 - FR, FR):
                start = (r + 1) * SUB + o
                t = float(FR - abs(o)) * padded[l, start : start + SUB]
                total = t if total is None else total + t
            measure = xz[l] * along(r * SUB + iota((SUB, LANE), 0), total_y, edge_tables(total_y)[1])
            design = early[r, 2 + l]
            at = l * tiles + r
            gain[at] = design * jnp.sqrt(jnp.maximum(total, 0.0) * measure)
            least[at] = jnp.maximum(design - MOVE_LIMIT, 0.0) * measure
            most[at] = jnp.minimum(design + MOVE_LIMIT, 1.0) * measure
            goal = goal + design * measure
        total = None
        for o in range(1 - FR, FR):
            t = float(FR - abs(o)) * padded[l, pl.ds(m * SUB + SUB + o, SUB)]
            total = t if total is None else total + t
        own[l] = total
    levels = [float(np.exp(-0.5 * (LEVEL_LOW + COARSE * (i + 1)))) for i in range(FAN - 1)]
    volumes(levels, gain, least, most, parts)
    parts[FAN - 1 : FAN] = jnp.sum(goal, axis=0, keepdims=True)
    row = lane_totals(parts)
    for k in range(out.shape[0]):
        out[k] = row


def added(got):
    total = got[0]
    for k in range(1, got.shape[0]):
        total = total + got[k]
    return total


def at_lane(row, k):
    return jnp.sum(jnp.where(iota(row.shape, 1) == k, row, 0.0), axis=1, keepdims=True)


def cells_above(row, goal):
    above = (row > goal) & (iota(row.shape, 1) < FAN - 1)
    return jnp.sum(jnp.where(above, 1.0, 0.0), axis=1, keepdims=True)


def second_round(got, gain, least, most, out, state, parts):
    row = added(got)
    goal = at_lane(row, FAN - 1)
    low = LEVEL_LOW + COARSE * cells_above(row, goal)
    state[0:1] = jnp.broadcast_to(low, (1, LANE))
    state[1:2] = jnp.broadcast_to(goal, (1, LANE))
    scale = jnp.exp(-0.5 * jnp.broadcast_to(low, (SUB, LANE)))
    levels = [scale * float(np.exp(-0.5 * FINE * (i + 1))) for i in range(FAN - 1)]
    volumes(levels, gain, least, most, parts)
    parts[FAN - 1 : FAN] = jnp.zeros((1, LANE), F32)
    row = lane_totals(parts)
    for k in range(out.shape[0]):
        out[k] = row


def last_update(got, state, own, design, sens_out, out, *, slab, mode, sizes):
    total_x, total_y, total_z = sizes
    m = lax.axis_index(mode)
    row = added(got)
    goal = state[1:2, 0:1]
    level = state[0:1, 0:1] + FINE * (cells_above(row, goal) + 0.5)
    scale = jnp.exp(jnp.broadcast_to(level, (SUB, LANE)))
    y = along(m * SUB + iota((SUB, LANE), 0), total_y, edge_tables(total_y)[1])
    xz = measure_xz(slab, total_x, total_z)
    for l in (0, 1):
        d, s = design[l], own[l]
        factor = jnp.sqrt(jnp.maximum(s, 0.0) / (scale * (xz[l] * y)))
        least = jnp.maximum(d - MOVE_LIMIT, 0.0)
        most = jnp.minimum(d + MOVE_LIMIT, 1.0)
        out[l] = jnp.minimum(jnp.maximum(d * factor, least), most)
        sens_out[l] = s


def call(kernel, outs, operands, specs=None, scratch=(), flops=1000):
    outs = [jax.ShapeDtypeStruct(o, F32) for o in outs]
    size = sum(4 * int(np.prod(o.shape)) for o in (*outs, *operands))
    single = len(outs) == 1
    return pl.pallas_call(
        kernel,
        out_shape=outs[0] if single else outs,
        in_specs=specs or [VMEM] * len(operands),
        out_specs=VMEM if single else [VMEM] * len(outs),
        scratch_shapes=[pltpu.VMEM(s, F32) for s in scratch],
        cost_estimate=pl.CostEstimate(flops=flops, bytes_accessed=size, transcendentals=0),
        compiler_params=pltpu.CompilerParams(vmem_limit_bytes=GRANT),
    )(*operands)


def neighbours(value, axis):
    count = lax.axis_size(axis)
    up = [(i, i + 1) for i in range(count - 1)]
    down = [(j, i) for i, j in up]
    before = lax.ppermute(value, axis, up)
    after = lax.ppermute(value, axis, down)
    return before, after


def exchange(value, axis):
    return lax.all_to_all(value, axis, 0, 0, tiled=True)


def local(design, mode_shapes, eigenvalues):
    slab, mode = "slab", "mode"
    slabs, modes = lax.axis_size(slab), lax.axis_size(mode)
    _, _, _, total_y, total_z = mode_shapes.shape
    sizes = (2 * slabs, total_y, total_z)
    pairs = (3, 2, 2, total_y + SUB, LANE)
    block = (2, SUB, LANE)
    padded = (2, total_y + 2 * SUB, LANE)
    place = dict(slab=slab, mode=mode, sizes=sizes)

    down = [(i + 1, i) for i in range(slabs - 1)]
    plane = lax.ppermute(mode_shapes[:, :, 0], slab, down)
    before, after = neighbours(design, slab)
    early = call(
        first_layer,
        [(modes, 5, SUB, LANE)],
        [mode_shapes, eigenvalues, design],
        specs=[VMEM, SMEM, VMEM],
        scratch=[pairs],
        flops=5_000_000,
    )
    early = exchange(early, mode)
    late, rows = call(
        functools.partial(second_layer, mode=mode),
        [(modes, 3, SUB, LANE), block],
        [mode_shapes, plane, eigenvalues, design, before, after],
        specs=[VMEM, VMEM, SMEM, VMEM, VMEM, VMEM],
        scratch=[pairs],
        flops=5_000_000,
    )
    late = exchange(late, mode)
    gradient = call(functools.partial(own_gradient, **place), [block], [early, late, rows])
    before, after = neighbours(gradient, slab)
    copies = call(gradient_copies, [(modes, *block)], [gradient, before, after])
    whole = exchange(copies, mode)
    vectors = 2 * modes
    gain, least, most, own, sent = call(
        functools.partial(first_round, **place),
        [(vectors, SUB, LANE)] * 3 + [block, (slabs, 1, LANE)],
        [whole, early],
        scratch=[padded, (FAN, LANE)],
    )
    got = exchange(sent, slab)
    sent, state = call(
        second_round,
        [(slabs, 1, LANE), (SUB, LANE)],
        [got, gain, least, most],
        scratch=[(FAN, LANE)],
    )
    got = exchange(sent, slab)
    return call(functools.partial(last_update, **place), [block, block], [got, state, own, design])


def solution(mesh):
    in_specs = (P("slab", "mode", None), P("mode", None, "slab", None, None), P("mode"))
    out_specs = (P("slab", "mode", None), P("slab", "mode", None))

    def step(design, mode_shapes, eigenvalues):
        return tuple(local(design, mode_shapes, eigenvalues))

    return jax.shard_map(step, mesh=mesh, in_specs=in_specs, out_specs=out_specs, check_vma=False)
```

```python
import functools

import jax
import jax.numpy as jnp
import numpy as np
from jax import lax
from jax.experimental import pallas as pl
from jax.experimental.pallas import tpu as pltpu
from jax.sharding import PartitionSpec as P


FR = 3
KS_SHARP = 2.0
PENALTY = 3.0
FLOOR_MODULUS = 0.001
MOVE_LIMIT = 0.2
POISSON = 0.3
LEVEL_LOW = -14.0
LEVEL_HIGH = 14.0
FAN = 64
COARSE = (LEVEL_HIGH - LEVEL_LOW) / FAN
FINE = COARSE / FAN
SUB, LANE = 8, 128
GRANT = 8 * 1024 * 1024
F32 = jnp.float32
VMEM = pl.BlockSpec(memory_space=pltpu.VMEM)
SMEM = pl.BlockSpec(memory_space=pltpu.SMEM)


def tent_1d(values):
    padded = np.pad(values, FR - 1)
    n = len(values)
    return sum((FR - abs(o)) * padded[FR - 1 + o : FR - 1 + o + n] for o in range(1 - FR, FR))


def edge_tables(n):
    span = tent_1d(np.ones(n))
    return 1.0 / span, tent_1d(1.0 / span)


def along(position, n, table):
    middle = float(table[n // 2])
    value = jnp.where(position >= 0, F32(middle), F32(0.0))
    for k in range(2 * (FR - 1)):
        if abs(table[k] - middle) > 1e-12:
            value = jnp.where((position == k) | (position == n - 1 - k), F32(table[k]), value)
    return value


def iota(shape, axis):
    return lax.broadcasted_iota(jnp.int32, shape, axis)


def tent_lanes(v):
    lanes = iota(v.shape, v.ndim - 1)
    axis = v.ndim - 1
    total = 3.0 * v
    for o in (1, 2):
        above = jnp.where(lanes < LANE - o, pltpu.roll(v, LANE - o, axis), 0.0)
        below = jnp.where(lanes >= o, pltpu.roll(v, o, axis), 0.0)
        total = total + float(FR - o) * (above + below)
    return total


def forms(load, eigen, store, pairs, tiles):
    lame = POISSON / ((1.0 + POISSON) * (1.0 - 2.0 * POISSON))
    shear = 0.5 / (1.0 + POISSON)
    rows = tiles * SUB
    lanes = iota((rows, LANE), 1)
    for c in range(3):
        for a in (0, 1):
            u = load(c, a)
            up = jnp.where(lanes < LANE - 1, pltpu.roll(u, LANE - 1, 1), 0.0)
            pairs[c, a, 0, :rows] = up + u
            pairs[c, a, 1, :rows] = up - u
            pairs[c, a, :, rows:] = jnp.zeros((2, SUB, LANE), F32)
    eigen_v = jnp.full((SUB, LANE), eigen, F32)
    weight = jnp.exp(-KS_SHARP * eigen_v)
    eigen_weight = weight * eigen_v
    normal = lame + 2.0 * shear
    ms, md = 0.25, 1.0 / 12.0
    m0, m1, m2, m3 = ms**3, ms * ms * md, ms * md * md, md**3

    def tile(r, _):
        base = pl.multiple_of(r * SUB, SUB)
        coef = {}
        for c in range(3):
            planes = []
            for a in (0, 1):
                here = {}
                for z in (0, 1):
                    p0 = pairs[c, a, z, pl.ds(base, SUB)]
                    p1 = pairs[c, a, z, pl.ds(base + 1, SUB)]
                    here[0, z] = p1 + p0
                    here[1, z] = p1 - p0
                planes.append(here)
            for y in (0, 1):
                for z in (0, 1):
                    coef[c, 0, y, z] = planes[1][y, z] + planes[0][y, z]
                    coef[c, 1, y, z] = planes[1][y, z] - planes[0][y, z]
        groups = [None] * 6
        for c in range(3):
            for x in (0, 1):
                for y in (0, 1):
                    for z in (0, 1):
                        d = (x, y, z)
                        n = x + y + z
                        g = {0: 0, 1: 1 if d[c] else 2, 2: 3 if d[c] else 4, 3: 5}[n]
                        v = coef[c, x, y, z]
                        groups[g] = v * v if groups[g] is None else groups[g] + v * v
        mass = m0 * groups[0] + m1 * (groups[1] + groups[2]) + m2 * (groups[3] + groups[4]) + m3 * groups[5]
        stiff = (
            (12.0 * m1 * normal) * groups[1]
            + (12.0 * m1 * shear) * groups[2]
            + (12.0 * m2 * (normal + shear)) * groups[3]
            + (12.0 * m2 * 2.0 * shear) * groups[4]
            + (12.0 * m3 * (normal + 2.0 * shear)) * groups[5]
        )
        for third in (0, 1):
            along_sum = across_sum = None
            for i, j, k in ((0, 1, 2), (0, 2, 1), (1, 2, 0)):

                def at(c, di, dj):
                    d = [0, 0, 0]
                    d[i], d[j], d[k] = di, dj, third
                    return coef[c, d[0], d[1], d[2]]

                t = at(i, 1, 0) * at(j, 0, 1)
                s = at(i, 0, 1) * at(j, 1, 0)
                along_sum = t if along_sum is None else along_sum + t
                across_sum = s if across_sum is None else across_sum + s
            m = (ms, md)[third] * 0.25
            stiff = stiff + (2.0 * lame * m) * along_sum + (2.0 * shear * m) * across_sum
        store(r, weight * stiff, eigen_weight * mass)
        return 0

    lax.fori_loop(0, tiles, tile, 0, unroll=2)
    return weight


def first_layer(modes, eigen, design, out, pairs):
    def store(r, stiff, mass):
        out[r, 0] = stiff
        out[r, 1] = mass

    tiles = out.shape[0]
    weight = forms(lambda c, a: modes[0, c, a], eigen[0], store, pairs, tiles)
    for r in range(tiles):
        out[r, 4] = design[0]
        out[r, 5] = design[1]
        out[r, 6] = weight


def shifted_rows(v, o):
    rows = iota(v.shape, 0)
    moved = pltpu.roll(v, (-o) % SUB, 0)
    return jnp.where((rows + o >= 0) & (rows + o < SUB), moved, 0.0)


def edge_rows(first, second):
    zero = jnp.zeros((4, LANE), F32)
    up, down = [], []
    for f in (first, second):
        up += [2.0 * f[7:8] + f[6:7], f[7:8]]
        down += [f[0:1], 2.0 * f[0:1] + f[1:2]]
    return jnp.concatenate([*up, zero], 0), jnp.concatenate([zero, *down], 0)


def second_layer(modes, plane, eigen, design, even, odd, _, out, rows, pairs, *, slab, mode):
    def store(r, stiff, mass):
        out[r, 2] = stiff
        out[r, 3] = mass

    def load(c, a):
        return plane[0, c] if a else modes[0, c, 1]

    m = lax.axis_index(mode)
    tiles = out.shape[0]
    pair = across_x(design, even, odd, slab)
    up, down = edge_rows(*pair)
    for l in (0, 1):
        rows[l] = pair[l]
    for r in range(tiles):
        to_next = jnp.where(m + 1 == r, F32(1.0), F32(0.0))
        to_last = jnp.where(m - 1 == r, F32(1.0), F32(0.0))
        out[r, 7] = up * to_next + down * to_last
    forms(load, eigen[0], store, pairs, tiles)


def across_x(own, even, odd, slab):
    is_even = lax.rem(lax.axis_index(slab), 2) == 0
    own_0, own_1, even_0, even_1, odd_0, odd_1 = own[0], own[1], even[0], even[1], odd[0], odd[1]
    before_0, before_1 = jnp.where(is_even, odd_0, even_0), jnp.where(is_even, odd_1, even_1)
    after_0, after_1 = jnp.where(is_even, even_0, odd_0), jnp.where(is_even, even_1, odd_1)
    first = before_0 + 2.0 * before_1 + 3.0 * own_0 + 2.0 * own_1 + after_0
    second = before_1 + 2.0 * own_0 + 3.0 * own_1 + 2.0 * after_0 + after_1
    return first, second


def over_modes(got, at):
    total = got[0, at]
    for r in range(1, got.shape[0]):
        total = total + got[r, at]
    return total


def own_gradient(got, rows, out, *, slab, mode, sizes):
    total_x, total_y, total_z = sizes
    s, m = lax.axis_index(slab), lax.axis_index(mode)
    stiff = (over_modes(got, 0), over_modes(got, 2))
    mass = (over_modes(got, 1), over_modes(got, 3))
    inverse_weight = 1.0 / over_modes(got, 6)
    edges = over_modes(got, 7)
    inverse_yz = along(m * SUB + iota((SUB, LANE), 0), total_y, edge_tables(total_y)[0]) * along(
        iota((SUB, LANE), 1), total_z, edge_tables(total_z)[0]
    )
    for l in (0, 1):
        own = rows[l]
        near = jnp.concatenate(
            [edges[2 * l : 2 * l + 2], jnp.zeros((4, LANE), F32), edges[4 + 2 * l : 6 + 2 * l]], 0
        )
        filtered = near
        for o in range(1 - FR, FR):
            filtered = filtered + float(FR - abs(o)) * (shifted_rows(own, o) if o else own)
        x = jnp.full((SUB, LANE), 2 * s + l, jnp.int32)
        inverse = inverse_yz * along(x, total_x, edge_tables(total_x)[0])
        density = tent_lanes(filtered) * inverse
        slope = (PENALTY * (1.0 - FLOOR_MODULUS)) * density * density
        out[l] = tent_lanes((slope * stiff[l] - mass[l]) * inverse_weight * inverse)


def gradient_copies(own, even, odd, out, *, slab):
    pair = across_x(own, even, odd, slab)
    for r in range(out.shape[0]):
        out[r, 0] = pair[0]
        out[r, 1] = pair[1]


def measure_xz(slab, total_x, total_z):
    s = lax.axis_index(slab)
    z = along(iota((SUB, LANE), 1), total_z, edge_tables(total_z)[1])
    return [
        z * along(jnp.full((SUB, LANE), 2 * s + l, jnp.int32), total_x, edge_tables(total_x)[1])
        for l in (0, 1)
    ]


def volumes(levels, gain, least, most, parts):
    count = gain.shape[0]
    for start in range(0, len(levels), 8):
        chunk = levels[start : start + 8]

        def body(v, totals):
            g, lo, hi = gain[v], least[v], most[v]
            return tuple(
                t + jnp.minimum(jnp.maximum(g * q, lo), hi) for t, q in zip(totals, chunk)
            )

        zeros = tuple(jnp.zeros((SUB, LANE), F32) for _ in chunk)
        totals = lax.fori_loop(0, count, body, zeros, unroll=4)
        for i, t in enumerate(totals):
            parts[start + i : start + i + 1] = jnp.sum(t, axis=0, keepdims=True)


def lane_totals(parts):
    column = jnp.sum(parts[...], axis=1, keepdims=True)
    shape = (FAN, LANE)
    spread = jnp.where(iota(shape, 0) == iota(shape, 1), jnp.broadcast_to(column, shape), 0.0)
    return jnp.sum(spread, axis=0, keepdims=True)


def first_round(got, early, gain, least, most, own, out, padded, parts, *, slab, mode, sizes):
    total_x, total_y, total_z = sizes
    tiles = got.shape[0]
    m = lax.axis_index(mode)
    for l in (0, 1):
        padded[l, :SUB] = jnp.zeros((SUB, LANE), F32)
        padded[l, (tiles + 1) * SUB :] = jnp.zeros((SUB, LANE), F32)
        for r in range(tiles):
            padded[l, (r + 1) * SUB : (r + 2) * SUB] = got[r, l]
    xz = measure_xz(slab, total_x, total_z)
    goal = jnp.zeros((SUB, LANE), F32)
    for l in (0, 1):
        for r in range(tiles):
            total = None
            for o in range(1 - FR, FR):
                start = (r + 1) * SUB + o
                t = float(FR - abs(o)) * padded[l, start : start + SUB]
                total = t if total is None else total + t
            measure = xz[l] * along(r * SUB + iota((SUB, LANE), 0), total_y, edge_tables(total_y)[1])
            design = early[r, 4 + l]
            at = l * tiles + r
            gain[at] = design * jnp.sqrt(jnp.maximum(total, 0.0) * measure)
            least[at] = jnp.maximum(design - MOVE_LIMIT, 0.0) * measure
            most[at] = jnp.minimum(design + MOVE_LIMIT, 1.0) * measure
            goal = goal + design * measure
        total = None
        for o in range(1 - FR, FR):
            t = float(FR - abs(o)) * padded[l, pl.ds(m * SUB + SUB + o, SUB)]
            total = t if total is None else total + t
        own[l] = total
    levels = [float(np.exp(-0.5 * (LEVEL_LOW + COARSE * (i + 1)))) for i in range(FAN - 1)]
    volumes(levels, gain, least, most, parts)
    parts[FAN - 1 : FAN] = jnp.sum(goal, axis=0, keepdims=True)
    row = lane_totals(parts)
    for k in range(out.shape[0]):
        out[k] = row


def added(got):
    total = got[0]
    for k in range(1, got.shape[0]):
        total = total + got[k]
    return total


def at_lane(row, k):
    return jnp.sum(jnp.where(iota(row.shape, 1) == k, row, 0.0), axis=1, keepdims=True)


def cells_above(row, goal):
    above = (row > goal) & (iota(row.shape, 1) < FAN - 1)
    return jnp.sum(jnp.where(above, 1.0, 0.0), axis=1, keepdims=True)


def second_round(got, gain, least, most, out, state, parts):
    row = added(got)
    goal = at_lane(row, FAN - 1)
    low = LEVEL_LOW + COARSE * cells_above(row, goal)
    state[0:1] = jnp.broadcast_to(low, (1, LANE))
    state[1:2] = jnp.broadcast_to(goal, (1, LANE))
    scale = jnp.exp(-0.5 * jnp.broadcast_to(low, (SUB, LANE)))
    levels = [scale * float(np.exp(-0.5 * FINE * (i + 1))) for i in range(FAN - 1)]
    volumes(levels, gain, least, most, parts)
    parts[FAN - 1 : FAN] = jnp.zeros((1, LANE), F32)
    row = lane_totals(parts)
    for k in range(out.shape[0]):
        out[k] = row


def last_update(got, state, own, design, sens_out, out, *, slab, mode, sizes):
    total_x, total_y, total_z = sizes
    m = lax.axis_index(mode)
    row = added(got)
    goal = state[1:2, 0:1]
    level = state[0:1, 0:1] + FINE * (cells_above(row, goal) + 0.5)
    scale = jnp.exp(jnp.broadcast_to(level, (SUB, LANE)))
    y = along(m * SUB + iota((SUB, LANE), 0), total_y, edge_tables(total_y)[1])
    xz = measure_xz(slab, total_x, total_z)
    for l in (0, 1):
        d, s = design[l], own[l]
        factor = jnp.sqrt(jnp.maximum(s, 0.0) / (scale * (xz[l] * y)))
        least = jnp.maximum(d - MOVE_LIMIT, 0.0)
        most = jnp.minimum(d + MOVE_LIMIT, 1.0)
        out[l] = jnp.minimum(jnp.maximum(d * factor, least), most)
        sens_out[l] = s


def call(kernel, outs, operands, specs=None, scratch=(), flops=1000, alias=None):
    outs = [jax.ShapeDtypeStruct(o, F32) for o in outs]
    size = sum(4 * int(np.prod(o.shape)) for o in (*outs, *operands))
    single = len(outs) == 1
    return pl.pallas_call(
        kernel,
        out_shape=outs[0] if single else outs,
        in_specs=specs or [VMEM] * len(operands),
        out_specs=VMEM if single else [VMEM] * len(outs),
        scratch_shapes=[pltpu.VMEM(s, F32) for s in scratch],
        cost_estimate=pl.CostEstimate(flops=flops, bytes_accessed=size, transcendentals=0),
        input_output_aliases=alias or {},
        compiler_params=pltpu.CompilerParams(vmem_limit_bytes=GRANT),
    )(*operands)


def neighbours(value, axis):
    count = lax.axis_size(axis)
    even = lax.ppermute(value, axis, [(i, i ^ 1) for i in range(count)])
    odd = lax.ppermute(value, axis, [(i, ((i + 1) ^ 1) - 1) for i in range(1, count - 1)])
    return even, odd


def exchange(value, axis):
    return lax.all_to_all(value, axis, 0, 0, tiled=True)


def local(design, mode_shapes, eigenvalues):
    slab, mode = "slab", "mode"
    slabs, modes = lax.axis_size(slab), lax.axis_size(mode)
    _, _, _, total_y, total_z = mode_shapes.shape
    sizes = (2 * slabs, total_y, total_z)
    pairs = (3, 2, 2, total_y + SUB, LANE)
    block = (2, SUB, LANE)
    padded = (2, total_y + 2 * SUB, LANE)
    place = dict(slab=slab, mode=mode, sizes=sizes)

    down = [(i + 1, i) for i in range(slabs - 1)]
    plane = lax.ppermute(mode_shapes[:, :, 0], slab, down)
    even, odd = neighbours(design, slab)
    sent = call(
        first_layer,
        [(modes, 8, SUB, LANE)],
        [mode_shapes, eigenvalues, design],
        specs=[VMEM, SMEM, VMEM],
        scratch=[pairs],
        flops=5_000_000,
    )
    sent, rows = call(
        functools.partial(second_layer, slab=slab, mode=mode),
        [(modes, 8, SUB, LANE), block],
        [mode_shapes, plane, eigenvalues, design, even, odd, sent],
        specs=[VMEM, VMEM, SMEM, VMEM, VMEM, VMEM, VMEM],
        scratch=[pairs],
        flops=5_000_000,
        alias={6: 0},
    )
    early = exchange(sent, mode)
    gradient = call(functools.partial(own_gradient, **place), [block], [early, rows])
    even, odd = neighbours(gradient, slab)
    copies = call(
        functools.partial(gradient_copies, slab=slab), [(modes, *block)], [gradient, even, odd]
    )
    whole = exchange(copies, mode)
    vectors = 2 * modes
    gain, least, most, own, sent = call(
        functools.partial(first_round, **place),
        [(vectors, SUB, LANE)] * 3 + [block, (slabs, 1, LANE)],
        [whole, early],
        scratch=[padded, (FAN, LANE)],
    )
    got = exchange(sent, slab)
    sent, state = call(
        second_round,
        [(slabs, 1, LANE), (SUB, LANE)],
        [got, gain, least, most],
        scratch=[(FAN, LANE)],
    )
    got = exchange(sent, slab)
    return call(functools.partial(last_update, **place), [block, block], [got, state, own, design])


def solution(mesh):
    in_specs = (P("slab", "mode", None), P("mode", None, "slab", None, None), P("mode"))
    out_specs = (P("slab", "mode", None), P("slab", "mode", None))

    def step(design, mode_shapes, eigenvalues):
        return tuple(local(design, mode_shapes, eigenvalues))

    return jax.shard_map(step, mesh=mesh, in_specs=in_specs, out_specs=out_specs, check_vma=False)
```

```python
import functools

import jax
import jax.numpy as jnp
import numpy as np
from jax import lax
from jax.experimental import pallas as pl
from jax.experimental.pallas import tpu as pltpu
from jax.sharding import PartitionSpec as P


FR = 3
KS_SHARP = 2.0
PENALTY = 3.0
FLOOR_MODULUS = 0.001
MOVE_LIMIT = 0.2
POISSON = 0.3
LEVEL_LOW = -14.0
LEVEL_HIGH = 14.0
FAN = 64
COARSE = (LEVEL_HIGH - LEVEL_LOW) / FAN
FINE = COARSE / FAN
SUB, LANE = 8, 128
GRANT = 8 * 1024 * 1024
F32 = jnp.float32
VMEM = pl.BlockSpec(memory_space=pltpu.VMEM)
SMEM = pl.BlockSpec(memory_space=pltpu.SMEM)


def tent_1d(values):
    padded = np.pad(values, FR - 1)
    n = len(values)
    return sum((FR - abs(o)) * padded[FR - 1 + o : FR - 1 + o + n] for o in range(1 - FR, FR))


def edge_tables(n):
    span = tent_1d(np.ones(n))
    return 1.0 / span, tent_1d(1.0 / span)


def along(position, n, table):
    middle = float(table[n // 2])
    value = jnp.where(position >= 0, F32(middle), F32(0.0))
    for k in range(2 * (FR - 1)):
        if abs(table[k] - middle) > 1e-12:
            value = jnp.where((position == k) | (position == n - 1 - k), F32(table[k]), value)
    return value


def iota(shape, axis):
    return lax.broadcasted_iota(jnp.int32, shape, axis)


def tent_lanes(v):
    lanes = iota(v.shape, v.ndim - 1)
    axis = v.ndim - 1
    total = 3.0 * v
    for o in (1, 2):
        above = jnp.where(lanes < LANE - o, pltpu.roll(v, LANE - o, axis), 0.0)
        below = jnp.where(lanes >= o, pltpu.roll(v, o, axis), 0.0)
        total = total + float(FR - o) * (above + below)
    return total


def forms(load, eigen, store, pairs, tiles):
    lame = POISSON / ((1.0 + POISSON) * (1.0 - 2.0 * POISSON))
    shear = 0.5 / (1.0 + POISSON)
    rows = tiles * SUB
    lanes = iota((rows, LANE), 1)
    for c in range(3):
        for a in (0, 1):
            u = load(c, a)
            up = jnp.where(lanes < LANE - 1, pltpu.roll(u, LANE - 1, 1), 0.0)
            pairs[c, a, 0, :rows] = up + u
            pairs[c, a, 1, :rows] = up - u
            pairs[c, a, :, rows:] = jnp.zeros((2, SUB, LANE), F32)
    eigen_v = jnp.full((SUB, LANE), eigen, F32)
    weight = jnp.exp(-KS_SHARP * eigen_v)
    eigen_weight = weight * eigen_v
    normal = lame + 2.0 * shear
    ms, md = 0.25, 1.0 / 12.0
    m0, m1, m2, m3 = ms**3, ms * ms * md, ms * md * md, md**3

    def tile(r, _):
        base = pl.multiple_of(r * SUB, SUB)
        coef = {}
        for c in range(3):
            planes = []
            for a in (0, 1):
                here = {}
                for z in (0, 1):
                    p0 = pairs[c, a, z, pl.ds(base, SUB)]
                    p1 = pairs[c, a, z, pl.ds(base + 1, SUB)]
                    here[0, z] = p1 + p0
                    here[1, z] = p1 - p0
                planes.append(here)
            for y in (0, 1):
                for z in (0, 1):
                    coef[c, 0, y, z] = planes[1][y, z] + planes[0][y, z]
                    coef[c, 1, y, z] = planes[1][y, z] - planes[0][y, z]
        groups = [None] * 6
        for c in range(3):
            for x in (0, 1):
                for y in (0, 1):
                    for z in (0, 1):
                        d = (x, y, z)
                        n = x + y + z
                        g = {0: 0, 1: 1 if d[c] else 2, 2: 3 if d[c] else 4, 3: 5}[n]
                        v = coef[c, x, y, z]
                        groups[g] = v * v if groups[g] is None else groups[g] + v * v
        mass = m0 * groups[0] + m1 * (groups[1] + groups[2]) + m2 * (groups[3] + groups[4]) + m3 * groups[5]
        stiff = (
            (12.0 * m1 * normal) * groups[1]
            + (12.0 * m1 * shear) * groups[2]
            + (12.0 * m2 * (normal + shear)) * groups[3]
            + (12.0 * m2 * 2.0 * shear) * groups[4]
            + (12.0 * m3 * (normal + 2.0 * shear)) * groups[5]
        )
        for third in (0, 1):
            along_sum = across_sum = None
            for i, j, k in ((0, 1, 2), (0, 2, 1), (1, 2, 0)):

                def at(c, di, dj):
                    d = [0, 0, 0]
                    d[i], d[j], d[k] = di, dj, third
                    return coef[c, d[0], d[1], d[2]]

                t = at(i, 1, 0) * at(j, 0, 1)
                s = at(i, 0, 1) * at(j, 1, 0)
                along_sum = t if along_sum is None else along_sum + t
                across_sum = s if across_sum is None else across_sum + s
            m = (ms, md)[third] * 0.25
            stiff = stiff + (2.0 * lame * m) * along_sum + (2.0 * shear * m) * across_sum
        store(r, weight * stiff, eigen_weight * mass)
        return 0

    lax.fori_loop(0, tiles, tile, 0, unroll=2)
    return weight


def tail_rows(packed, k):
    start = packed.shape[0] - (2 - k) * SUB
    return packed[start : start + SUB]


def first_layer(modes, eigen, packed, out, pairs):
    def store(r, stiff, mass):
        out[r, 0] = stiff
        out[r, 1] = mass

    tiles = out.shape[0]
    forms(lambda c, a: modes[0, c, a], eigen[0], store, pairs, tiles)
    design = tail_rows(packed, 0), tail_rows(packed, 1)
    for r in range(tiles):
        out[r, 4] = design[0]
        out[r, 5] = design[1]


def shifted_rows(v, o):
    rows = iota(v.shape, 0)
    moved = pltpu.roll(v, (-o) % SUB, 0)
    return jnp.where((rows + o >= 0) & (rows + o < SUB), moved, 0.0)


def edge_rows(first, second):
    up, down = [], []
    for f in (first, second):
        up += [2.0 * f[7:8] + f[6:7], f[7:8]]
        down += [f[0:1], 2.0 * f[0:1] + f[1:2]]
    return jnp.concatenate(up, 0), jnp.concatenate(down, 0)


def second_layer(modes, eigen, packed, got, before, _, out, rows, pairs, *, mode):
    def store(r, stiff, mass):
        out[r, 2] = stiff
        out[r, 3] = mass

    tiles = out.shape[0]
    span = tiles * SUB

    def load(c, a):
        return got[c * span : (c + 1) * span] if a else modes[0, c, 1]

    m = lax.axis_index(mode)
    own = tail_rows(packed, 0), tail_rows(packed, 1)
    after = tail_rows(got, 0), tail_rows(got, 1)
    pair = across_x(own, before, after)
    up, down = edge_rows(*pair)
    for l in (0, 1):
        rows[l] = pair[l]
    weight = forms(load, eigen[0], store, pairs, tiles)
    half = SUB // 2
    for r in range(tiles):
        out[r, 6, :half] = jnp.where(m + 1 == r, up, weight[:half])
        out[r, 6, half:] = jnp.where(m - 1 == r, down, weight[half:])


def across_x(own, before, after):
    first = before[0] + 2.0 * before[1] + 3.0 * own[0] + 2.0 * own[1] + after[0]
    second = before[1] + 2.0 * own[0] + 3.0 * own[1] + 2.0 * after[0] + after[1]
    return first, second


def over_modes(got, at):
    total = got[0, at]
    for r in range(1, got.shape[0]):
        total = total + got[r, at]
    return total


def own_gradient(got, rows, out, *, slab, mode, sizes):
    total_x, total_y, total_z = sizes
    s, m = lax.axis_index(slab), lax.axis_index(mode)
    stiff = (over_modes(got, 0), over_modes(got, 2))
    mass = (over_modes(got, 1), over_modes(got, 3))
    tiles = got.shape[0]
    half = SUB // 2
    weight = None
    for r in range(tiles):
        w = jnp.where(m - 1 == r, got[r, 6, half : half + 1], got[r, 6, :1])
        weight = w if weight is None else weight + w
    inverse_weight = 1.0 / jnp.broadcast_to(weight, (SUB, LANE))
    from_last = jnp.where(m > 0, got[jnp.maximum(m - 1, 0), 6, :half], 0.0)
    from_next = jnp.where(m < tiles - 1, got[jnp.minimum(m + 1, tiles - 1), 6, half:], 0.0)
    inverse_yz = along(m * SUB + iota((SUB, LANE), 0), total_y, edge_tables(total_y)[0]) * along(
        iota((SUB, LANE), 1), total_z, edge_tables(total_z)[0]
    )
    for l in (0, 1):
        own = rows[l]
        near = jnp.concatenate(
            [from_last[2 * l : 2 * l + 2], jnp.zeros((4, LANE), F32), from_next[2 * l : 2 * l + 2]], 0
        )
        filtered = near
        for o in range(1 - FR, FR):
            filtered = filtered + float(FR - abs(o)) * (shifted_rows(own, o) if o else own)
        x = jnp.full((SUB, LANE), 2 * s + l, jnp.int32)
        inverse = inverse_yz * along(x, total_x, edge_tables(total_x)[0])
        density = tent_lanes(filtered) * inverse
        slope = (PENALTY * (1.0 - FLOOR_MODULUS)) * density * density
        out[l] = tent_lanes((slope * stiff[l] - mass[l]) * inverse_weight * inverse)


def gradient_copies(own, before, after, out):
    pair = across_x(own, before, after)
    for r in range(out.shape[0]):
        out[r, 0] = pair[0]
        out[r, 1] = pair[1]


def measure_xz(slab, total_x, total_z):
    s = lax.axis_index(slab)
    z = along(iota((SUB, LANE), 1), total_z, edge_tables(total_z)[1])
    return [
        z * along(jnp.full((SUB, LANE), 2 * s + l, jnp.int32), total_x, edge_tables(total_x)[1])
        for l in (0, 1)
    ]


def volumes(levels, gain, least, most, parts):
    count = gain.shape[0]
    for start in range(0, len(levels), 8):
        chunk = levels[start : start + 8]

        def body(v, totals):
            g, lo, hi = gain[v], least[v], most[v]
            return tuple(
                t + jnp.minimum(jnp.maximum(g * q, lo), hi) for t, q in zip(totals, chunk)
            )

        zeros = tuple(jnp.zeros((SUB, LANE), F32) for _ in chunk)
        totals = lax.fori_loop(0, count, body, zeros, unroll=4)
        for i, t in enumerate(totals):
            parts[start + i : start + i + 1] = jnp.sum(t, axis=0, keepdims=True)


def lane_totals(parts):
    column = jnp.sum(parts[...], axis=1, keepdims=True)
    shape = (FAN, LANE)
    spread = jnp.where(iota(shape, 0) == iota(shape, 1), jnp.broadcast_to(column, shape), 0.0)
    return jnp.sum(spread, axis=0, keepdims=True)


def first_round(got, early, gain, least, most, own, out, padded, parts, *, slab, mode, sizes):
    total_x, total_y, total_z = sizes
    tiles = got.shape[0]
    m = lax.axis_index(mode)
    for l in (0, 1):
        padded[l, :SUB] = jnp.zeros((SUB, LANE), F32)
        padded[l, (tiles + 1) * SUB :] = jnp.zeros((SUB, LANE), F32)
        for r in range(tiles):
            padded[l, (r + 1) * SUB : (r + 2) * SUB] = got[r, l]
    xz = measure_xz(slab, total_x, total_z)
    goal = jnp.zeros((SUB, LANE), F32)
    for l in (0, 1):
        for r in range(tiles):
            total = None
            for o in range(1 - FR, FR):
                start = (r + 1) * SUB + o
                t = float(FR - abs(o)) * padded[l, start : start + SUB]
                total = t if total is None else total + t
            measure = xz[l] * along(r * SUB + iota((SUB, LANE), 0), total_y, edge_tables(total_y)[1])
            design = early[r, 4 + l]
            at = l * tiles + r
            gain[at] = design * jnp.sqrt(jnp.maximum(total, 0.0) * measure)
            least[at] = jnp.maximum(design - MOVE_LIMIT, 0.0) * measure
            most[at] = jnp.minimum(design + MOVE_LIMIT, 1.0) * measure
            goal = goal + design * measure
        total = None
        for o in range(1 - FR, FR):
            t = float(FR - abs(o)) * padded[l, pl.ds(m * SUB + SUB + o, SUB)]
            total = t if total is None else total + t
        own[l] = total
    levels = [float(np.exp(-0.5 * (LEVEL_LOW + COARSE * (i + 1)))) for i in range(FAN - 1)]
    volumes(levels, gain, least, most, parts)
    parts[FAN - 1 : FAN] = jnp.sum(goal, axis=0, keepdims=True)
    row = lane_totals(parts)
    for k in range(out.shape[0]):
        out[k] = row


def added(got):
    total = got[0]
    for k in range(1, got.shape[0]):
        total = total + got[k]
    return total


def at_lane(row, k):
    return jnp.sum(jnp.where(iota(row.shape, 1) == k, row, 0.0), axis=1, keepdims=True)


def cells_above(row, goal):
    above = (row > goal) & (iota(row.shape, 1) < FAN - 1)
    return jnp.sum(jnp.where(above, 1.0, 0.0), axis=1, keepdims=True)


def second_round(got, gain, least, most, out, state, parts):
    row = added(got)
    goal = at_lane(row, FAN - 1)
    low = LEVEL_LOW + COARSE * cells_above(row, goal)
    state[0:1] = jnp.broadcast_to(low, (1, LANE))
    state[1:2] = jnp.broadcast_to(goal, (1, LANE))
    scale = jnp.exp(-0.5 * jnp.broadcast_to(low, (SUB, LANE)))
    levels = [scale * float(np.exp(-0.5 * FINE * (i + 1))) for i in range(FAN - 1)]
    volumes(levels, gain, least, most, parts)
    parts[FAN - 1 : FAN] = jnp.zeros((1, LANE), F32)
    row = lane_totals(parts)
    for k in range(out.shape[0]):
        out[k] = row


def last_update(got, state, own, design, sens_out, out, *, slab, mode, sizes):
    total_x, total_y, total_z = sizes
    m = lax.axis_index(mode)
    row = added(got)
    goal = state[1:2, 0:1]
    level = state[0:1, 0:1] + FINE * (cells_above(row, goal) + 0.5)
    scale = jnp.exp(jnp.broadcast_to(level, (SUB, LANE)))
    y = along(m * SUB + iota((SUB, LANE), 0), total_y, edge_tables(total_y)[1])
    xz = measure_xz(slab, total_x, total_z)
    for l in (0, 1):
        d, s = design[l], own[l]
        factor = jnp.sqrt(jnp.maximum(s, 0.0) / (scale * (xz[l] * y)))
        least = jnp.maximum(d - MOVE_LIMIT, 0.0)
        most = jnp.minimum(d + MOVE_LIMIT, 1.0)
        out[l] = jnp.minimum(jnp.maximum(d * factor, least), most)
        sens_out[l] = s


def call(kernel, outs, operands, specs=None, scratch=(), flops=1000, alias=None):
    outs = [jax.ShapeDtypeStruct(o, F32) for o in outs]
    size = sum(4 * int(np.prod(o.shape)) for o in (*outs, *operands))
    single = len(outs) == 1
    return pl.pallas_call(
        kernel,
        out_shape=outs[0] if single else outs,
        in_specs=specs or [VMEM] * len(operands),
        out_specs=VMEM if single else [VMEM] * len(outs),
        scratch_shapes=[pltpu.VMEM(s, F32) for s in scratch],
        cost_estimate=pl.CostEstimate(flops=flops, bytes_accessed=size, transcendentals=0),
        input_output_aliases=alias or {},
        compiler_params=pltpu.CompilerParams(vmem_limit_bytes=GRANT),
    )(*operands)


def from_before(value, axis):
    count = lax.axis_size(axis)
    return lax.ppermute(value, axis, [(i, i + 1) for i in range(count - 1)])


def from_after(value, axis):
    count = lax.axis_size(axis)
    return lax.ppermute(value, axis, [(i + 1, i) for i in range(count - 1)])


def exchange(value, axis):
    return lax.all_to_all(value, axis, 0, 0, tiled=True)


def local(design, mode_shapes, eigenvalues):
    slab, mode = "slab", "mode"
    slabs, modes = lax.axis_size(slab), lax.axis_size(mode)
    _, _, _, total_y, total_z = mode_shapes.shape
    sizes = (2 * slabs, total_y, total_z)
    pairs = (3, 2, 2, total_y + SUB, LANE)
    block = (2, SUB, LANE)
    padded = (2, total_y + 2 * SUB, LANE)
    place = dict(slab=slab, mode=mode, sizes=sizes)

    packed = jnp.concatenate([mode_shapes[0, :, 0].reshape(-1, LANE), design.reshape(-1, LANE)], 0)
    got = from_after(packed, slab)
    before = from_before(design, slab)
    sent = call(
        first_layer,
        [(modes, 7, SUB, LANE)],
        [mode_shapes, eigenvalues, packed],
        specs=[VMEM, SMEM, VMEM],
        scratch=[pairs],
        flops=5_000_000,
    )
    sent, rows = call(
        functools.partial(second_layer, mode=mode),
        [(modes, 7, SUB, LANE), block],
        [mode_shapes, eigenvalues, packed, got, before, sent],
        specs=[VMEM, SMEM, VMEM, VMEM, VMEM, VMEM],
        scratch=[pairs],
        flops=5_000_000,
        alias={5: 0},
    )
    early = exchange(sent, mode)
    gradient = call(functools.partial(own_gradient, **place), [block], [early, rows])
    after = from_after(gradient, slab)
    before = from_before(gradient, slab)
    copies = call(gradient_copies, [(modes, *block)], [gradient, before, after])
    whole = exchange(copies, mode)
    vectors = 2 * modes
    gain, least, most, own, sent = call(
        functools.partial(first_round, **place),
        [(vectors, SUB, LANE)] * 3 + [block, (slabs, 1, LANE)],
        [whole, early],
        scratch=[padded, (FAN, LANE)],
    )
    got = exchange(sent, slab)
    sent, state = call(
        second_round,
        [(slabs, 1, LANE), (SUB, LANE)],
        [got, gain, least, most],
        scratch=[(FAN, LANE)],
    )
    got = exchange(sent, slab)
    return call(functools.partial(last_update, **place), [block, block], [got, state, own, design])


def solution(mesh):
    in_specs = (P("slab", "mode", None), P("mode", None, "slab", None, None), P("mode"))
    out_specs = (P("slab", "mode", None), P("slab", "mode", None))

    def step(design, mode_shapes, eigenvalues):
        return tuple(local(design, mode_shapes, eigenvalues))

    return jax.shard_map(step, mesh=mesh, in_specs=in_specs, out_specs=out_specs, check_vma=False)
```

```python
import functools

import jax
import jax.numpy as jnp
import numpy as np
from jax import lax
from jax.experimental import pallas as pl
from jax.experimental.pallas import tpu as pltpu
from jax.sharding import PartitionSpec as P


FR = 3
KS_SHARP = 2.0
PENALTY = 3.0
FLOOR_MODULUS = 0.001
MOVE_LIMIT = 0.2
POISSON = 0.3
LEVEL_LOW = -14.0
LEVEL_HIGH = 14.0
FAN = 64
COARSE = (LEVEL_HIGH - LEVEL_LOW) / FAN
FINE = COARSE / FAN
SUB, LANE = 8, 128
GRANT = 8 * 1024 * 1024
F32 = jnp.float32
VMEM = pl.BlockSpec(memory_space=pltpu.VMEM)
SMEM = pl.BlockSpec(memory_space=pltpu.SMEM)


def tent_1d(values):
    padded = np.pad(values, FR - 1)
    n = len(values)
    return sum((FR - abs(o)) * padded[FR - 1 + o : FR - 1 + o + n] for o in range(1 - FR, FR))


def edge_tables(n):
    span = tent_1d(np.ones(n))
    return 1.0 / span, tent_1d(1.0 / span)


def along(position, n, table):
    middle = float(table[n // 2])
    value = jnp.where(position >= 0, F32(middle), F32(0.0))
    for k in range(2 * (FR - 1)):
        if abs(table[k] - middle) > 1e-12:
            value = jnp.where((position == k) | (position == n - 1 - k), F32(table[k]), value)
    return value


def iota(shape, axis):
    return lax.broadcasted_iota(jnp.int32, shape, axis)


def tent_lanes(v):
    lanes = iota(v.shape, v.ndim - 1)
    axis = v.ndim - 1
    total = 3.0 * v
    for o in (1, 2):
        above = jnp.where(lanes < LANE - o, pltpu.roll(v, LANE - o, axis), 0.0)
        below = jnp.where(lanes >= o, pltpu.roll(v, o, axis), 0.0)
        total = total + float(FR - o) * (above + below)
    return total


def forms(load, eigen, store, pairs, tiles):
    lame = POISSON / ((1.0 + POISSON) * (1.0 - 2.0 * POISSON))
    shear = 0.5 / (1.0 + POISSON)
    rows = tiles * SUB
    lanes = iota((rows, LANE), 1)
    for c in range(3):
        for a in (0, 1):
            u = load(c, a)
            up = jnp.where(lanes < LANE - 1, pltpu.roll(u, LANE - 1, 1), 0.0)
            pairs[c, a, 0, :rows] = up + u
            pairs[c, a, 1, :rows] = up - u
            pairs[c, a, :, rows:] = jnp.zeros((2, SUB, LANE), F32)
    eigen_v = jnp.full((SUB, LANE), eigen, F32)
    weight = jnp.exp(-KS_SHARP * eigen_v)
    eigen_weight = weight * eigen_v
    normal = lame + 2.0 * shear
    ms, md = 0.25, 1.0 / 12.0
    m0, m1, m2, m3 = ms**3, ms * ms * md, ms * md * md, md**3

    def tile(r, _):
        base = pl.multiple_of(r * SUB, SUB)
        coef = {}
        for c in range(3):
            planes = []
            for a in (0, 1):
                here = {}
                for z in (0, 1):
                    p0 = pairs[c, a, z, pl.ds(base, SUB)]
                    p1 = pairs[c, a, z, pl.ds(base + 1, SUB)]
                    here[0, z] = p1 + p0
                    here[1, z] = p1 - p0
                planes.append(here)
            for y in (0, 1):
                for z in (0, 1):
                    coef[c, 0, y, z] = planes[1][y, z] + planes[0][y, z]
                    coef[c, 1, y, z] = planes[1][y, z] - planes[0][y, z]
        groups = [None] * 6
        for c in range(3):
            for x in (0, 1):
                for y in (0, 1):
                    for z in (0, 1):
                        d = (x, y, z)
                        n = x + y + z
                        g = {0: 0, 1: 1 if d[c] else 2, 2: 3 if d[c] else 4, 3: 5}[n]
                        v = coef[c, x, y, z]
                        groups[g] = v * v if groups[g] is None else groups[g] + v * v
        mass = m0 * groups[0] + m1 * (groups[1] + groups[2]) + m2 * (groups[3] + groups[4]) + m3 * groups[5]
        stiff = (
            (12.0 * m1 * normal) * groups[1]
            + (12.0 * m1 * shear) * groups[2]
            + (12.0 * m2 * (normal + shear)) * groups[3]
            + (12.0 * m2 * 2.0 * shear) * groups[4]
            + (12.0 * m3 * (normal + 2.0 * shear)) * groups[5]
        )
        for third in (0, 1):
            along_sum = across_sum = None
            for i, j, k in ((0, 1, 2), (0, 2, 1), (1, 2, 0)):

                def at(c, di, dj):
                    d = [0, 0, 0]
                    d[i], d[j], d[k] = di, dj, third
                    return coef[c, d[0], d[1], d[2]]

                t = at(i, 1, 0) * at(j, 0, 1)
                s = at(i, 0, 1) * at(j, 1, 0)
                along_sum = t if along_sum is None else along_sum + t
                across_sum = s if across_sum is None else across_sum + s
            m = (ms, md)[third] * 0.25
            stiff = stiff + (2.0 * lame * m) * along_sum + (2.0 * shear * m) * across_sum
        store(r, weight * stiff, eigen_weight * mass)
        return 0

    lax.fori_loop(0, tiles, tile, 0, unroll=2)
    return weight


def tail_rows(packed, k):
    start = packed.shape[0] - (2 - k) * SUB
    return packed[start : start + SUB]


def first_layer(modes, eigen, packed, out, pairs):
    def store(r, stiff, mass):
        out[r, 0] = stiff
        out[r, 1] = mass

    tiles = out.shape[0]
    forms(lambda c, a: modes[0, c, a], eigen[0], store, pairs, tiles)
    design = tail_rows(packed, 0), tail_rows(packed, 1)
    for r in range(tiles):
        out[r, 4] = design[0]
        out[r, 5] = design[1]


def shifted_rows(v, o):
    rows = iota(v.shape, 0)
    moved = pltpu.roll(v, (-o) % SUB, 0)
    return jnp.where((rows + o >= 0) & (rows + o < SUB), moved, 0.0)


def edge_rows(first, second):
    up, down = [], []
    for f in (first, second):
        up += [2.0 * f[7:8] + f[6:7], f[7:8]]
        down += [f[0:1], 2.0 * f[0:1] + f[1:2]]
    return jnp.concatenate(up, 0), jnp.concatenate(down, 0)


def second_layer(modes, eigen, packed, got, before, _, out, rows, pairs, *, mode):
    def store(r, stiff, mass):
        out[r, 2] = stiff
        out[r, 3] = mass

    tiles = out.shape[0]
    span = tiles * SUB

    def load(c, a):
        return got[c * span : (c + 1) * span] if a else modes[0, c, 1]

    m = lax.axis_index(mode)
    own = tail_rows(packed, 0), tail_rows(packed, 1)
    after = tail_rows(got, 0), tail_rows(got, 1)
    pair = across_x(own, before, after)
    up, down = edge_rows(*pair)
    for l in (0, 1):
        rows[l] = pair[l]
    weight = forms(load, eigen[0], store, pairs, tiles)
    half = SUB // 2
    for r in range(tiles):
        out[r, 6, :half] = jnp.where(m + 1 == r, up, weight[:half])
        out[r, 6, half:] = jnp.where(m - 1 == r, down, weight[half:])


def across_x(own, before, after):
    first = before[0] + 2.0 * before[1] + 3.0 * own[0] + 2.0 * own[1] + after[0]
    second = before[1] + 2.0 * own[0] + 3.0 * own[1] + 2.0 * after[0] + after[1]
    return first, second


def over_modes(got, at):
    total = got[0, at]
    for r in range(1, got.shape[0]):
        total = total + got[r, at]
    return total


def own_gradient(got, rows, out, *, slab, mode, sizes):
    total_x, total_y, total_z = sizes
    s, m = lax.axis_index(slab), lax.axis_index(mode)
    stiff = (over_modes(got, 0), over_modes(got, 2))
    mass = (over_modes(got, 1), over_modes(got, 3))
    tiles = got.shape[0]
    half = SUB // 2
    weight = None
    for r in range(tiles):
        w = jnp.where(m - 1 == r, got[r, 6, half : half + 1], got[r, 6, :1])
        weight = w if weight is None else weight + w
    inverse_weight = 1.0 / jnp.broadcast_to(weight, (SUB, LANE))
    from_last = jnp.where(m > 0, got[jnp.maximum(m - 1, 0), 6, :half], 0.0)
    from_next = jnp.where(m < tiles - 1, got[jnp.minimum(m + 1, tiles - 1), 6, half:], 0.0)
    inverse_yz = along(m * SUB + iota((SUB, LANE), 0), total_y, edge_tables(total_y)[0]) * along(
        iota((SUB, LANE), 1), total_z, edge_tables(total_z)[0]
    )
    for l in (0, 1):
        own = rows[l]
        near = jnp.concatenate(
            [from_last[2 * l : 2 * l + 2], jnp.zeros((4, LANE), F32), from_next[2 * l : 2 * l + 2]], 0
        )
        filtered = near
        for o in range(1 - FR, FR):
            filtered = filtered + float(FR - abs(o)) * (shifted_rows(own, o) if o else own)
        x = jnp.full((SUB, LANE), 2 * s + l, jnp.int32)
        inverse = inverse_yz * along(x, total_x, edge_tables(total_x)[0])
        density = tent_lanes(filtered) * inverse
        slope = (PENALTY * (1.0 - FLOOR_MODULUS)) * density * density
        out[l] = tent_lanes((slope * stiff[l] - mass[l]) * inverse_weight * inverse)


def gradient_copies(own, before, after, out):
    pair = across_x(own, before, after)
    for r in range(out.shape[0]):
        out[r, 0] = pair[0]
        out[r, 1] = pair[1]


def measure_xz(slab, total_x, total_z):
    s = lax.axis_index(slab)
    z = along(iota((SUB, LANE), 1), total_z, edge_tables(total_z)[1])
    return [
        z * along(jnp.full((SUB, LANE), 2 * s + l, jnp.int32), total_x, edge_tables(total_x)[1])
        for l in (0, 1)
    ]


def volumes(levels, gain, least, most, parts):
    count = gain.shape[0]
    for start in range(0, len(levels), 8):
        chunk = levels[start : start + 8]

        def body(v, totals):
            g, lo, hi = gain[v], least[v], most[v]
            return tuple(
                t + jnp.minimum(jnp.maximum(g * q, lo), hi) for t, q in zip(totals, chunk)
            )

        zeros = tuple(jnp.zeros((SUB, LANE), F32) for _ in chunk)
        totals = lax.fori_loop(0, count, body, zeros, unroll=16)
        for i, t in enumerate(totals):
            parts[start + i : start + i + 1] = jnp.sum(t, axis=0, keepdims=True)


def lane_totals(parts):
    column = jnp.sum(parts[...], axis=1, keepdims=True)
    shape = (FAN, LANE)
    spread = jnp.where(iota(shape, 0) == iota(shape, 1), jnp.broadcast_to(column, shape), 0.0)
    return jnp.sum(spread, axis=0, keepdims=True)


def bounds(early, least, most, goals, measures, *, slab, sizes):
    total_x, total_y, total_z = sizes
    tiles = early.shape[0]
    xz = measure_xz(slab, total_x, total_z)
    goal = jnp.zeros((SUB, LANE), F32)
    for r in range(tiles):
        y = along(r * SUB + iota((SUB, LANE), 0), total_y, edge_tables(total_y)[1])
        for l in (0, 1):
            measure = xz[l] * y
            design = early[r, 4 + l]
            at = l * tiles + r
            least[at] = jnp.maximum(design - MOVE_LIMIT, 0.0) * measure
            most[at] = jnp.minimum(design + MOVE_LIMIT, 1.0) * measure
            measures[at] = measure
            goal = goal + design * measure
    goals[0:1] = jnp.sum(goal, axis=0, keepdims=True)


def first_round(got, early, least, most, goals, measures, gain, own, out, padded, parts, *, mode):
    tiles = got.shape[0]
    m = lax.axis_index(mode)
    for l in (0, 1):
        padded[l, :SUB] = jnp.zeros((SUB, LANE), F32)
        padded[l, (tiles + 1) * SUB :] = jnp.zeros((SUB, LANE), F32)
        for r in range(tiles):
            padded[l, (r + 1) * SUB : (r + 2) * SUB] = got[r, l]
    for l in (0, 1):
        for r in range(tiles):
            total = None
            for o in range(1 - FR, FR):
                start = (r + 1) * SUB + o
                t = float(FR - abs(o)) * padded[l, start : start + SUB]
                total = t if total is None else total + t
            at = l * tiles + r
            gain[at] = early[r, 4 + l] * jnp.sqrt(jnp.maximum(total, 0.0) * measures[at])
        total = None
        for o in range(1 - FR, FR):
            t = float(FR - abs(o)) * padded[l, pl.ds(m * SUB + SUB + o, SUB)]
            total = t if total is None else total + t
        own[l] = total
    levels = [float(np.exp(-0.5 * (LEVEL_LOW + COARSE * (i + 1)))) for i in range(FAN - 1)]
    volumes(levels, gain, least, most, parts)
    parts[FAN - 1 : FAN] = goals[0:1]
    row = lane_totals(parts)
    for k in range(out.shape[0]):
        out[k] = row


def added(got):
    total = got[0]
    for k in range(1, got.shape[0]):
        total = total + got[k]
    return total


def at_lane(row, k):
    return jnp.sum(jnp.where(iota(row.shape, 1) == k, row, 0.0), axis=1, keepdims=True)


def cells_above(row, goal):
    above = (row > goal) & (iota(row.shape, 1) < FAN - 1)
    return jnp.sum(jnp.where(above, 1.0, 0.0), axis=1, keepdims=True)


def second_round(got, gain, least, most, out, state, parts):
    row = added(got)
    goal = at_lane(row, FAN - 1)
    low = LEVEL_LOW + COARSE * cells_above(row, goal)
    state[0:1] = jnp.broadcast_to(low, (1, LANE))
    state[1:2] = jnp.broadcast_to(goal, (1, LANE))
    scale = jnp.exp(-0.5 * jnp.broadcast_to(low, (SUB, LANE)))
    levels = [scale * float(np.exp(-0.5 * FINE * (i + 1))) for i in range(FAN - 1)]
    volumes(levels, gain, least, most, parts)
    parts[FAN - 1 : FAN] = jnp.zeros((1, LANE), F32)
    row = lane_totals(parts)
    for k in range(out.shape[0]):
        out[k] = row


def last_update(got, state, own, design, sens_out, out, *, slab, mode, sizes):
    total_x, total_y, total_z = sizes
    m = lax.axis_index(mode)
    row = added(got)
    goal = state[1:2, 0:1]
    level = state[0:1, 0:1] + FINE * (cells_above(row, goal) + 0.5)
    scale = jnp.exp(jnp.broadcast_to(level, (SUB, LANE)))
    y = along(m * SUB + iota((SUB, LANE), 0), total_y, edge_tables(total_y)[1])
    xz = measure_xz(slab, total_x, total_z)
    for l in (0, 1):
        d, s = design[l], own[l]
        factor = jnp.sqrt(jnp.maximum(s, 0.0) / (scale * (xz[l] * y)))
        least = jnp.maximum(d - MOVE_LIMIT, 0.0)
        most = jnp.minimum(d + MOVE_LIMIT, 1.0)
        out[l] = jnp.minimum(jnp.maximum(d * factor, least), most)
        sens_out[l] = s


def call(kernel, outs, operands, specs=None, scratch=(), flops=1000, alias=None):
    outs = [jax.ShapeDtypeStruct(o, F32) for o in outs]
    size = sum(4 * int(np.prod(o.shape)) for o in (*outs, *operands))
    single = len(outs) == 1
    return pl.pallas_call(
        kernel,
        out_shape=outs[0] if single else outs,
        in_specs=specs or [VMEM] * len(operands),
        out_specs=VMEM if single else [VMEM] * len(outs),
        scratch_shapes=[pltpu.VMEM(s, F32) for s in scratch],
        cost_estimate=pl.CostEstimate(flops=flops, bytes_accessed=size, transcendentals=0),
        input_output_aliases=alias or {},
        compiler_params=pltpu.CompilerParams(vmem_limit_bytes=GRANT),
    )(*operands)


def from_before(value, axis):
    count = lax.axis_size(axis)
    return lax.ppermute(value, axis, [(i, i + 1) for i in range(count - 1)])


def from_after(value, axis):
    count = lax.axis_size(axis)
    return lax.ppermute(value, axis, [(i + 1, i) for i in range(count - 1)])


def exchange(value, axis):
    return lax.all_to_all(value, axis, 0, 0, tiled=True)


def local(design, mode_shapes, eigenvalues):
    slab, mode = "slab", "mode"
    slabs, modes = lax.axis_size(slab), lax.axis_size(mode)
    _, _, _, total_y, total_z = mode_shapes.shape
    sizes = (2 * slabs, total_y, total_z)
    pairs = (3, 2, 2, total_y + SUB, LANE)
    block = (2, SUB, LANE)
    padded = (2, total_y + 2 * SUB, LANE)
    place = dict(slab=slab, mode=mode, sizes=sizes)

    packed = jnp.concatenate([mode_shapes[0, :, 0].reshape(-1, LANE), design.reshape(-1, LANE)], 0)
    got = from_after(packed, slab)
    before = from_before(design, slab)
    sent = call(
        first_layer,
        [(modes, 7, SUB, LANE)],
        [mode_shapes, eigenvalues, packed],
        specs=[VMEM, SMEM, VMEM],
        scratch=[pairs],
        flops=5_000_000,
    )
    sent, rows = call(
        functools.partial(second_layer, mode=mode),
        [(modes, 7, SUB, LANE), block],
        [mode_shapes, eigenvalues, packed, got, before, sent],
        specs=[VMEM, SMEM, VMEM, VMEM, VMEM, VMEM],
        scratch=[pairs],
        flops=5_000_000,
        alias={5: 0},
    )
    early = exchange(sent, mode)
    gradient = call(functools.partial(own_gradient, **place), [block], [early, rows])
    after = from_after(gradient, slab)
    before = from_before(gradient, slab)
    copies = call(gradient_copies, [(modes, *block)], [gradient, before, after])
    whole = exchange(copies, mode)
    vectors = (2 * modes, SUB, LANE)
    least, most, goals, measures = call(
        functools.partial(bounds, slab=slab, sizes=sizes),
        [vectors, vectors, (SUB, LANE), vectors],
        [early],
        flops=100_000,
    )
    gain, own, sent = call(
        functools.partial(first_round, mode=mode),
        [vectors, block, (slabs, 1, LANE)],
        [whole, early, least, most, goals, measures],
        scratch=[padded, (FAN, LANE)],
    )
    got = exchange(sent, slab)
    sent, state = call(
        second_round,
        [(slabs, 1, LANE), (SUB, LANE)],
        [got, gain, least, most],
        scratch=[(FAN, LANE)],
    )
    got = exchange(sent, slab)
    return call(functools.partial(last_update, **place), [block, block], [got, state, own, design])


def solution(mesh):
    in_specs = (P("slab", "mode", None), P("mode", None, "slab", None, None), P("mode"))
    out_specs = (P("slab", "mode", None), P("slab", "mode", None))

    def step(design, mode_shapes, eigenvalues):
        return tuple(local(design, mode_shapes, eigenvalues))

    return jax.shard_map(step, mesh=mesh, in_specs=in_specs, out_specs=out_specs, check_vma=False)
```

```python
import functools

import jax
import jax.numpy as jnp
import numpy as np
from jax import lax
from jax.experimental import pallas as pl
from jax.experimental.pallas import tpu as pltpu
from jax.sharding import PartitionSpec as P


FR = 3
KS_SHARP = 2.0
PENALTY = 3.0
FLOOR_MODULUS = 0.001
MOVE_LIMIT = 0.2
POISSON = 0.3
LEVEL_LOW = -14.0
LEVEL_HIGH = 14.0
FAN = 64
COARSE = (LEVEL_HIGH - LEVEL_LOW) / FAN
FINE = COARSE / FAN
SUB, LANE = 8, 128
GRANT = 8 * 1024 * 1024
F32 = jnp.float32
VMEM = pl.BlockSpec(memory_space=pltpu.VMEM)
SMEM = pl.BlockSpec(memory_space=pltpu.SMEM)


def tent_1d(values):
    padded = np.pad(values, FR - 1)
    n = len(values)
    return sum((FR - abs(o)) * padded[FR - 1 + o : FR - 1 + o + n] for o in range(1 - FR, FR))


def edge_tables(n):
    span = tent_1d(np.ones(n))
    return 1.0 / span, tent_1d(1.0 / span)


def along(position, n, table):
    middle = float(table[n // 2])
    value = jnp.where(position >= 0, F32(middle), F32(0.0))
    for k in range(2 * (FR - 1)):
        if abs(table[k] - middle) > 1e-12:
            value = jnp.where((position == k) | (position == n - 1 - k), F32(table[k]), value)
    return value


def iota(shape, axis):
    return lax.broadcasted_iota(jnp.int32, shape, axis)


def tent_lanes(v):
    lanes = iota(v.shape, v.ndim - 1)
    axis = v.ndim - 1
    total = 3.0 * v
    for o in (1, 2):
        above = jnp.where(lanes < LANE - o, pltpu.roll(v, LANE - o, axis), 0.0)
        below = jnp.where(lanes >= o, pltpu.roll(v, o, axis), 0.0)
        total = total + float(FR - o) * (above + below)
    return total


def forms(load, eigen, store, pairs, tiles):
    lame = POISSON / ((1.0 + POISSON) * (1.0 - 2.0 * POISSON))
    shear = 0.5 / (1.0 + POISSON)
    rows = tiles * SUB
    lanes = iota((rows, LANE), 1)
    for c in range(3):
        for a in (0, 1):
            u = load(c, a)
            up = jnp.where(lanes < LANE - 1, pltpu.roll(u, LANE - 1, 1), 0.0)
            pairs[c, a, 0, :rows] = up + u
            pairs[c, a, 1, :rows] = up - u
            pairs[c, a, :, rows:] = jnp.zeros((2, SUB, LANE), F32)
    eigen_v = jnp.full((SUB, LANE), eigen, F32)
    weight = jnp.exp(-KS_SHARP * eigen_v)
    eigen_weight = weight * eigen_v
    normal = lame + 2.0 * shear
    ms, md = 0.25, 1.0 / 12.0
    m0, m1, m2, m3 = ms**3, ms * ms * md, ms * md * md, md**3

    def tile(r, _):
        base = pl.multiple_of(r * SUB, SUB)
        coef = {}
        for c in range(3):
            planes = []
            for a in (0, 1):
                here = {}
                for z in (0, 1):
                    p0 = pairs[c, a, z, pl.ds(base, SUB)]
                    p1 = pairs[c, a, z, pl.ds(base + 1, SUB)]
                    here[0, z] = p1 + p0
                    here[1, z] = p1 - p0
                planes.append(here)
            for y in (0, 1):
                for z in (0, 1):
                    coef[c, 0, y, z] = planes[1][y, z] + planes[0][y, z]
                    coef[c, 1, y, z] = planes[1][y, z] - planes[0][y, z]
        groups = [None] * 6
        for c in range(3):
            for x in (0, 1):
                for y in (0, 1):
                    for z in (0, 1):
                        d = (x, y, z)
                        n = x + y + z
                        g = {0: 0, 1: 1 if d[c] else 2, 2: 3 if d[c] else 4, 3: 5}[n]
                        v = coef[c, x, y, z]
                        groups[g] = v * v if groups[g] is None else groups[g] + v * v
        mass = m0 * groups[0] + m1 * (groups[1] + groups[2]) + m2 * (groups[3] + groups[4]) + m3 * groups[5]
        stiff = (
            (12.0 * m1 * normal) * groups[1]
            + (12.0 * m1 * shear) * groups[2]
            + (12.0 * m2 * (normal + shear)) * groups[3]
            + (12.0 * m2 * 2.0 * shear) * groups[4]
            + (12.0 * m3 * (normal + 2.0 * shear)) * groups[5]
        )
        for third in (0, 1):
            along_sum = across_sum = None
            for i, j, k in ((0, 1, 2), (0, 2, 1), (1, 2, 0)):

                def at(c, di, dj):
                    d = [0, 0, 0]
                    d[i], d[j], d[k] = di, dj, third
                    return coef[c, d[0], d[1], d[2]]

                t = at(i, 1, 0) * at(j, 0, 1)
                s = at(i, 0, 1) * at(j, 1, 0)
                along_sum = t if along_sum is None else along_sum + t
                across_sum = s if across_sum is None else across_sum + s
            m = (ms, md)[third] * 0.25
            stiff = stiff + (2.0 * lame * m) * along_sum + (2.0 * shear * m) * across_sum
        store(r, weight * stiff, eigen_weight * mass)
        return 0

    lax.fori_loop(0, tiles, tile, 0, unroll=2)
    return weight


def first_layer(modes, eigen, out, pairs):
    def store(r, stiff, mass):
        out[r, 0] = stiff
        out[r, 1] = mass

    forms(lambda c, a: modes[0, c, a], eigen[0], store, pairs, out.shape[0])


def shifted_rows(v, o):
    rows = iota(v.shape, 0)
    moved = pltpu.roll(v, (-o) % SUB, 0)
    return jnp.where((rows + o >= 0) & (rows + o < SUB), moved, 0.0)


def edge_rows(first, second):
    up, down = [], []
    for f in (first, second):
        up += [2.0 * f[7:8] + f[6:7], f[7:8]]
        down += [f[0:1], 2.0 * f[0:1] + f[1:2]]
    return jnp.concatenate(up, 0), jnp.concatenate(down, 0)


def second_layer(modes, eigen, plane, design, before, after, _, out, rows, pairs, *, mode):
    def store(r, stiff, mass):
        out[r, 2] = stiff
        out[r, 3] = mass

    def load(c, a):
        return plane[c] if a else modes[0, c, 1]

    m = lax.axis_index(mode)
    tiles = out.shape[0]
    pair = across_x(design, before, after)
    up, down = edge_rows(*pair)
    for l in (0, 1):
        rows[l] = pair[l]
    weight = forms(load, eigen[0], store, pairs, tiles)
    half = SUB // 2
    for r in range(tiles):
        out[r, 4] = design[0]
        out[r, 5] = design[1]
        out[r, 6, :half] = jnp.where(m + 1 == r, up, weight[:half])
        out[r, 6, half:] = jnp.where(m - 1 == r, down, weight[half:])


def across_x(own, before, after):
    first = before[0] + 2.0 * before[1] + 3.0 * own[0] + 2.0 * own[1] + after[0]
    second = before[1] + 2.0 * own[0] + 3.0 * own[1] + 2.0 * after[0] + after[1]
    return first, second


def over_modes(got, at):
    total = got[0, at]
    for r in range(1, got.shape[0]):
        total = total + got[r, at]
    return total


def own_gradient(got, rows, out, *, slab, mode, sizes):
    total_x, total_y, total_z = sizes
    s, m = lax.axis_index(slab), lax.axis_index(mode)
    stiff = (over_modes(got, 0), over_modes(got, 2))
    mass = (over_modes(got, 1), over_modes(got, 3))
    tiles = got.shape[0]
    half = SUB // 2
    weight = None
    for r in range(tiles):
        w = jnp.where(m - 1 == r, got[r, 6, half : half + 1], got[r, 6, :1])
        weight = w if weight is None else weight + w
    inverse_weight = 1.0 / jnp.broadcast_to(weight, (SUB, LANE))
    from_last = jnp.where(m > 0, got[jnp.maximum(m - 1, 0), 6, :half], 0.0)
    from_next = jnp.where(m < tiles - 1, got[jnp.minimum(m + 1, tiles - 1), 6, half:], 0.0)
    inverse_yz = along(m * SUB + iota((SUB, LANE), 0), total_y, edge_tables(total_y)[0]) * along(
        iota((SUB, LANE), 1), total_z, edge_tables(total_z)[0]
    )
    for l in (0, 1):
        own = rows[l]
        near = jnp.concatenate(
            [from_last[2 * l : 2 * l + 2], jnp.zeros((4, LANE), F32), from_next[2 * l : 2 * l + 2]], 0
        )
        filtered = near
        for o in range(1 - FR, FR):
            filtered = filtered + float(FR - abs(o)) * (shifted_rows(own, o) if o else own)
        x = jnp.full((SUB, LANE), 2 * s + l, jnp.int32)
        inverse = inverse_yz * along(x, total_x, edge_tables(total_x)[0])
        density = tent_lanes(filtered) * inverse
        slope = (PENALTY * (1.0 - FLOOR_MODULUS)) * density * density
        out[l] = tent_lanes((slope * stiff[l] - mass[l]) * inverse_weight * inverse)


def gradient_copies(own, before, after, out):
    pair = across_x(own, before, after)
    for r in range(out.shape[0]):
        out[r, 0] = pair[0]
        out[r, 1] = pair[1]


def measure_xz(slab, total_x, total_z):
    s = lax.axis_index(slab)
    z = along(iota((SUB, LANE), 1), total_z, edge_tables(total_z)[1])
    return [
        z * along(jnp.full((SUB, LANE), 2 * s + l, jnp.int32), total_x, edge_tables(total_x)[1])
        for l in (0, 1)
    ]


def volumes(levels, gain, least, most, parts):
    count = gain.shape[0]
    for start in range(0, len(levels), 8):
        chunk = levels[start : start + 8]

        def body(v, totals):
            g, lo, hi = gain[v], least[v], most[v]
            return tuple(
                t + jnp.minimum(jnp.maximum(g * q, lo), hi) for t, q in zip(totals, chunk)
            )

        zeros = tuple(jnp.zeros((SUB, LANE), F32) for _ in chunk)
        totals = lax.fori_loop(0, count, body, zeros, unroll=16)
        for i, t in enumerate(totals):
            parts[start + i : start + i + 1] = jnp.sum(t, axis=0, keepdims=True)


def lane_totals(parts):
    column = jnp.sum(parts[...], axis=1, keepdims=True)
    shape = (FAN, LANE)
    spread = jnp.where(iota(shape, 0) == iota(shape, 1), jnp.broadcast_to(column, shape), 0.0)
    return jnp.sum(spread, axis=0, keepdims=True)


def bounds(early, least, most, goals, measures, *, slab, sizes):
    total_x, total_y, total_z = sizes
    tiles = early.shape[0]
    xz = measure_xz(slab, total_x, total_z)
    goal = jnp.zeros((SUB, LANE), F32)
    for r in range(tiles):
        y = along(r * SUB + iota((SUB, LANE), 0), total_y, edge_tables(total_y)[1])
        for l in (0, 1):
            measure = xz[l] * y
            design = early[r, 4 + l]
            at = l * tiles + r
            least[at] = jnp.maximum(design - MOVE_LIMIT, 0.0) * measure
            most[at] = jnp.minimum(design + MOVE_LIMIT, 1.0) * measure
            measures[at] = measure
            goal = goal + design * measure
    goals[0:1] = jnp.sum(goal, axis=0, keepdims=True)


def first_round(got, early, least, most, goals, measures, gain, own, out, padded, parts, *, mode):
    tiles = got.shape[0]
    m = lax.axis_index(mode)
    for l in (0, 1):
        padded[l, :SUB] = jnp.zeros((SUB, LANE), F32)
        padded[l, (tiles + 1) * SUB :] = jnp.zeros((SUB, LANE), F32)
        for r in range(tiles):
            padded[l, (r + 1) * SUB : (r + 2) * SUB] = got[r, l]
    for l in (0, 1):
        for r in range(tiles):
            total = None
            for o in range(1 - FR, FR):
                start = (r + 1) * SUB + o
                t = float(FR - abs(o)) * padded[l, start : start + SUB]
                total = t if total is None else total + t
            at = l * tiles + r
            gain[at] = early[r, 4 + l] * jnp.sqrt(jnp.maximum(total, 0.0) * measures[at])
        total = None
        for o in range(1 - FR, FR):
            t = float(FR - abs(o)) * padded[l, pl.ds(m * SUB + SUB + o, SUB)]
            total = t if total is None else total + t
        own[l] = total
    levels = [float(np.exp(-0.5 * (LEVEL_LOW + COARSE * (i + 1)))) for i in range(FAN - 1)]
    volumes(levels, gain, least, most, parts)
    parts[FAN - 1 : FAN] = goals[0:1]
    row = lane_totals(parts)
    for k in range(out.shape[0]):
        out[k] = row


def added(got):
    total = got[0]
    for k in range(1, got.shape[0]):
        total = total + got[k]
    return total


def at_lane(row, k):
    return jnp.sum(jnp.where(iota(row.shape, 1) == k, row, 0.0), axis=1, keepdims=True)


def cells_above(row, goal):
    above = (row > goal) & (iota(row.shape, 1) < FAN - 1)
    return jnp.sum(jnp.where(above, 1.0, 0.0), axis=1, keepdims=True)


def second_round(got, gain, least, most, out, state, parts):
    row = added(got)
    goal = at_lane(row, FAN - 1)
    low = LEVEL_LOW + COARSE * cells_above(row, goal)
    state[0:1] = jnp.broadcast_to(low, (1, LANE))
    state[1:2] = jnp.broadcast_to(goal, (1, LANE))
    scale = jnp.exp(-0.5 * jnp.broadcast_to(low, (SUB, LANE)))
    levels = [scale * float(np.exp(-0.5 * FINE * (i + 1))) for i in range(FAN - 1)]
    volumes(levels, gain, least, most, parts)
    parts[FAN - 1 : FAN] = jnp.zeros((1, LANE), F32)
    row = lane_totals(parts)
    for k in range(out.shape[0]):
        out[k] = row


def last_update(got, state, own, design, sens_out, out, *, slab, mode, sizes):
    total_x, total_y, total_z = sizes
    m = lax.axis_index(mode)
    row = added(got)
    goal = state[1:2, 0:1]
    level = state[0:1, 0:1] + FINE * (cells_above(row, goal) + 0.5)
    scale = jnp.exp(jnp.broadcast_to(level, (SUB, LANE)))
    y = along(m * SUB + iota((SUB, LANE), 0), total_y, edge_tables(total_y)[1])
    xz = measure_xz(slab, total_x, total_z)
    for l in (0, 1):
        d, s = design[l], own[l]
        factor = jnp.sqrt(jnp.maximum(s, 0.0) / (scale * (xz[l] * y)))
        least = jnp.maximum(d - MOVE_LIMIT, 0.0)
        most = jnp.minimum(d + MOVE_LIMIT, 1.0)
        out[l] = jnp.minimum(jnp.maximum(d * factor, least), most)
        sens_out[l] = s


def call(kernel, outs, operands, specs=None, scratch=(), flops=1000, alias=None):
    outs = [jax.ShapeDtypeStruct(o, F32) for o in outs]
    size = sum(4 * int(np.prod(o.shape)) for o in (*outs, *operands))
    single = len(outs) == 1
    return pl.pallas_call(
        kernel,
        out_shape=outs[0] if single else outs,
        in_specs=specs or [VMEM] * len(operands),
        out_specs=VMEM if single else [VMEM] * len(outs),
        scratch_shapes=[pltpu.VMEM(s, F32) for s in scratch],
        cost_estimate=pl.CostEstimate(flops=flops, bytes_accessed=size, transcendentals=0),
        input_output_aliases=alias or {},
        compiler_params=pltpu.CompilerParams(vmem_limit_bytes=GRANT),
    )(*operands)


def from_before(value, axis):
    count = lax.axis_size(axis)
    return lax.ppermute(value, axis, [(i, i + 1) for i in range(count - 1)])


def from_after(value, axis):
    count = lax.axis_size(axis)
    return lax.ppermute(value, axis, [(i + 1, i) for i in range(count - 1)])


def exchange(value, axis):
    return lax.all_to_all(value, axis, 0, 0, tiled=True)


def local(design, mode_shapes, eigenvalues):
    slab, mode = "slab", "mode"
    slabs, modes = lax.axis_size(slab), lax.axis_size(mode)
    _, _, _, total_y, total_z = mode_shapes.shape
    sizes = (2 * slabs, total_y, total_z)
    pairs = (3, 2, 2, total_y + SUB, LANE)
    block = (2, SUB, LANE)
    padded = (2, total_y + 2 * SUB, LANE)
    place = dict(slab=slab, mode=mode, sizes=sizes)

    plane = from_after(mode_shapes[0, :, 0], slab)
    after = from_after(design, slab)
    before = from_before(design, slab)
    sent = call(
        first_layer,
        [(modes, 7, SUB, LANE)],
        [mode_shapes, eigenvalues],
        specs=[VMEM, SMEM],
        scratch=[pairs],
        flops=5_000_000,
    )
    sent, rows = call(
        functools.partial(second_layer, mode=mode),
        [(modes, 7, SUB, LANE), block],
        [mode_shapes, eigenvalues, plane, design, before, after, sent],
        specs=[VMEM, SMEM, VMEM, VMEM, VMEM, VMEM, VMEM],
        scratch=[pairs],
        flops=5_000_000,
        alias={6: 0},
    )
    early = exchange(sent, mode)
    gradient = call(functools.partial(own_gradient, **place), [block], [early, rows])
    after = from_after(gradient, slab)
    before = from_before(gradient, slab)
    copies = call(gradient_copies, [(modes, *block)], [gradient, before, after])
    whole = exchange(copies, mode)
    vectors = (2 * modes, SUB, LANE)
    least, most, goals, measures = call(
        functools.partial(bounds, slab=slab, sizes=sizes),
        [vectors, vectors, (SUB, LANE), vectors],
        [early],
        flops=100_000,
    )
    gain, own, sent = call(
        functools.partial(first_round, mode=mode),
        [vectors, block, (slabs, 1, LANE)],
        [whole, early, least, most, goals, measures],
        scratch=[padded, (FAN, LANE)],
    )
    got = exchange(sent, slab)
    sent, state = call(
        second_round,
        [(slabs, 1, LANE), (SUB, LANE)],
        [got, gain, least, most],
        scratch=[(FAN, LANE)],
    )
    got = exchange(sent, slab)
    return call(functools.partial(last_update, **place), [block, block], [got, state, own, design])


def solution(mesh):
    in_specs = (P("slab", "mode", None), P("mode", None, "slab", None, None), P("mode"))
    out_specs = (P("slab", "mode", None), P("slab", "mode", None))

    def step(design, mode_shapes, eigenvalues):
        return tuple(local(design, mode_shapes, eigenvalues))

    return jax.shard_map(step, mesh=mesh, in_specs=in_specs, out_specs=out_specs, check_vma=False)
```

```python
import functools

import jax
import jax.numpy as jnp
import numpy as np
from jax import lax
from jax.experimental import pallas as pl
from jax.experimental.pallas import tpu as pltpu
from jax.sharding import PartitionSpec as P


FR = 3
KS_SHARP = 2.0
PENALTY = 3.0
FLOOR_MODULUS = 0.001
MOVE_LIMIT = 0.2
POISSON = 0.3
LEVEL_LOW = -14.0
LEVEL_HIGH = 14.0
FAN = 64
COARSE = (LEVEL_HIGH - LEVEL_LOW) / FAN
FINE = COARSE / FAN
SUB, LANE = 8, 128
GRANT = 8 * 1024 * 1024
F32 = jnp.float32
VMEM = pl.BlockSpec(memory_space=pltpu.VMEM)
SMEM = pl.BlockSpec(memory_space=pltpu.SMEM)


def tent_1d(values):
    padded = np.pad(values, FR - 1)
    n = len(values)
    return sum((FR - abs(o)) * padded[FR - 1 + o : FR - 1 + o + n] for o in range(1 - FR, FR))


def edge_tables(n):
    span = tent_1d(np.ones(n))
    return 1.0 / span, tent_1d(1.0 / span)


def along(position, n, table):
    middle = float(table[n // 2])
    value = jnp.where(position >= 0, F32(middle), F32(0.0))
    for k in range(2 * (FR - 1)):
        if abs(table[k] - middle) > 1e-12:
            value = jnp.where((position == k) | (position == n - 1 - k), F32(table[k]), value)
    return value


def iota(shape, axis):
    return lax.broadcasted_iota(jnp.int32, shape, axis)


def tent_lanes(v):
    lanes = iota(v.shape, v.ndim - 1)
    axis = v.ndim - 1
    total = 3.0 * v
    for o in (1, 2):
        above = jnp.where(lanes < LANE - o, pltpu.roll(v, LANE - o, axis), 0.0)
        below = jnp.where(lanes >= o, pltpu.roll(v, o, axis), 0.0)
        total = total + float(FR - o) * (above + below)
    return total


def forms(load, eigen, store, pairs, tiles):
    lame = POISSON / ((1.0 + POISSON) * (1.0 - 2.0 * POISSON))
    shear = 0.5 / (1.0 + POISSON)
    rows = tiles * SUB
    lanes = iota((rows, LANE), 1)
    for c in range(3):
        for a in (0, 1):
            u = load(c, a)
            up = jnp.where(lanes < LANE - 1, pltpu.roll(u, LANE - 1, 1), 0.0)
            pairs[c, a, 0, :rows] = up + u
            pairs[c, a, 1, :rows] = up - u
            pairs[c, a, :, rows:] = jnp.zeros((2, SUB, LANE), F32)
    eigen_v = jnp.full((SUB, LANE), eigen, F32)
    weight = jnp.exp(-KS_SHARP * eigen_v)
    eigen_weight = weight * eigen_v
    normal = lame + 2.0 * shear
    ms, md = 0.25, 1.0 / 12.0
    m0, m1, m2, m3 = ms**3, ms * ms * md, ms * md * md, md**3

    def tile(r, _):
        base = pl.multiple_of(r * SUB, SUB)
        coef = {}
        for c in range(3):
            planes = []
            for a in (0, 1):
                here = {}
                for z in (0, 1):
                    p0 = pairs[c, a, z, pl.ds(base, SUB)]
                    p1 = pairs[c, a, z, pl.ds(base + 1, SUB)]
                    here[0, z] = p1 + p0
                    here[1, z] = p1 - p0
                planes.append(here)
            for y in (0, 1):
                for z in (0, 1):
                    coef[c, 0, y, z] = planes[1][y, z] + planes[0][y, z]
                    coef[c, 1, y, z] = planes[1][y, z] - planes[0][y, z]
        groups = [None] * 6
        for c in range(3):
            for x in (0, 1):
                for y in (0, 1):
                    for z in (0, 1):
                        d = (x, y, z)
                        n = x + y + z
                        g = {0: 0, 1: 1 if d[c] else 2, 2: 3 if d[c] else 4, 3: 5}[n]
                        v = coef[c, x, y, z]
                        groups[g] = v * v if groups[g] is None else groups[g] + v * v
        mass = m0 * groups[0] + m1 * (groups[1] + groups[2]) + m2 * (groups[3] + groups[4]) + m3 * groups[5]
        stiff = (
            (12.0 * m1 * normal) * groups[1]
            + (12.0 * m1 * shear) * groups[2]
            + (12.0 * m2 * (normal + shear)) * groups[3]
            + (12.0 * m2 * 2.0 * shear) * groups[4]
            + (12.0 * m3 * (normal + 2.0 * shear)) * groups[5]
        )
        for third in (0, 1):
            along_sum = across_sum = None
            for i, j, k in ((0, 1, 2), (0, 2, 1), (1, 2, 0)):

                def at(c, di, dj):
                    d = [0, 0, 0]
                    d[i], d[j], d[k] = di, dj, third
                    return coef[c, d[0], d[1], d[2]]

                t = at(i, 1, 0) * at(j, 0, 1)
                s = at(i, 0, 1) * at(j, 1, 0)
                along_sum = t if along_sum is None else along_sum + t
                across_sum = s if across_sum is None else across_sum + s
            m = (ms, md)[third] * 0.25
            stiff = stiff + (2.0 * lame * m) * along_sum + (2.0 * shear * m) * across_sum
        store(r, weight * stiff, eigen_weight * mass)
        return 0

    lax.fori_loop(0, tiles, tile, 0, unroll=2)
    return weight


def tail_rows(packed, k):
    start = packed.shape[0] - (2 - k) * SUB
    return packed[start : start + SUB]


def first_layer(modes, eigen, packed, out, pairs):
    def store(r, stiff, mass):
        out[r, 0] = stiff
        out[r, 1] = mass

    tiles = out.shape[0]
    forms(lambda c, a: modes[0, c, a], eigen[0], store, pairs, tiles)
    design = tail_rows(packed, 0), tail_rows(packed, 1)
    for r in range(tiles):
        out[r, 4] = design[0]
        out[r, 5] = design[1]


def shifted_rows(v, o):
    rows = iota(v.shape, 0)
    moved = pltpu.roll(v, (-o) % SUB, 0)
    return jnp.where((rows + o >= 0) & (rows + o < SUB), moved, 0.0)


def edge_rows(first, second):
    up, down = [], []
    for f in (first, second):
        up += [2.0 * f[7:8] + f[6:7], f[7:8]]
        down += [f[0:1], 2.0 * f[0:1] + f[1:2]]
    return jnp.concatenate(up, 0), jnp.concatenate(down, 0)


def second_layer(modes, eigen, packed, got, before, _, out, rows, pairs, *, mode):
    def store(r, stiff, mass):
        out[r, 2] = stiff
        out[r, 3] = mass

    tiles = out.shape[0]
    span = tiles * SUB

    def load(c, a):
        return got[c * span : (c + 1) * span] if a else modes[0, c, 1]

    m = lax.axis_index(mode)
    own = tail_rows(packed, 0), tail_rows(packed, 1)
    after = tail_rows(got, 0), tail_rows(got, 1)
    pair = across_x(own, before, after)
    up, down = edge_rows(*pair)
    for l in (0, 1):
        rows[l] = pair[l]
    weight = forms(load, eigen[0], store, pairs, tiles)
    half = SUB // 2
    for r in range(tiles):
        out[r, 6, :half] = jnp.where(m + 1 == r, up, weight[:half])
        out[r, 6, half:] = jnp.where(m - 1 == r, down, weight[half:])


def across_x(own, before, after):
    first = before[0] + 2.0 * before[1] + 3.0 * own[0] + 2.0 * own[1] + after[0]
    second = before[1] + 2.0 * own[0] + 3.0 * own[1] + 2.0 * after[0] + after[1]
    return first, second


def over_modes(got, at):
    total = got[0, at]
    for r in range(1, got.shape[0]):
        total = total + got[r, at]
    return total


def own_gradient(got, rows, out, *, slab, mode, sizes):
    total_x, total_y, total_z = sizes
    s, m = lax.axis_index(slab), lax.axis_index(mode)
    stiff = (over_modes(got, 0), over_modes(got, 2))
    mass = (over_modes(got, 1), over_modes(got, 3))
    tiles = got.shape[0]
    half = SUB // 2
    weight = None
    for r in range(tiles):
        w = jnp.where(m - 1 == r, got[r, 6, half : half + 1], got[r, 6, :1])
        weight = w if weight is None else weight + w
    inverse_weight = 1.0 / jnp.broadcast_to(weight, (SUB, LANE))
    from_last = jnp.where(m > 0, got[jnp.maximum(m - 1, 0), 6, :half], 0.0)
    from_next = jnp.where(m < tiles - 1, got[jnp.minimum(m + 1, tiles - 1), 6, half:], 0.0)
    inverse_yz = along(m * SUB + iota((SUB, LANE), 0), total_y, edge_tables(total_y)[0]) * along(
        iota((SUB, LANE), 1), total_z, edge_tables(total_z)[0]
    )
    for l in (0, 1):
        own = rows[l]
        near = jnp.concatenate(
            [from_last[2 * l : 2 * l + 2], jnp.zeros((4, LANE), F32), from_next[2 * l : 2 * l + 2]], 0
        )
        filtered = near
        for o in range(1 - FR, FR):
            filtered = filtered + float(FR - abs(o)) * (shifted_rows(own, o) if o else own)
        x = jnp.full((SUB, LANE), 2 * s + l, jnp.int32)
        inverse = inverse_yz * along(x, total_x, edge_tables(total_x)[0])
        density = tent_lanes(filtered) * inverse
        slope = (PENALTY * (1.0 - FLOOR_MODULUS)) * density * density
        out[l] = tent_lanes((slope * stiff[l] - mass[l]) * inverse_weight * inverse)


def gradient_copies(own, even, odd, out, *, slab):
    is_even = lax.rem(lax.axis_index(slab), 2) == 0
    before = [jnp.where(is_even, odd[l], even[l]) for l in (0, 1)]
    after = [jnp.where(is_even, even[l], odd[l]) for l in (0, 1)]
    pair = across_x(own, before, after)
    for r in range(out.shape[0]):
        out[r, 0] = pair[0]
        out[r, 1] = pair[1]


def measure_xz(slab, total_x, total_z):
    s = lax.axis_index(slab)
    z = along(iota((SUB, LANE), 1), total_z, edge_tables(total_z)[1])
    return [
        z * along(jnp.full((SUB, LANE), 2 * s + l, jnp.int32), total_x, edge_tables(total_x)[1])
        for l in (0, 1)
    ]


def volumes(levels, gain, least, most, parts):
    count = gain.shape[0]
    for start in range(0, len(levels), 8):
        chunk = levels[start : start + 8]

        def body(v, totals):
            g, lo, hi = gain[v], least[v], most[v]
            return tuple(
                t + jnp.minimum(jnp.maximum(g * q, lo), hi) for t, q in zip(totals, chunk)
            )

        zeros = tuple(jnp.zeros((SUB, LANE), F32) for _ in chunk)
        totals = lax.fori_loop(0, count, body, zeros, unroll=16)
        for i, t in enumerate(totals):
            parts[start + i : start + i + 1] = jnp.sum(t, axis=0, keepdims=True)


def lane_totals(parts):
    column = jnp.sum(parts[...], axis=1, keepdims=True)
    shape = (FAN, LANE)
    spread = jnp.where(iota(shape, 0) == iota(shape, 1), jnp.broadcast_to(column, shape), 0.0)
    return jnp.sum(spread, axis=0, keepdims=True)


def bounds(early, least, most, goals, measures, *, slab, sizes):
    total_x, total_y, total_z = sizes
    tiles = early.shape[0]
    xz = measure_xz(slab, total_x, total_z)
    goal = jnp.zeros((SUB, LANE), F32)
    for r in range(tiles):
        y = along(r * SUB + iota((SUB, LANE), 0), total_y, edge_tables(total_y)[1])
        for l in (0, 1):
            measure = xz[l] * y
            design = early[r, 4 + l]
            at = l * tiles + r
            least[at] = jnp.maximum(design - MOVE_LIMIT, 0.0) * measure
            most[at] = jnp.minimum(design + MOVE_LIMIT, 1.0) * measure
            measures[at] = measure
            goal = goal + design * measure
    goals[0:1] = jnp.sum(goal, axis=0, keepdims=True)


def first_round(got, early, least, most, goals, measures, gain, own, out, padded, parts, *, mode):
    tiles = got.shape[0]
    m = lax.axis_index(mode)
    for l in (0, 1):
        padded[l, :SUB] = jnp.zeros((SUB, LANE), F32)
        padded[l, (tiles + 1) * SUB :] = jnp.zeros((SUB, LANE), F32)
        for r in range(tiles):
            padded[l, (r + 1) * SUB : (r + 2) * SUB] = got[r, l]
    for l in (0, 1):
        for r in range(tiles):
            total = None
            for o in range(1 - FR, FR):
                start = (r + 1) * SUB + o
                t = float(FR - abs(o)) * padded[l, start : start + SUB]
                total = t if total is None else total + t
            at = l * tiles + r
            gain[at] = early[r, 4 + l] * jnp.sqrt(jnp.maximum(total, 0.0) * measures[at])
        total = None
        for o in range(1 - FR, FR):
            t = float(FR - abs(o)) * padded[l, pl.ds(m * SUB + SUB + o, SUB)]
            total = t if total is None else total + t
        own[l] = total
    levels = [float(np.exp(-0.5 * (LEVEL_LOW + COARSE * (i + 1)))) for i in range(FAN - 1)]
    volumes(levels, gain, least, most, parts)
    parts[FAN - 1 : FAN] = goals[0:1]
    row = lane_totals(parts)
    for k in range(out.shape[0]):
        out[k] = row


def added(got):
    total = got[0]
    for k in range(1, got.shape[0]):
        total = total + got[k]
    return total


def at_lane(row, k):
    return jnp.sum(jnp.where(iota(row.shape, 1) == k, row, 0.0), axis=1, keepdims=True)


def cells_above(row, goal):
    above = (row > goal) & (iota(row.shape, 1) < FAN - 1)
    return jnp.sum(jnp.where(above, 1.0, 0.0), axis=1, keepdims=True)


def second_round(got, gain, least, most, out, state, parts):
    row = added(got)
    goal = at_lane(row, FAN - 1)
    low = LEVEL_LOW + COARSE * cells_above(row, goal)
    state[0:1] = jnp.broadcast_to(low, (1, LANE))
    state[1:2] = jnp.broadcast_to(goal, (1, LANE))
    scale = jnp.exp(-0.5 * jnp.broadcast_to(low, (SUB, LANE)))
    levels = [scale * float(np.exp(-0.5 * FINE * (i + 1))) for i in range(FAN - 1)]
    volumes(levels, gain, least, most, parts)
    parts[FAN - 1 : FAN] = jnp.zeros((1, LANE), F32)
    row = lane_totals(parts)
    for k in range(out.shape[0]):
        out[k] = row


def last_update(got, state, own, design, sens_out, out, *, slab, mode, sizes):
    total_x, total_y, total_z = sizes
    m = lax.axis_index(mode)
    row = added(got)
    goal = state[1:2, 0:1]
    level = state[0:1, 0:1] + FINE * (cells_above(row, goal) + 0.5)
    scale = jnp.exp(jnp.broadcast_to(level, (SUB, LANE)))
    y = along(m * SUB + iota((SUB, LANE), 0), total_y, edge_tables(total_y)[1])
    xz = measure_xz(slab, total_x, total_z)
    for l in (0, 1):
        d, s = design[l], own[l]
        factor = jnp.sqrt(jnp.maximum(s, 0.0) / (scale * (xz[l] * y)))
        least = jnp.maximum(d - MOVE_LIMIT, 0.0)
        most = jnp.minimum(d + MOVE_LIMIT, 1.0)
        out[l] = jnp.minimum(jnp.maximum(d * factor, least), most)
        sens_out[l] = s


def call(kernel, outs, operands, specs=None, scratch=(), flops=1000, alias=None):
    outs = [jax.ShapeDtypeStruct(o, F32) for o in outs]
    size = sum(4 * int(np.prod(o.shape)) for o in (*outs, *operands))
    single = len(outs) == 1
    return pl.pallas_call(
        kernel,
        out_shape=outs[0] if single else outs,
        in_specs=specs or [VMEM] * len(operands),
        out_specs=VMEM if single else [VMEM] * len(outs),
        scratch_shapes=[pltpu.VMEM(s, F32) for s in scratch],
        cost_estimate=pl.CostEstimate(flops=flops, bytes_accessed=size, transcendentals=0),
        input_output_aliases=alias or {},
        compiler_params=pltpu.CompilerParams(vmem_limit_bytes=GRANT),
    )(*operands)


def from_before(value, axis):
    count = lax.axis_size(axis)
    return lax.ppermute(value, axis, [(i, i + 1) for i in range(count - 1)])


def from_after(value, axis):
    count = lax.axis_size(axis)
    return lax.ppermute(value, axis, [(i + 1, i) for i in range(count - 1)])


def swapped(value, axis, first):
    pairs = []
    for i in range(first, lax.axis_size(axis) - 1, 2):
        pairs += [(i, i + 1), (i + 1, i)]
    return lax.ppermute(value, axis, pairs)


def exchange(value, axis):
    return lax.all_to_all(value, axis, 0, 0, tiled=True)


def local(design, mode_shapes, eigenvalues):
    slab, mode = "slab", "mode"
    slabs, modes = lax.axis_size(slab), lax.axis_size(mode)
    _, _, _, total_y, total_z = mode_shapes.shape
    sizes = (2 * slabs, total_y, total_z)
    pairs = (3, 2, 2, total_y + SUB, LANE)
    block = (2, SUB, LANE)
    padded = (2, total_y + 2 * SUB, LANE)
    place = dict(slab=slab, mode=mode, sizes=sizes)

    packed = jnp.concatenate([mode_shapes[0, :, 0].reshape(-1, LANE), design.reshape(-1, LANE)], 0)
    got = from_after(packed, slab)
    before = from_before(design, slab)
    sent = call(
        first_layer,
        [(modes, 7, SUB, LANE)],
        [mode_shapes, eigenvalues, packed],
        specs=[VMEM, SMEM, VMEM],
        scratch=[pairs],
        flops=5_000_000,
    )
    sent, rows = call(
        functools.partial(second_layer, mode=mode),
        [(modes, 7, SUB, LANE), block],
        [mode_shapes, eigenvalues, packed, got, before, sent],
        specs=[VMEM, SMEM, VMEM, VMEM, VMEM, VMEM],
        scratch=[pairs],
        flops=5_000_000,
        alias={5: 0},
    )
    early = exchange(sent, mode)
    gradient = call(functools.partial(own_gradient, **place), [block], [early, rows])
    even = swapped(gradient, slab, 0)
    odd = swapped(gradient, slab, 1)
    copies = call(
        functools.partial(gradient_copies, slab=slab), [(modes, *block)], [gradient, even, odd]
    )
    whole = exchange(copies, mode)
    vectors = (2 * modes, SUB, LANE)
    least, most, goals, measures = call(
        functools.partial(bounds, slab=slab, sizes=sizes),
        [vectors, vectors, (SUB, LANE), vectors],
        [early],
        flops=100_000,
    )
    gain, own, sent = call(
        functools.partial(first_round, mode=mode),
        [vectors, block, (slabs, 1, LANE)],
        [whole, early, least, most, goals, measures],
        scratch=[padded, (FAN, LANE)],
    )
    got = exchange(sent, slab)
    sent, state = call(
        second_round,
        [(slabs, 1, LANE), (SUB, LANE)],
        [got, gain, least, most],
        scratch=[(FAN, LANE)],
    )
    got = exchange(sent, slab)
    return call(functools.partial(last_update, **place), [block, block], [got, state, own, design])


def solution(mesh):
    in_specs = (P("slab", "mode", None), P("mode", None, "slab", None, None), P("mode"))
    out_specs = (P("slab", "mode", None), P("slab", "mode", None))

    def step(design, mode_shapes, eigenvalues):
        return tuple(local(design, mode_shapes, eigenvalues))

    return jax.shard_map(step, mesh=mesh, in_specs=in_specs, out_specs=out_specs, check_vma=False)
```

```python
import functools

import jax
import jax.numpy as jnp
import numpy as np
from jax import lax
from jax.experimental import pallas as pl
from jax.experimental.pallas import tpu as pltpu
from jax.sharding import PartitionSpec as P


FR = 3
KS_SHARP = 2.0
PENALTY = 3.0
FLOOR_MODULUS = 0.001
MOVE_LIMIT = 0.2
POISSON = 0.3
LEVEL_LOW = -14.0
LEVEL_HIGH = 14.0
FAN = 64
COARSE = (LEVEL_HIGH - LEVEL_LOW) / FAN
FINE = COARSE / FAN
SUB, LANE = 8, 128
GRANT = 8 * 1024 * 1024
F32 = jnp.float32
VMEM = pl.BlockSpec(memory_space=pltpu.VMEM)
SMEM = pl.BlockSpec(memory_space=pltpu.SMEM)


def tent_1d(values):
    padded = np.pad(values, FR - 1)
    n = len(values)
    return sum((FR - abs(o)) * padded[FR - 1 + o : FR - 1 + o + n] for o in range(1 - FR, FR))


def edge_tables(n):
    span = tent_1d(np.ones(n))
    return 1.0 / span, tent_1d(1.0 / span)


def along(position, n, table):
    middle = float(table[n // 2])
    value = jnp.where(position >= 0, F32(middle), F32(0.0))
    for k in range(2 * (FR - 1)):
        if abs(table[k] - middle) > 1e-12:
            value = jnp.where((position == k) | (position == n - 1 - k), F32(table[k]), value)
    return value


def iota(shape, axis):
    return lax.broadcasted_iota(jnp.int32, shape, axis)


def tent_lanes(v):
    lanes = iota(v.shape, v.ndim - 1)
    axis = v.ndim - 1
    total = 3.0 * v
    for o in (1, 2):
        above = jnp.where(lanes < LANE - o, pltpu.roll(v, LANE - o, axis), 0.0)
        below = jnp.where(lanes >= o, pltpu.roll(v, o, axis), 0.0)
        total = total + float(FR - o) * (above + below)
    return total


def forms(load, eigen, store, pairs, tiles):
    lame = POISSON / ((1.0 + POISSON) * (1.0 - 2.0 * POISSON))
    shear = 0.5 / (1.0 + POISSON)
    rows = tiles * SUB
    lanes = iota((rows, LANE), 1)
    for c in range(3):
        for a in (0, 1):
            u = load(c, a)
            up = jnp.where(lanes < LANE - 1, pltpu.roll(u, LANE - 1, 1), 0.0)
            pairs[c, a, 0, :rows] = up + u
            pairs[c, a, 1, :rows] = up - u
            pairs[c, a, :, rows:] = jnp.zeros((2, SUB, LANE), F32)
    eigen_v = jnp.full((SUB, LANE), eigen, F32)
    weight = jnp.exp(-KS_SHARP * eigen_v)
    eigen_weight = weight * eigen_v
    normal = lame + 2.0 * shear
    ms, md = 0.25, 1.0 / 12.0
    m0, m1, m2, m3 = ms**3, ms * ms * md, ms * md * md, md**3

    def tile(r, _):
        base = pl.multiple_of(r * SUB, SUB)
        coef = {}
        for c in range(3):
            planes = []
            for a in (0, 1):
                here = {}
                for z in (0, 1):
                    p0 = pairs[c, a, z, pl.ds(base, SUB)]
                    p1 = pairs[c, a, z, pl.ds(base + 1, SUB)]
                    here[0, z] = p1 + p0
                    here[1, z] = p1 - p0
                planes.append(here)
            for y in (0, 1):
                for z in (0, 1):
                    coef[c, 0, y, z] = planes[1][y, z] + planes[0][y, z]
                    coef[c, 1, y, z] = planes[1][y, z] - planes[0][y, z]
        groups = [None] * 6
        for c in range(3):
            for x in (0, 1):
                for y in (0, 1):
                    for z in (0, 1):
                        d = (x, y, z)
                        n = x + y + z
                        g = {0: 0, 1: 1 if d[c] else 2, 2: 3 if d[c] else 4, 3: 5}[n]
                        v = coef[c, x, y, z]
                        groups[g] = v * v if groups[g] is None else groups[g] + v * v
        mass = m0 * groups[0] + m1 * (groups[1] + groups[2]) + m2 * (groups[3] + groups[4]) + m3 * groups[5]
        stiff = (
            (12.0 * m1 * normal) * groups[1]
            + (12.0 * m1 * shear) * groups[2]
            + (12.0 * m2 * (normal + shear)) * groups[3]
            + (12.0 * m2 * 2.0 * shear) * groups[4]
            + (12.0 * m3 * (normal + 2.0 * shear)) * groups[5]
        )
        for third in (0, 1):
            along_sum = across_sum = None
            for i, j, k in ((0, 1, 2), (0, 2, 1), (1, 2, 0)):

                def at(c, di, dj):
                    d = [0, 0, 0]
                    d[i], d[j], d[k] = di, dj, third
                    return coef[c, d[0], d[1], d[2]]

                t = at(i, 1, 0) * at(j, 0, 1)
                s = at(i, 0, 1) * at(j, 1, 0)
                along_sum = t if along_sum is None else along_sum + t
                across_sum = s if across_sum is None else across_sum + s
            m = (ms, md)[third] * 0.25
            stiff = stiff + (2.0 * lame * m) * along_sum + (2.0 * shear * m) * across_sum
        store(r, weight * stiff, eigen_weight * mass)
        return 0

    lax.fori_loop(0, tiles, tile, 0, unroll=2)
    return weight


def pack(modes, design, out, sems):
    planes, rows = modes.shape[1], modes.shape[3]
    copies = [
        pltpu.make_async_copy(modes.at[0, c, 0], out.at[pl.ds(c * rows, rows)], sems.at[c])
        for c in range(planes)
    ]
    for l in (0, 1):
        start = planes * rows + l * SUB
        copies.append(
            pltpu.make_async_copy(design.at[l], out.at[pl.ds(start, SUB)], sems.at[planes + l])
        )
    for copy in copies:
        copy.start()
    for copy in copies:
        copy.wait()


def tail_rows(packed, k):
    start = packed.shape[0] - (2 - k) * SUB
    return packed[start : start + SUB]


def first_layer(modes, eigen, packed, out, pairs):
    def store(r, stiff, mass):
        out[r, 0] = stiff
        out[r, 1] = mass

    tiles = out.shape[0]
    forms(lambda c, a: modes[0, c, a], eigen[0], store, pairs, tiles)
    design = tail_rows(packed, 0), tail_rows(packed, 1)
    for r in range(tiles):
        out[r, 4] = design[0]
        out[r, 5] = design[1]


def shifted_rows(v, o):
    rows = iota(v.shape, 0)
    moved = pltpu.roll(v, (-o) % SUB, 0)
    return jnp.where((rows + o >= 0) & (rows + o < SUB), moved, 0.0)


def edge_rows(first, second):
    up, down = [], []
    for f in (first, second):
        up += [2.0 * f[7:8] + f[6:7], f[7:8]]
        down += [f[0:1], 2.0 * f[0:1] + f[1:2]]
    return jnp.concatenate(up, 0), jnp.concatenate(down, 0)


def second_layer(modes, eigen, packed, got, before, _, out, rows, pairs, *, mode):
    def store(r, stiff, mass):
        out[r, 2] = stiff
        out[r, 3] = mass

    tiles = out.shape[0]
    span = tiles * SUB

    def load(c, a):
        return got[c * span : (c + 1) * span] if a else modes[0, c, 1]

    m = lax.axis_index(mode)
    own = tail_rows(packed, 0), tail_rows(packed, 1)
    after = tail_rows(got, 0), tail_rows(got, 1)
    pair = across_x(own, before, after)
    up, down = edge_rows(*pair)
    for l in (0, 1):
        rows[l] = pair[l]
    weight = forms(load, eigen[0], store, pairs, tiles)
    half = SUB // 2
    for r in range(tiles):
        out[r, 6, :half] = jnp.where(m + 1 == r, up, weight[:half])
        out[r, 6, half:] = jnp.where(m - 1 == r, down, weight[half:])


def across_x(own, before, after):
    first = before[0] + 2.0 * before[1] + 3.0 * own[0] + 2.0 * own[1] + after[0]
    second = before[1] + 2.0 * own[0] + 3.0 * own[1] + 2.0 * after[0] + after[1]
    return first, second


def over_modes(got, at):
    total = got[0, at]
    for r in range(1, got.shape[0]):
        total = total + got[r, at]
    return total


def own_gradient(got, rows, out, *, slab, mode, sizes):
    total_x, total_y, total_z = sizes
    s, m = lax.axis_index(slab), lax.axis_index(mode)
    stiff = (over_modes(got, 0), over_modes(got, 2))
    mass = (over_modes(got, 1), over_modes(got, 3))
    tiles = got.shape[0]
    half = SUB // 2
    weight = None
    for r in range(tiles):
        w = jnp.where(m - 1 == r, got[r, 6, half : half + 1], got[r, 6, :1])
        weight = w if weight is None else weight + w
    inverse_weight = 1.0 / jnp.broadcast_to(weight, (SUB, LANE))
    from_last = jnp.where(m > 0, got[jnp.maximum(m - 1, 0), 6, :half], 0.0)
    from_next = jnp.where(m < tiles - 1, got[jnp.minimum(m + 1, tiles - 1), 6, half:], 0.0)
    inverse_yz = along(m * SUB + iota((SUB, LANE), 0), total_y, edge_tables(total_y)[0]) * along(
        iota((SUB, LANE), 1), total_z, edge_tables(total_z)[0]
    )
    for l in (0, 1):
        own = rows[l]
        near = jnp.concatenate(
            [from_last[2 * l : 2 * l + 2], jnp.zeros((4, LANE), F32), from_next[2 * l : 2 * l + 2]], 0
        )
        filtered = near
        for o in range(1 - FR, FR):
            filtered = filtered + float(FR - abs(o)) * (shifted_rows(own, o) if o else own)
        x = jnp.full((SUB, LANE), 2 * s + l, jnp.int32)
        inverse = inverse_yz * along(x, total_x, edge_tables(total_x)[0])
        density = tent_lanes(filtered) * inverse
        slope = (PENALTY * (1.0 - FLOOR_MODULUS)) * density * density
        out[l] = tent_lanes((slope * stiff[l] - mass[l]) * inverse_weight * inverse)


def gradient_copies(own, even, odd, out, *, slab):
    is_even = lax.rem(lax.axis_index(slab), 2) == 0
    before = [jnp.where(is_even, odd[l], even[l]) for l in (0, 1)]
    after = [jnp.where(is_even, even[l], odd[l]) for l in (0, 1)]
    pair = across_x(own, before, after)
    for r in range(out.shape[0]):
        out[r, 0] = pair[0]
        out[r, 1] = pair[1]


def measure_xz(slab, total_x, total_z):
    s = lax.axis_index(slab)
    z = along(iota((SUB, LANE), 1), total_z, edge_tables(total_z)[1])
    return [
        z * along(jnp.full((SUB, LANE), 2 * s + l, jnp.int32), total_x, edge_tables(total_x)[1])
        for l in (0, 1)
    ]


def volumes(levels, gain, least, most, parts):
    count = gain.shape[0]
    for start in range(0, len(levels), 8):
        chunk = levels[start : start + 8]

        def body(v, totals):
            g, lo, hi = gain[v], least[v], most[v]
            return tuple(
                t + jnp.minimum(jnp.maximum(g * q, lo), hi) for t, q in zip(totals, chunk)
            )

        zeros = tuple(jnp.zeros((SUB, LANE), F32) for _ in chunk)
        totals = lax.fori_loop(0, count, body, zeros, unroll=16)
        for i, t in enumerate(totals):
            parts[start + i : start + i + 1] = jnp.sum(t, axis=0, keepdims=True)


def lane_totals(parts):
    column = jnp.sum(parts[...], axis=1, keepdims=True)
    shape = (FAN, LANE)
    spread = jnp.where(iota(shape, 0) == iota(shape, 1), jnp.broadcast_to(column, shape), 0.0)
    return jnp.sum(spread, axis=0, keepdims=True)


def bounds(early, least, most, goals, measures, *, slab, sizes):
    total_x, total_y, total_z = sizes
    tiles = early.shape[0]
    xz = measure_xz(slab, total_x, total_z)
    goal = jnp.zeros((SUB, LANE), F32)
    for r in range(tiles):
        y = along(r * SUB + iota((SUB, LANE), 0), total_y, edge_tables(total_y)[1])
        for l in (0, 1):
            measure = xz[l] * y
            design = early[r, 4 + l]
            at = l * tiles + r
            least[at] = jnp.maximum(design - MOVE_LIMIT, 0.0) * measure
            most[at] = jnp.minimum(design + MOVE_LIMIT, 1.0) * measure
            measures[at] = measure
            goal = goal + design * measure
    goals[0:1] = jnp.sum(goal, axis=0, keepdims=True)


def first_round(got, early, least, most, goals, measures, gain, own, out, padded, parts, *, mode):
    tiles = got.shape[0]
    m = lax.axis_index(mode)
    for l in (0, 1):
        padded[l, :SUB] = jnp.zeros((SUB, LANE), F32)
        padded[l, (tiles + 1) * SUB :] = jnp.zeros((SUB, LANE), F32)
        for r in range(tiles):
            padded[l, (r + 1) * SUB : (r + 2) * SUB] = got[r, l]
    for l in (0, 1):
        for r in range(tiles):
            total = None
            for o in range(1 - FR, FR):
                start = (r + 1) * SUB + o
                t = float(FR - abs(o)) * padded[l, start : start + SUB]
                total = t if total is None else total + t
            at = l * tiles + r
            gain[at] = early[r, 4 + l] * jnp.sqrt(jnp.maximum(total, 0.0) * measures[at])
        total = None
        for o in range(1 - FR, FR):
            t = float(FR - abs(o)) * padded[l, pl.ds(m * SUB + SUB + o, SUB)]
            total = t if total is None else total + t
        own[l] = total
    levels = [float(np.exp(-0.5 * (LEVEL_LOW + COARSE * (i + 1)))) for i in range(FAN - 1)]
    volumes(levels, gain, least, most, parts)
    parts[FAN - 1 : FAN] = goals[0:1]
    row = lane_totals(parts)
    for k in range(out.shape[0]):
        out[k] = row


def added(got):
    total = got[0]
    for k in range(1, got.shape[0]):
        total = total + got[k]
    return total


def at_lane(row, k):
    return jnp.sum(jnp.where(iota(row.shape, 1) == k, row, 0.0), axis=1, keepdims=True)


def cells_above(row, goal):
    above = (row > goal) & (iota(row.shape, 1) < FAN - 1)
    return jnp.sum(jnp.where(above, 1.0, 0.0), axis=1, keepdims=True)


def second_round(got, gain, least, most, out, state, parts):
    row = added(got)
    goal = at_lane(row, FAN - 1)
    low = LEVEL_LOW + COARSE * cells_above(row, goal)
    state[0:1] = jnp.broadcast_to(low, (1, LANE))
    state[1:2] = jnp.broadcast_to(goal, (1, LANE))
    scale = jnp.exp(-0.5 * jnp.broadcast_to(low, (SUB, LANE)))
    levels = [scale * float(np.exp(-0.5 * FINE * (i + 1))) for i in range(FAN - 1)]
    volumes(levels, gain, least, most, parts)
    parts[FAN - 1 : FAN] = jnp.zeros((1, LANE), F32)
    row = lane_totals(parts)
    for k in range(out.shape[0]):
        out[k] = row


def last_update(got, state, own, design, sens_out, out, *, slab, mode, sizes):
    total_x, total_y, total_z = sizes
    m = lax.axis_index(mode)
    row = added(got)
    goal = state[1:2, 0:1]
    level = state[0:1, 0:1] + FINE * (cells_above(row, goal) + 0.5)
    scale = jnp.exp(jnp.broadcast_to(level, (SUB, LANE)))
    y = along(m * SUB + iota((SUB, LANE), 0), total_y, edge_tables(total_y)[1])
    xz = measure_xz(slab, total_x, total_z)
    for l in (0, 1):
        d, s = design[l], own[l]
        factor = jnp.sqrt(jnp.maximum(s, 0.0) / (scale * (xz[l] * y)))
        least = jnp.maximum(d - MOVE_LIMIT, 0.0)
        most = jnp.minimum(d + MOVE_LIMIT, 1.0)
        out[l] = jnp.minimum(jnp.maximum(d * factor, least), most)
        sens_out[l] = s


def call(kernel, outs, operands, specs=None, scratch=(), flops=1000, alias=None):
    outs = [jax.ShapeDtypeStruct(o, F32) for o in outs]
    size = sum(4 * int(np.prod(o.shape)) for o in (*outs, *operands))
    single = len(outs) == 1
    return pl.pallas_call(
        kernel,
        out_shape=outs[0] if single else outs,
        in_specs=specs or [VMEM] * len(operands),
        out_specs=VMEM if single else [VMEM] * len(outs),
        scratch_shapes=[pltpu.VMEM(s, F32) for s in scratch],
        cost_estimate=pl.CostEstimate(flops=flops, bytes_accessed=size, transcendentals=0),
        input_output_aliases=alias or {},
        compiler_params=pltpu.CompilerParams(vmem_limit_bytes=GRANT),
    )(*operands)


def from_before(value, axis):
    count = lax.axis_size(axis)
    return lax.ppermute(value, axis, [(i, i + 1) for i in range(count - 1)])


def from_after(value, axis):
    count = lax.axis_size(axis)
    return lax.ppermute(value, axis, [(i + 1, i) for i in range(count - 1)])


def swapped(value, axis, first):
    pairs = []
    for i in range(first, lax.axis_size(axis) - 1, 2):
        pairs += [(i, i + 1), (i + 1, i)]
    return lax.ppermute(value, axis, pairs)


def exchange(value, axis):
    return lax.all_to_all(value, axis, 0, 0, tiled=True)


def local(design, mode_shapes, eigenvalues):
    slab, mode = "slab", "mode"
    slabs, modes = lax.axis_size(slab), lax.axis_size(mode)
    _, _, _, total_y, total_z = mode_shapes.shape
    sizes = (2 * slabs, total_y, total_z)
    pairs = (3, 2, 2, total_y + SUB, LANE)
    block = (2, SUB, LANE)
    padded = (2, total_y + 2 * SUB, LANE)
    place = dict(slab=slab, mode=mode, sizes=sizes)

    packed = pl.pallas_call(
        pack,
        out_shape=jax.ShapeDtypeStruct((3 * total_y + 2 * SUB, LANE), F32),
        in_specs=[pl.BlockSpec(memory_space=pltpu.HBM)] * 2,
        out_specs=VMEM,
        scratch_shapes=[pltpu.SemaphoreType.DMA((5,))],
        compiler_params=pltpu.CompilerParams(vmem_limit_bytes=GRANT),
        name="pack",
    )(
        pltpu.with_memory_space_constraint(mode_shapes, pltpu.HBM),
        pltpu.with_memory_space_constraint(design, pltpu.HBM),
    )
    got = from_after(packed, slab)
    before = from_before(design, slab)
    sent = call(
        first_layer,
        [(modes, 7, SUB, LANE)],
        [mode_shapes, eigenvalues, packed],
        specs=[VMEM, SMEM, VMEM],
        scratch=[pairs],
        flops=5_000_000,
    )
    sent, rows = call(
        functools.partial(second_layer, mode=mode),
        [(modes, 7, SUB, LANE), block],
        [mode_shapes, eigenvalues, packed, got, before, sent],
        specs=[VMEM, SMEM, VMEM, VMEM, VMEM, VMEM],
        scratch=[pairs],
        flops=5_000_000,
        alias={5: 0},
    )
    early = exchange(sent, mode)
    gradient = call(functools.partial(own_gradient, **place), [block], [early, rows])
    even = swapped(gradient, slab, 0)
    odd = swapped(gradient, slab, 1)
    copies = call(
        functools.partial(gradient_copies, slab=slab), [(modes, *block)], [gradient, even, odd]
    )
    whole = exchange(copies, mode)
    vectors = (2 * modes, SUB, LANE)
    least, most, goals, measures = call(
        functools.partial(bounds, slab=slab, sizes=sizes),
        [vectors, vectors, (SUB, LANE), vectors],
        [early],
        flops=100_000,
    )
    gain, own, sent = call(
        functools.partial(first_round, mode=mode),
        [vectors, block, (slabs, 1, LANE)],
        [whole, early, least, most, goals, measures],
        scratch=[padded, (FAN, LANE)],
    )
    got = exchange(sent, slab)
    sent, state = call(
        second_round,
        [(slabs, 1, LANE), (SUB, LANE)],
        [got, gain, least, most],
        scratch=[(FAN, LANE)],
    )
    got = exchange(sent, slab)
    return call(functools.partial(last_update, **place), [block, block], [got, state, own, design])


def solution(mesh):
    in_specs = (P("slab", "mode", None), P("mode", None, "slab", None, None), P("mode"))
    out_specs = (P("slab", "mode", None), P("slab", "mode", None))

    def step(design, mode_shapes, eigenvalues):
        return tuple(local(design, mode_shapes, eigenvalues))

    return jax.shard_map(step, mesh=mesh, in_specs=in_specs, out_specs=out_specs, check_vma=False)
```

```python
import functools

import jax
import jax.numpy as jnp
import numpy as np
from jax import lax
from jax.experimental import pallas as pl
from jax.experimental.pallas import tpu as pltpu
from jax.sharding import PartitionSpec as P


FR = 3
KS_SHARP = 2.0
PENALTY = 3.0
FLOOR_MODULUS = 0.001
MOVE_LIMIT = 0.2
POISSON = 0.3
LEVEL_LOW = -14.0
LEVEL_HIGH = 14.0
FAN = 64
COARSE = (LEVEL_HIGH - LEVEL_LOW) / FAN
FINE = COARSE / FAN
SUB, LANE = 8, 128
GRANT = 8 * 1024 * 1024
F32 = jnp.float32
VMEM = pl.BlockSpec(memory_space=pltpu.VMEM)
SMEM = pl.BlockSpec(memory_space=pltpu.SMEM)


def tent_1d(values):
    padded = np.pad(values, FR - 1)
    n = len(values)
    return sum((FR - abs(o)) * padded[FR - 1 + o : FR - 1 + o + n] for o in range(1 - FR, FR))


def edge_tables(n):
    span = tent_1d(np.ones(n))
    return 1.0 / span, tent_1d(1.0 / span)


def along(position, n, table):
    middle = float(table[n // 2])
    value = jnp.where(position >= 0, F32(middle), F32(0.0))
    for k in range(2 * (FR - 1)):
        if abs(table[k] - middle) > 1e-12:
            value = jnp.where((position == k) | (position == n - 1 - k), F32(table[k]), value)
    return value


def iota(shape, axis):
    return lax.broadcasted_iota(jnp.int32, shape, axis)


def tent_lanes(v):
    lanes = iota(v.shape, v.ndim - 1)
    axis = v.ndim - 1
    total = 3.0 * v
    for o in (1, 2):
        above = jnp.where(lanes < LANE - o, pltpu.roll(v, LANE - o, axis), 0.0)
        below = jnp.where(lanes >= o, pltpu.roll(v, o, axis), 0.0)
        total = total + float(FR - o) * (above + below)
    return total


def forms(load, eigen, store, pairs, tiles):
    lame = POISSON / ((1.0 + POISSON) * (1.0 - 2.0 * POISSON))
    shear = 0.5 / (1.0 + POISSON)
    rows = tiles * SUB
    lanes = iota((rows, LANE), 1)
    for c in range(3):
        for a in (0, 1):
            u = load(c, a)
            up = jnp.where(lanes < LANE - 1, pltpu.roll(u, LANE - 1, 1), 0.0)
            pairs[c, a, 0, :rows] = up + u
            pairs[c, a, 1, :rows] = up - u
            pairs[c, a, :, rows:] = jnp.zeros((2, SUB, LANE), F32)
    eigen_v = jnp.full((SUB, LANE), eigen, F32)
    weight = jnp.exp(-KS_SHARP * eigen_v)
    eigen_weight = weight * eigen_v
    normal = lame + 2.0 * shear
    ms, md = 0.25, 1.0 / 12.0
    m0, m1, m2, m3 = ms**3, ms * ms * md, ms * md * md, md**3

    def tile(r, _):
        base = pl.multiple_of(r * SUB, SUB)
        coef = {}
        for c in range(3):
            planes = []
            for a in (0, 1):
                here = {}
                for z in (0, 1):
                    p0 = pairs[c, a, z, pl.ds(base, SUB)]
                    p1 = pairs[c, a, z, pl.ds(base + 1, SUB)]
                    here[0, z] = p1 + p0
                    here[1, z] = p1 - p0
                planes.append(here)
            for y in (0, 1):
                for z in (0, 1):
                    coef[c, 0, y, z] = planes[1][y, z] + planes[0][y, z]
                    coef[c, 1, y, z] = planes[1][y, z] - planes[0][y, z]
        groups = [None] * 6
        for c in range(3):
            for x in (0, 1):
                for y in (0, 1):
                    for z in (0, 1):
                        d = (x, y, z)
                        n = x + y + z
                        g = {0: 0, 1: 1 if d[c] else 2, 2: 3 if d[c] else 4, 3: 5}[n]
                        v = coef[c, x, y, z]
                        groups[g] = v * v if groups[g] is None else groups[g] + v * v
        mass = m0 * groups[0] + m1 * (groups[1] + groups[2]) + m2 * (groups[3] + groups[4]) + m3 * groups[5]
        stiff = (
            (12.0 * m1 * normal) * groups[1]
            + (12.0 * m1 * shear) * groups[2]
            + (12.0 * m2 * (normal + shear)) * groups[3]
            + (12.0 * m2 * 2.0 * shear) * groups[4]
            + (12.0 * m3 * (normal + 2.0 * shear)) * groups[5]
        )
        for third in (0, 1):
            along_sum = across_sum = None
            for i, j, k in ((0, 1, 2), (0, 2, 1), (1, 2, 0)):

                def at(c, di, dj):
                    d = [0, 0, 0]
                    d[i], d[j], d[k] = di, dj, third
                    return coef[c, d[0], d[1], d[2]]

                t = at(i, 1, 0) * at(j, 0, 1)
                s = at(i, 0, 1) * at(j, 1, 0)
                along_sum = t if along_sum is None else along_sum + t
                across_sum = s if across_sum is None else across_sum + s
            m = (ms, md)[third] * 0.25
            stiff = stiff + (2.0 * lame * m) * along_sum + (2.0 * shear * m) * across_sum
        store(r, weight * stiff, eigen_weight * mass)
        return 0

    lax.fori_loop(0, tiles, tile, 0, unroll=2)
    return weight


def pack(modes, design, out, upper, sems):
    planes, rows = modes.shape[1], modes.shape[3]
    pieces = [(modes.at[0, c, 0], out, c * rows, rows) for c in range(planes)]
    pieces += [(design.at[l], out, planes * rows + l * SUB, SUB) for l in (0, 1)]
    pieces += [(modes.at[0, c, 1], upper, c * rows, rows) for c in range(planes)]
    copies = [
        pltpu.make_async_copy(source, to.at[pl.ds(start, size)], sems.at[k])
        for k, (source, to, start, size) in enumerate(pieces)
    ]
    for copy in copies:
        copy.start()
    for copy in copies:
        copy.wait()


def tail_rows(packed, k):
    start = packed.shape[0] - (2 - k) * SUB
    return packed[start : start + SUB]


def plane_rows(packed, c, rows):
    return packed[c * rows : (c + 1) * rows]


def first_layer(packed, upper, eigen, out, pairs):
    def store(r, stiff, mass):
        out[r, 0] = stiff
        out[r, 1] = mass

    tiles = out.shape[0]
    span = tiles * SUB

    def load(c, a):
        return plane_rows(upper if a else packed, c, span)

    forms(load, eigen[0], store, pairs, tiles)
    design = tail_rows(packed, 0), tail_rows(packed, 1)
    for r in range(tiles):
        out[r, 4] = design[0]
        out[r, 5] = design[1]


def shifted_rows(v, o):
    rows = iota(v.shape, 0)
    moved = pltpu.roll(v, (-o) % SUB, 0)
    return jnp.where((rows + o >= 0) & (rows + o < SUB), moved, 0.0)


def edge_rows(first, second):
    up, down = [], []
    for f in (first, second):
        up += [2.0 * f[7:8] + f[6:7], f[7:8]]
        down += [f[0:1], 2.0 * f[0:1] + f[1:2]]
    return jnp.concatenate(up, 0), jnp.concatenate(down, 0)


def second_layer(packed, upper, eigen, got, before, _, out, rows, pairs, *, mode):
    def store(r, stiff, mass):
        out[r, 2] = stiff
        out[r, 3] = mass

    tiles = out.shape[0]
    span = tiles * SUB

    def load(c, a):
        return plane_rows(got if a else upper, c, span)

    m = lax.axis_index(mode)
    own = tail_rows(packed, 0), tail_rows(packed, 1)
    after = tail_rows(got, 0), tail_rows(got, 1)
    pair = across_x(own, before, after)
    up, down = edge_rows(*pair)
    for l in (0, 1):
        rows[l] = pair[l]
    weight = forms(load, eigen[0], store, pairs, tiles)
    half = SUB // 2
    for r in range(tiles):
        out[r, 6, :half] = jnp.where(m + 1 == r, up, weight[:half])
        out[r, 6, half:] = jnp.where(m - 1 == r, down, weight[half:])


def across_x(own, before, after):
    first = before[0] + 2.0 * before[1] + 3.0 * own[0] + 2.0 * own[1] + after[0]
    second = before[1] + 2.0 * own[0] + 3.0 * own[1] + 2.0 * after[0] + after[1]
    return first, second


def over_modes(got, at):
    total = got[0, at]
    for r in range(1, got.shape[0]):
        total = total + got[r, at]
    return total


def own_gradient(got, rows, out, *, slab, mode, sizes):
    total_x, total_y, total_z = sizes
    s, m = lax.axis_index(slab), lax.axis_index(mode)
    stiff = (over_modes(got, 0), over_modes(got, 2))
    mass = (over_modes(got, 1), over_modes(got, 3))
    tiles = got.shape[0]
    half = SUB // 2
    weight = None
    for r in range(tiles):
        w = jnp.where(m - 1 == r, got[r, 6, half : half + 1], got[r, 6, :1])
        weight = w if weight is None else weight + w
    inverse_weight = 1.0 / jnp.broadcast_to(weight, (SUB, LANE))
    from_last = jnp.where(m > 0, got[jnp.maximum(m - 1, 0), 6, :half], 0.0)
    from_next = jnp.where(m < tiles - 1, got[jnp.minimum(m + 1, tiles - 1), 6, half:], 0.0)
    inverse_yz = along(m * SUB + iota((SUB, LANE), 0), total_y, edge_tables(total_y)[0]) * along(
        iota((SUB, LANE), 1), total_z, edge_tables(total_z)[0]
    )
    for l in (0, 1):
        own = rows[l]
        near = jnp.concatenate(
            [from_last[2 * l : 2 * l + 2], jnp.zeros((4, LANE), F32), from_next[2 * l : 2 * l + 2]], 0
        )
        filtered = near
        for o in range(1 - FR, FR):
            filtered = filtered + float(FR - abs(o)) * (shifted_rows(own, o) if o else own)
        x = jnp.full((SUB, LANE), 2 * s + l, jnp.int32)
        inverse = inverse_yz * along(x, total_x, edge_tables(total_x)[0])
        density = tent_lanes(filtered) * inverse
        slope = (PENALTY * (1.0 - FLOOR_MODULUS)) * density * density
        out[l] = tent_lanes((slope * stiff[l] - mass[l]) * inverse_weight * inverse)


def gradient_copies(own, even, odd, out, *, slab):
    is_even = lax.rem(lax.axis_index(slab), 2) == 0
    before = [jnp.where(is_even, odd[l], even[l]) for l in (0, 1)]
    after = [jnp.where(is_even, even[l], odd[l]) for l in (0, 1)]
    pair = across_x(own, before, after)
    for r in range(out.shape[0]):
        out[r, 0] = pair[0]
        out[r, 1] = pair[1]


def measure_xz(slab, total_x, total_z):
    s = lax.axis_index(slab)
    z = along(iota((SUB, LANE), 1), total_z, edge_tables(total_z)[1])
    return [
        z * along(jnp.full((SUB, LANE), 2 * s + l, jnp.int32), total_x, edge_tables(total_x)[1])
        for l in (0, 1)
    ]


def volumes(levels, gain, least, most, parts):
    count = gain.shape[0]
    for start in range(0, len(levels), 8):
        chunk = levels[start : start + 8]

        def body(v, totals):
            g, lo, hi = gain[v], least[v], most[v]
            return tuple(
                t + jnp.minimum(jnp.maximum(g * q, lo), hi) for t, q in zip(totals, chunk)
            )

        zeros = tuple(jnp.zeros((SUB, LANE), F32) for _ in chunk)
        totals = lax.fori_loop(0, count, body, zeros, unroll=16)
        for i, t in enumerate(totals):
            parts[start + i : start + i + 1] = jnp.sum(t, axis=0, keepdims=True)


def lane_totals(parts):
    column = jnp.sum(parts[...], axis=1, keepdims=True)
    shape = (FAN, LANE)
    spread = jnp.where(iota(shape, 0) == iota(shape, 1), jnp.broadcast_to(column, shape), 0.0)
    return jnp.sum(spread, axis=0, keepdims=True)


def bounds(early, least, most, goals, measures, *, slab, sizes):
    total_x, total_y, total_z = sizes
    tiles = early.shape[0]
    xz = measure_xz(slab, total_x, total_z)
    goal = jnp.zeros((SUB, LANE), F32)
    for r in range(tiles):
        y = along(r * SUB + iota((SUB, LANE), 0), total_y, edge_tables(total_y)[1])
        for l in (0, 1):
            measure = xz[l] * y
            design = early[r, 4 + l]
            at = l * tiles + r
            least[at] = jnp.maximum(design - MOVE_LIMIT, 0.0) * measure
            most[at] = jnp.minimum(design + MOVE_LIMIT, 1.0) * measure
            measures[at] = measure
            goal = goal + design * measure
    goals[0:1] = jnp.sum(goal, axis=0, keepdims=True)


def first_round(got, early, least, most, goals, measures, gain, own, out, padded, parts, *, mode):
    tiles = got.shape[0]
    m = lax.axis_index(mode)
    for l in (0, 1):
        padded[l, :SUB] = jnp.zeros((SUB, LANE), F32)
        padded[l, (tiles + 1) * SUB :] = jnp.zeros((SUB, LANE), F32)
        for r in range(tiles):
            padded[l, (r + 1) * SUB : (r + 2) * SUB] = got[r, l]
    for l in (0, 1):
        for r in range(tiles):
            total = None
            for o in range(1 - FR, FR):
                start = (r + 1) * SUB + o
                t = float(FR - abs(o)) * padded[l, start : start + SUB]
                total = t if total is None else total + t
            at = l * tiles + r
            gain[at] = early[r, 4 + l] * jnp.sqrt(jnp.maximum(total, 0.0) * measures[at])
        total = None
        for o in range(1 - FR, FR):
            t = float(FR - abs(o)) * padded[l, pl.ds(m * SUB + SUB + o, SUB)]
            total = t if total is None else total + t
        own[l] = total
    levels = [float(np.exp(-0.5 * (LEVEL_LOW + COARSE * (i + 1)))) for i in range(FAN - 1)]
    volumes(levels, gain, least, most, parts)
    parts[FAN - 1 : FAN] = goals[0:1]
    row = lane_totals(parts)
    for k in range(out.shape[0]):
        out[k] = row


def added(got):
    total = got[0]
    for k in range(1, got.shape[0]):
        total = total + got[k]
    return total


def at_lane(row, k):
    return jnp.sum(jnp.where(iota(row.shape, 1) == k, row, 0.0), axis=1, keepdims=True)


def cells_above(row, goal):
    above = (row > goal) & (iota(row.shape, 1) < FAN - 1)
    return jnp.sum(jnp.where(above, 1.0, 0.0), axis=1, keepdims=True)


def second_round(got, gain, least, most, out, state, parts):
    row = added(got)
    goal = at_lane(row, FAN - 1)
    low = LEVEL_LOW + COARSE * cells_above(row, goal)
    state[0:1] = jnp.broadcast_to(low, (1, LANE))
    state[1:2] = jnp.broadcast_to(goal, (1, LANE))
    scale = jnp.exp(-0.5 * jnp.broadcast_to(low, (SUB, LANE)))
    levels = [scale * float(np.exp(-0.5 * FINE * (i + 1))) for i in range(FAN - 1)]
    volumes(levels, gain, least, most, parts)
    parts[FAN - 1 : FAN] = jnp.zeros((1, LANE), F32)
    row = lane_totals(parts)
    for k in range(out.shape[0]):
        out[k] = row


def last_update(got, state, own, design, sens_out, out, *, slab, mode, sizes):
    total_x, total_y, total_z = sizes
    m = lax.axis_index(mode)
    row = added(got)
    goal = state[1:2, 0:1]
    level = state[0:1, 0:1] + FINE * (cells_above(row, goal) + 0.5)
    scale = jnp.exp(jnp.broadcast_to(level, (SUB, LANE)))
    y = along(m * SUB + iota((SUB, LANE), 0), total_y, edge_tables(total_y)[1])
    xz = measure_xz(slab, total_x, total_z)
    for l in (0, 1):
        d, s = design[l], own[l]
        factor = jnp.sqrt(jnp.maximum(s, 0.0) / (scale * (xz[l] * y)))
        least = jnp.maximum(d - MOVE_LIMIT, 0.0)
        most = jnp.minimum(d + MOVE_LIMIT, 1.0)
        out[l] = jnp.minimum(jnp.maximum(d * factor, least), most)
        sens_out[l] = s


def call(kernel, outs, operands, specs=None, scratch=(), flops=1000, alias=None):
    outs = [jax.ShapeDtypeStruct(o, F32) for o in outs]
    size = sum(4 * int(np.prod(o.shape)) for o in (*outs, *operands))
    single = len(outs) == 1
    return pl.pallas_call(
        kernel,
        out_shape=outs[0] if single else outs,
        in_specs=specs or [VMEM] * len(operands),
        out_specs=VMEM if single else [VMEM] * len(outs),
        scratch_shapes=[pltpu.VMEM(s, F32) for s in scratch],
        cost_estimate=pl.CostEstimate(flops=flops, bytes_accessed=size, transcendentals=0),
        input_output_aliases=alias or {},
        compiler_params=pltpu.CompilerParams(vmem_limit_bytes=GRANT),
    )(*operands)


def from_before(value, axis):
    count = lax.axis_size(axis)
    return lax.ppermute(value, axis, [(i, i + 1) for i in range(count - 1)])


def from_after(value, axis):
    count = lax.axis_size(axis)
    return lax.ppermute(value, axis, [(i + 1, i) for i in range(count - 1)])


def swapped(value, axis, first):
    pairs = []
    for i in range(first, lax.axis_size(axis) - 1, 2):
        pairs += [(i, i + 1), (i + 1, i)]
    return lax.ppermute(value, axis, pairs)


def exchange(value, axis):
    return lax.all_to_all(value, axis, 0, 0, tiled=True)


def local(design, mode_shapes, eigenvalues):
    slab, mode = "slab", "mode"
    slabs, modes = lax.axis_size(slab), lax.axis_size(mode)
    _, _, _, total_y, total_z = mode_shapes.shape
    sizes = (2 * slabs, total_y, total_z)
    pairs = (3, 2, 2, total_y + SUB, LANE)
    block = (2, SUB, LANE)
    padded = (2, total_y + 2 * SUB, LANE)
    place = dict(slab=slab, mode=mode, sizes=sizes)

    packed, upper = pl.pallas_call(
        pack,
        out_shape=[
            jax.ShapeDtypeStruct((3 * total_y + 2 * SUB, LANE), F32),
            jax.ShapeDtypeStruct((3 * total_y, LANE), F32),
        ],
        in_specs=[pl.BlockSpec(memory_space=pltpu.HBM)] * 2,
        out_specs=[VMEM] * 2,
        scratch_shapes=[pltpu.SemaphoreType.DMA((8,))],
        compiler_params=pltpu.CompilerParams(vmem_limit_bytes=GRANT),
        name="pack",
    )(
        pltpu.with_memory_space_constraint(mode_shapes, pltpu.HBM),
        pltpu.with_memory_space_constraint(design, pltpu.HBM),
    )
    got = from_after(packed, slab)
    before = from_before(design, slab)
    sent = call(
        first_layer,
        [(modes, 7, SUB, LANE)],
        [packed, upper, eigenvalues],
        specs=[VMEM, VMEM, SMEM],
        scratch=[pairs],
        flops=5_000_000,
    )
    sent, rows = call(
        functools.partial(second_layer, mode=mode),
        [(modes, 7, SUB, LANE), block],
        [packed, upper, eigenvalues, got, before, sent],
        specs=[VMEM, VMEM, SMEM, VMEM, VMEM, VMEM],
        scratch=[pairs],
        flops=5_000_000,
        alias={5: 0},
    )
    early = exchange(sent, mode)
    gradient = call(functools.partial(own_gradient, **place), [block], [early, rows])
    even = swapped(gradient, slab, 0)
    odd = swapped(gradient, slab, 1)
    copies = call(
        functools.partial(gradient_copies, slab=slab), [(modes, *block)], [gradient, even, odd]
    )
    whole = exchange(copies, mode)
    vectors = (2 * modes, SUB, LANE)
    least, most, goals, measures = call(
        functools.partial(bounds, slab=slab, sizes=sizes),
        [vectors, vectors, (SUB, LANE), vectors],
        [early],
        flops=100_000,
    )
    gain, own, sent = call(
        functools.partial(first_round, mode=mode),
        [vectors, block, (slabs, 1, LANE)],
        [whole, early, least, most, goals, measures],
        scratch=[padded, (FAN, LANE)],
    )
    got = exchange(sent, slab)
    sent, state = call(
        second_round,
        [(slabs, 1, LANE), (SUB, LANE)],
        [got, gain, least, most],
        scratch=[(FAN, LANE)],
    )
    got = exchange(sent, slab)
    return call(functools.partial(last_update, **place), [block, block], [got, state, own, design])


def solution(mesh):
    in_specs = (P("slab", "mode", None), P("mode", None, "slab", None, None), P("mode"))
    out_specs = (P("slab", "mode", None), P("slab", "mode", None))

    def step(design, mode_shapes, eigenvalues):
        return tuple(local(design, mode_shapes, eigenvalues))

    return jax.shard_map(step, mesh=mesh, in_specs=in_specs, out_specs=out_specs, check_vma=False)
```

```python
import functools

import jax
import jax.numpy as jnp
import numpy as np
from jax import lax
from jax.experimental import pallas as pl
from jax.experimental.pallas import tpu as pltpu
from jax.sharding import PartitionSpec as P


FR = 3
KS_SHARP = 2.0
PENALTY = 3.0
FLOOR_MODULUS = 0.001
MOVE_LIMIT = 0.2
POISSON = 0.3
LEVEL_LOW = -14.0
LEVEL_HIGH = 14.0
FAN = 64
COARSE = (LEVEL_HIGH - LEVEL_LOW) / FAN
FINE = COARSE / FAN
SUB, LANE = 8, 128
GRANT = 8 * 1024 * 1024
F32 = jnp.float32
VMEM = pl.BlockSpec(memory_space=pltpu.VMEM)
SMEM = pl.BlockSpec(memory_space=pltpu.SMEM)


def tent_1d(values):
    padded = np.pad(values, FR - 1)
    n = len(values)
    return sum((FR - abs(o)) * padded[FR - 1 + o : FR - 1 + o + n] for o in range(1 - FR, FR))


def edge_tables(n):
    span = tent_1d(np.ones(n))
    return 1.0 / span, tent_1d(1.0 / span)


def along(position, n, table):
    middle = float(table[n // 2])
    value = jnp.where(position >= 0, F32(middle), F32(0.0))
    for k in range(2 * (FR - 1)):
        if abs(table[k] - middle) > 1e-12:
            value = jnp.where((position == k) | (position == n - 1 - k), F32(table[k]), value)
    return value


def iota(shape, axis):
    return lax.broadcasted_iota(jnp.int32, shape, axis)


def tent_lanes(v):
    lanes = iota(v.shape, v.ndim - 1)
    axis = v.ndim - 1
    total = 3.0 * v
    for o in (1, 2):
        above = jnp.where(lanes < LANE - o, pltpu.roll(v, LANE - o, axis), 0.0)
        below = jnp.where(lanes >= o, pltpu.roll(v, o, axis), 0.0)
        total = total + float(FR - o) * (above + below)
    return total


def forms(load, eigen, store, pairs, tiles):
    lame = POISSON / ((1.0 + POISSON) * (1.0 - 2.0 * POISSON))
    shear = 0.5 / (1.0 + POISSON)
    rows = tiles * SUB
    lanes = iota((rows, LANE), 1)
    for c in range(3):
        for a in (0, 1):
            u = load(c, a)
            up = jnp.where(lanes < LANE - 1, pltpu.roll(u, LANE - 1, 1), 0.0)
            pairs[c, a, 0, :rows] = up + u
            pairs[c, a, 1, :rows] = up - u
            pairs[c, a, :, rows:] = jnp.zeros((2, SUB, LANE), F32)
    eigen_v = jnp.full((SUB, LANE), eigen, F32)
    weight = jnp.exp(-KS_SHARP * eigen_v)
    eigen_weight = weight * eigen_v
    normal = lame + 2.0 * shear
    ms, md = 0.25, 1.0 / 12.0
    m0, m1, m2, m3 = ms**3, ms * ms * md, ms * md * md, md**3

    def tile(r, _):
        base = pl.multiple_of(r * SUB, SUB)
        coef = {}
        for c in range(3):
            planes = []
            for a in (0, 1):
                here = {}
                for z in (0, 1):
                    p0 = pairs[c, a, z, pl.ds(base, SUB)]
                    p1 = pairs[c, a, z, pl.ds(base + 1, SUB)]
                    here[0, z] = p1 + p0
                    here[1, z] = p1 - p0
                planes.append(here)
            for y in (0, 1):
                for z in (0, 1):
                    coef[c, 0, y, z] = planes[1][y, z] + planes[0][y, z]
                    coef[c, 1, y, z] = planes[1][y, z] - planes[0][y, z]
        groups = [None] * 6
        for c in range(3):
            for x in (0, 1):
                for y in (0, 1):
                    for z in (0, 1):
                        d = (x, y, z)
                        n = x + y + z
                        g = {0: 0, 1: 1 if d[c] else 2, 2: 3 if d[c] else 4, 3: 5}[n]
                        v = coef[c, x, y, z]
                        groups[g] = v * v if groups[g] is None else groups[g] + v * v
        mass = m0 * groups[0] + m1 * (groups[1] + groups[2]) + m2 * (groups[3] + groups[4]) + m3 * groups[5]
        stiff = (
            (12.0 * m1 * normal) * groups[1]
            + (12.0 * m1 * shear) * groups[2]
            + (12.0 * m2 * (normal + shear)) * groups[3]
            + (12.0 * m2 * 2.0 * shear) * groups[4]
            + (12.0 * m3 * (normal + 2.0 * shear)) * groups[5]
        )
        for third in (0, 1):
            along_sum = across_sum = None
            for i, j, k in ((0, 1, 2), (0, 2, 1), (1, 2, 0)):

                def at(c, di, dj):
                    d = [0, 0, 0]
                    d[i], d[j], d[k] = di, dj, third
                    return coef[c, d[0], d[1], d[2]]

                t = at(i, 1, 0) * at(j, 0, 1)
                s = at(i, 0, 1) * at(j, 1, 0)
                along_sum = t if along_sum is None else along_sum + t
                across_sum = s if across_sum is None else across_sum + s
            m = (ms, md)[third] * 0.25
            stiff = stiff + (2.0 * lame * m) * along_sum + (2.0 * shear * m) * across_sum
        store(r, weight * stiff, eigen_weight * mass)
        return 0

    lax.fori_loop(0, tiles, tile, 0, unroll=2)
    return weight


def fetch(pieces, sems):
    return [
        pltpu.make_async_copy(source, to.at[pl.ds(start, size)], sems.at[k])
        for k, (source, to, start, size) in enumerate(pieces)
    ]


def pack(modes, design, out, sems):
    planes, rows = modes.shape[1], modes.shape[3]
    pieces = [(modes.at[0, c, 0], out, c * rows, rows) for c in range(planes)]
    pieces += [(design.at[l], out, planes * rows + l * SUB, SUB) for l in (0, 1)]
    copies = fetch(pieces, sems)
    for copy in copies:
        copy.start()
    for copy in copies:
        copy.wait()


def tail_rows(packed, k):
    start = packed.shape[0] - (2 - k) * SUB
    return packed[start : start + SUB]


def plane_rows(packed, c, rows):
    return packed[c * rows : (c + 1) * rows]


def first_layer(modes, packed, eigen, out, upper, pairs, sems):
    planes, rows = modes.shape[1], modes.shape[3]
    copies = fetch([(modes.at[0, c, 1], upper, c * rows, rows) for c in range(planes)], sems)
    for copy in copies:
        copy.start()
    design = tail_rows(packed, 0), tail_rows(packed, 1)
    for r in range(out.shape[0]):
        out[r, 4] = design[0]
        out[r, 5] = design[1]
    for copy in copies:
        copy.wait()

    def store(r, stiff, mass):
        out[r, 0] = stiff
        out[r, 1] = mass

    tiles = out.shape[0]
    span = tiles * SUB

    def load(c, a):
        return plane_rows(upper if a else packed, c, span)

    forms(load, eigen[0], store, pairs, tiles)


def shifted_rows(v, o):
    rows = iota(v.shape, 0)
    moved = pltpu.roll(v, (-o) % SUB, 0)
    return jnp.where((rows + o >= 0) & (rows + o < SUB), moved, 0.0)


def edge_rows(first, second):
    up, down = [], []
    for f in (first, second):
        up += [2.0 * f[7:8] + f[6:7], f[7:8]]
        down += [f[0:1], 2.0 * f[0:1] + f[1:2]]
    return jnp.concatenate(up, 0), jnp.concatenate(down, 0)


def second_layer(packed, upper, eigen, got, before, _, out, rows, pairs, *, mode):
    def store(r, stiff, mass):
        out[r, 2] = stiff
        out[r, 3] = mass

    tiles = out.shape[0]
    span = tiles * SUB

    def load(c, a):
        return plane_rows(got if a else upper, c, span)

    m = lax.axis_index(mode)
    own = tail_rows(packed, 0), tail_rows(packed, 1)
    after = tail_rows(got, 0), tail_rows(got, 1)
    pair = across_x(own, before, after)
    up, down = edge_rows(*pair)
    for l in (0, 1):
        rows[l] = pair[l]
    weight = forms(load, eigen[0], store, pairs, tiles)
    half = SUB // 2
    for r in range(tiles):
        out[r, 6, :half] = jnp.where(m + 1 == r, up, weight[:half])
        out[r, 6, half:] = jnp.where(m - 1 == r, down, weight[half:])


def across_x(own, before, after):
    first = before[0] + 2.0 * before[1] + 3.0 * own[0] + 2.0 * own[1] + after[0]
    second = before[1] + 2.0 * own[0] + 3.0 * own[1] + 2.0 * after[0] + after[1]
    return first, second


def over_modes(got, at):
    total = got[0, at]
    for r in range(1, got.shape[0]):
        total = total + got[r, at]
    return total


def own_gradient(got, rows, out, *, slab, mode, sizes):
    total_x, total_y, total_z = sizes
    s, m = lax.axis_index(slab), lax.axis_index(mode)
    stiff = (over_modes(got, 0), over_modes(got, 2))
    mass = (over_modes(got, 1), over_modes(got, 3))
    tiles = got.shape[0]
    half = SUB // 2
    weight = None
    for r in range(tiles):
        w = jnp.where(m - 1 == r, got[r, 6, half : half + 1], got[r, 6, :1])
        weight = w if weight is None else weight + w
    inverse_weight = 1.0 / jnp.broadcast_to(weight, (SUB, LANE))
    from_last = jnp.where(m > 0, got[jnp.maximum(m - 1, 0), 6, :half], 0.0)
    from_next = jnp.where(m < tiles - 1, got[jnp.minimum(m + 1, tiles - 1), 6, half:], 0.0)
    inverse_yz = along(m * SUB + iota((SUB, LANE), 0), total_y, edge_tables(total_y)[0]) * along(
        iota((SUB, LANE), 1), total_z, edge_tables(total_z)[0]
    )
    for l in (0, 1):
        own = rows[l]
        near = jnp.concatenate(
            [from_last[2 * l : 2 * l + 2], jnp.zeros((4, LANE), F32), from_next[2 * l : 2 * l + 2]], 0
        )
        filtered = near
        for o in range(1 - FR, FR):
            filtered = filtered + float(FR - abs(o)) * (shifted_rows(own, o) if o else own)
        x = jnp.full((SUB, LANE), 2 * s + l, jnp.int32)
        inverse = inverse_yz * along(x, total_x, edge_tables(total_x)[0])
        density = tent_lanes(filtered) * inverse
        slope = (PENALTY * (1.0 - FLOOR_MODULUS)) * density * density
        out[l] = tent_lanes((slope * stiff[l] - mass[l]) * inverse_weight * inverse)


def gradient_copies(own, even, odd, out, *, slab):
    is_even = lax.rem(lax.axis_index(slab), 2) == 0
    before = [jnp.where(is_even, odd[l], even[l]) for l in (0, 1)]
    after = [jnp.where(is_even, even[l], odd[l]) for l in (0, 1)]
    pair = across_x(own, before, after)
    for r in range(out.shape[0]):
        out[r, 0] = pair[0]
        out[r, 1] = pair[1]


def measure_xz(slab, total_x, total_z):
    s = lax.axis_index(slab)
    z = along(iota((SUB, LANE), 1), total_z, edge_tables(total_z)[1])
    return [
        z * along(jnp.full((SUB, LANE), 2 * s + l, jnp.int32), total_x, edge_tables(total_x)[1])
        for l in (0, 1)
    ]


def volumes(levels, gain, least, most, parts):
    count = gain.shape[0]
    for start in range(0, len(levels), 8):
        chunk = levels[start : start + 8]

        def body(v, totals):
            g, lo, hi = gain[v], least[v], most[v]
            return tuple(
                t + jnp.minimum(jnp.maximum(g * q, lo), hi) for t, q in zip(totals, chunk)
            )

        zeros = tuple(jnp.zeros((SUB, LANE), F32) for _ in chunk)
        totals = lax.fori_loop(0, count, body, zeros, unroll=16)
        for i, t in enumerate(totals):
            parts[start + i : start + i + 1] = jnp.sum(t, axis=0, keepdims=True)


def lane_totals(parts):
    column = jnp.sum(parts[...], axis=1, keepdims=True)
    shape = (FAN, LANE)
    mine = iota(shape, 0) == jnp.minimum(iota(shape, 1), FAN - 1)
    spread = jnp.where(mine, jnp.broadcast_to(column, shape), 0.0)
    return jnp.sum(spread, axis=0, keepdims=True)


def bounds(early, least, most, goals, measures, *, slab, sizes):
    total_x, total_y, total_z = sizes
    tiles = early.shape[0]
    xz = measure_xz(slab, total_x, total_z)
    goal = jnp.zeros((SUB, LANE), F32)
    for r in range(tiles):
        y = along(r * SUB + iota((SUB, LANE), 0), total_y, edge_tables(total_y)[1])
        for l in (0, 1):
            measure = xz[l] * y
            design = early[r, 4 + l]
            at = l * tiles + r
            least[at] = jnp.maximum(design - MOVE_LIMIT, 0.0) * measure
            most[at] = jnp.minimum(design + MOVE_LIMIT, 1.0) * measure
            measures[at] = measure
            goal = goal + design * measure
    goals[0:1] = jnp.sum(goal, axis=0, keepdims=True)


def first_round(got, early, least, most, goals, measures, gain, own, out, padded, parts, *, mode):
    tiles = got.shape[0]
    m = lax.axis_index(mode)
    for l in (0, 1):
        padded[l, :SUB] = jnp.zeros((SUB, LANE), F32)
        padded[l, (tiles + 1) * SUB :] = jnp.zeros((SUB, LANE), F32)
        for r in range(tiles):
            padded[l, (r + 1) * SUB : (r + 2) * SUB] = got[r, l]
    for l in (0, 1):
        for r in range(tiles):
            total = None
            for o in range(1 - FR, FR):
                start = (r + 1) * SUB + o
                t = float(FR - abs(o)) * padded[l, start : start + SUB]
                total = t if total is None else total + t
            at = l * tiles + r
            gain[at] = early[r, 4 + l] * jnp.sqrt(jnp.maximum(total, 0.0) * measures[at])
        total = None
        for o in range(1 - FR, FR):
            t = float(FR - abs(o)) * padded[l, pl.ds(m * SUB + SUB + o, SUB)]
            total = t if total is None else total + t
        own[l] = total
    levels = [float(np.exp(-0.5 * (LEVEL_LOW + COARSE * (i + 1)))) for i in range(FAN - 1)]
    volumes(levels, gain, least, most, parts)
    parts[FAN - 1 : FAN] = goals[0:1]
    row = lane_totals(parts)
    for k in range(out.shape[0]):
        out[k] = row


def added(got):
    rows = [got[k] for k in range(got.shape[0])]
    while len(rows) > 1:
        rows = [a + b for a, b in zip(rows[::2], rows[1::2])] + rows[len(rows) & ~1 :]
    return rows[0]


def cells_above(row, goal):
    above = (row > goal) & (iota(row.shape, 1) < FAN - 1)
    return jnp.sum(jnp.where(above, 1.0, 0.0), axis=1, keepdims=True)


def second_round(got, gain, least, most, out, state, parts):
    row = added(got)
    goal = pltpu.roll(row, LANE - FAN, 1)
    low = LEVEL_LOW + COARSE * cells_above(row, goal)
    state[0:1] = jnp.broadcast_to(low, (1, LANE))
    state[1:2] = goal
    scale = jnp.exp(-0.5 * jnp.broadcast_to(low, (SUB, LANE)))
    levels = [scale * float(np.exp(-0.5 * FINE * (i + 1))) for i in range(FAN - 1)]
    volumes(levels, gain, least, most, parts)
    parts[FAN - 1 : FAN] = jnp.zeros((1, LANE), F32)
    row = lane_totals(parts)
    for k in range(out.shape[0]):
        out[k] = row


def last_update(got, state, own, design, sens_out, out, *, slab, mode, sizes):
    total_x, total_y, total_z = sizes
    m = lax.axis_index(mode)
    row = added(got)
    goal = state[1:2]
    level = state[0:1, 0:1] + FINE * (cells_above(row, goal) + 0.5)
    scale = jnp.exp(jnp.broadcast_to(level, (SUB, LANE)))
    y = along(m * SUB + iota((SUB, LANE), 0), total_y, edge_tables(total_y)[1])
    xz = measure_xz(slab, total_x, total_z)
    for l in (0, 1):
        d, s = design[l], own[l]
        factor = jnp.sqrt(jnp.maximum(s, 0.0) / (scale * (xz[l] * y)))
        least = jnp.maximum(d - MOVE_LIMIT, 0.0)
        most = jnp.minimum(d + MOVE_LIMIT, 1.0)
        out[l] = jnp.minimum(jnp.maximum(d * factor, least), most)
        sens_out[l] = s


def call(kernel, outs, operands, specs=None, scratch=(), flops=1000, alias=None):
    outs = [jax.ShapeDtypeStruct(o, F32) for o in outs]
    size = sum(4 * int(np.prod(o.shape)) for o in (*outs, *operands))
    single = len(outs) == 1
    return pl.pallas_call(
        kernel,
        out_shape=outs[0] if single else outs,
        in_specs=specs or [VMEM] * len(operands),
        out_specs=VMEM if single else [VMEM] * len(outs),
        scratch_shapes=[pltpu.VMEM(s, F32) for s in scratch],
        cost_estimate=pl.CostEstimate(flops=flops, bytes_accessed=size, transcendentals=0),
        input_output_aliases=alias or {},
        compiler_params=pltpu.CompilerParams(vmem_limit_bytes=GRANT),
    )(*operands)


def from_before(value, axis):
    count = lax.axis_size(axis)
    return lax.ppermute(value, axis, [(i, i + 1) for i in range(count - 1)])


def from_after(value, axis):
    count = lax.axis_size(axis)
    return lax.ppermute(value, axis, [(i + 1, i) for i in range(count - 1)])


def swapped(value, axis, first):
    pairs = []
    for i in range(first, lax.axis_size(axis) - 1, 2):
        pairs += [(i, i + 1), (i + 1, i)]
    return lax.ppermute(value, axis, pairs)


def exchange(value, axis):
    return lax.all_to_all(value, axis, 0, 0, tiled=True)


def local(design, mode_shapes, eigenvalues):
    slab, mode = "slab", "mode"
    slabs, modes = lax.axis_size(slab), lax.axis_size(mode)
    _, _, _, total_y, total_z = mode_shapes.shape
    sizes = (2 * slabs, total_y, total_z)
    pairs = (3, 2, 2, total_y + SUB, LANE)
    block = (2, SUB, LANE)
    padded = (2, total_y + 2 * SUB, LANE)
    place = dict(slab=slab, mode=mode, sizes=sizes)

    held = pltpu.with_memory_space_constraint(mode_shapes, pltpu.HBM)
    params = pltpu.CompilerParams(vmem_limit_bytes=GRANT)
    hbm = pl.BlockSpec(memory_space=pltpu.HBM)
    packed = pl.pallas_call(
        pack,
        out_shape=jax.ShapeDtypeStruct((3 * total_y + 2 * SUB, LANE), F32),
        in_specs=[hbm, hbm],
        out_specs=VMEM,
        scratch_shapes=[pltpu.SemaphoreType.DMA((5,))],
        compiler_params=params,
        name="pack",
    )(held, pltpu.with_memory_space_constraint(design, pltpu.HBM))
    got = from_after(packed, slab)
    before = from_before(design, slab)
    sent, upper = pl.pallas_call(
        first_layer,
        out_shape=[
            jax.ShapeDtypeStruct((modes, 7, SUB, LANE), F32),
            jax.ShapeDtypeStruct((3 * total_y, LANE), F32),
        ],
        in_specs=[hbm, VMEM, SMEM],
        out_specs=[VMEM, VMEM],
        scratch_shapes=[pltpu.VMEM(pairs, F32), pltpu.SemaphoreType.DMA((3,))],
        cost_estimate=pl.CostEstimate(flops=5_000_000, bytes_accessed=600_000, transcendentals=0),
        compiler_params=params,
        name="first_layer",
    )(held, packed, eigenvalues)
    sent, rows = call(
        functools.partial(second_layer, mode=mode),
        [(modes, 7, SUB, LANE), block],
        [packed, upper, eigenvalues, got, before, sent],
        specs=[VMEM, VMEM, SMEM, VMEM, VMEM, VMEM],
        scratch=[pairs],
        flops=5_000_000,
        alias={5: 0},
    )
    early = exchange(sent, mode)
    gradient = call(functools.partial(own_gradient, **place), [block], [early, rows])
    even = swapped(gradient, slab, 0)
    odd = swapped(gradient, slab, 1)
    copies = call(
        functools.partial(gradient_copies, slab=slab), [(modes, *block)], [gradient, even, odd]
    )
    whole = exchange(copies, mode)
    vectors = (2 * modes, SUB, LANE)
    least, most, goals, measures = call(
        functools.partial(bounds, slab=slab, sizes=sizes),
        [vectors, vectors, (SUB, LANE), vectors],
        [early],
        flops=100_000,
    )
    gain, own, sent = call(
        functools.partial(first_round, mode=mode),
        [vectors, block, (slabs, 1, LANE)],
        [whole, early, least, most, goals, measures],
        scratch=[padded, (FAN, LANE)],
    )
    got = exchange(sent, slab)
    sent, state = call(
        second_round,
        [(slabs, 1, LANE), (SUB, LANE)],
        [got, gain, least, most],
        scratch=[(FAN, LANE)],
    )
    got = exchange(sent, slab)
    return call(functools.partial(last_update, **place), [block, block], [got, state, own, design])


def solution(mesh):
    in_specs = (P("slab", "mode", None), P("mode", None, "slab", None, None), P("mode"))
    out_specs = (P("slab", "mode", None), P("slab", "mode", None))

    def step(design, mode_shapes, eigenvalues):
        return tuple(local(design, mode_shapes, eigenvalues))

    return jax.shard_map(step, mesh=mesh, in_specs=in_specs, out_specs=out_specs, check_vma=False)
```

```python
import functools

import jax
import jax.numpy as jnp
import numpy as np
from jax import lax
from jax.experimental import pallas as pl
from jax.experimental.pallas import tpu as pltpu
from jax.sharding import PartitionSpec as P


FR = 3
KS_SHARP = 2.0
PENALTY = 3.0
FLOOR_MODULUS = 0.001
MOVE_LIMIT = 0.2
POISSON = 0.3
LEVEL_LOW = -14.0
LEVEL_HIGH = 14.0
FAN = 64
COARSE = (LEVEL_HIGH - LEVEL_LOW) / FAN
FINE = COARSE / FAN
SUB, LANE = 8, 128
GRANT = 8 * 1024 * 1024
F32 = jnp.float32
VMEM = pl.BlockSpec(memory_space=pltpu.VMEM)
SMEM = pl.BlockSpec(memory_space=pltpu.SMEM)


def tent_1d(values):
    padded = np.pad(values, FR - 1)
    n = len(values)
    return sum((FR - abs(o)) * padded[FR - 1 + o : FR - 1 + o + n] for o in range(1 - FR, FR))


def edge_tables(n):
    span = tent_1d(np.ones(n))
    return 1.0 / span, tent_1d(1.0 / span)


def along(position, n, table):
    middle = float(table[n // 2])
    value = jnp.where(position >= 0, F32(middle), F32(0.0))
    for k in range(2 * (FR - 1)):
        if abs(table[k] - middle) > 1e-12:
            value = jnp.where((position == k) | (position == n - 1 - k), F32(table[k]), value)
    return value


def iota(shape, axis):
    return lax.broadcasted_iota(jnp.int32, shape, axis)


def tent_lanes(v):
    lanes = iota(v.shape, v.ndim - 1)
    axis = v.ndim - 1
    total = 3.0 * v
    for o in (1, 2):
        above = jnp.where(lanes < LANE - o, pltpu.roll(v, LANE - o, axis), 0.0)
        below = jnp.where(lanes >= o, pltpu.roll(v, o, axis), 0.0)
        total = total + float(FR - o) * (above + below)
    return total


def forms(load, eigen, store, pairs, tiles):
    lame = POISSON / ((1.0 + POISSON) * (1.0 - 2.0 * POISSON))
    shear = 0.5 / (1.0 + POISSON)
    rows = tiles * SUB
    lanes = iota((rows, LANE), 1)
    for c in range(3):
        for a in (0, 1):
            u = load(c, a)
            up = jnp.where(lanes < LANE - 1, pltpu.roll(u, LANE - 1, 1), 0.0)
            pairs[c, a, 0, :rows] = up + u
            pairs[c, a, 1, :rows] = up - u
            pairs[c, a, :, rows:] = jnp.zeros((2, SUB, LANE), F32)
    eigen_v = jnp.full((SUB, LANE), eigen, F32)
    weight = jnp.exp(-KS_SHARP * eigen_v)
    eigen_weight = weight * eigen_v
    normal = lame + 2.0 * shear
    ms, md = 0.25, 1.0 / 12.0
    m0, m1, m2, m3 = ms**3, ms * ms * md, ms * md * md, md**3

    def tile(r, _):
        base = pl.multiple_of(r * SUB, SUB)
        coef = {}
        for c in range(3):
            planes = []
            for a in (0, 1):
                here = {}
                for z in (0, 1):
                    p0 = pairs[c, a, z, pl.ds(base, SUB)]
                    p1 = pairs[c, a, z, pl.ds(base + 1, SUB)]
                    here[0, z] = p1 + p0
                    here[1, z] = p1 - p0
                planes.append(here)
            for y in (0, 1):
                for z in (0, 1):
                    coef[c, 0, y, z] = planes[1][y, z] + planes[0][y, z]
                    coef[c, 1, y, z] = planes[1][y, z] - planes[0][y, z]
        groups = [None] * 6
        for c in range(3):
            for x in (0, 1):
                for y in (0, 1):
                    for z in (0, 1):
                        d = (x, y, z)
                        n = x + y + z
                        g = {0: 0, 1: 1 if d[c] else 2, 2: 3 if d[c] else 4, 3: 5}[n]
                        v = coef[c, x, y, z]
                        groups[g] = v * v if groups[g] is None else groups[g] + v * v
        mass = m0 * groups[0] + m1 * (groups[1] + groups[2]) + m2 * (groups[3] + groups[4]) + m3 * groups[5]
        stiff = (
            (12.0 * m1 * normal) * groups[1]
            + (12.0 * m1 * shear) * groups[2]
            + (12.0 * m2 * (normal + shear)) * groups[3]
            + (12.0 * m2 * 2.0 * shear) * groups[4]
            + (12.0 * m3 * (normal + 2.0 * shear)) * groups[5]
        )
        for third in (0, 1):
            along_sum = across_sum = None
            for i, j, k in ((0, 1, 2), (0, 2, 1), (1, 2, 0)):

                def at(c, di, dj):
                    d = [0, 0, 0]
                    d[i], d[j], d[k] = di, dj, third
                    return coef[c, d[0], d[1], d[2]]

                t = at(i, 1, 0) * at(j, 0, 1)
                s = at(i, 0, 1) * at(j, 1, 0)
                along_sum = t if along_sum is None else along_sum + t
                across_sum = s if across_sum is None else across_sum + s
            m = (ms, md)[third] * 0.25
            stiff = stiff + (2.0 * lame * m) * along_sum + (2.0 * shear * m) * across_sum
        store(r, weight * stiff, eigen_weight * mass)
        return 0

    lax.fori_loop(0, tiles, tile, 0, unroll=2)
    return weight


def fetch(pieces, sems):
    return [
        pltpu.make_async_copy(source, to.at[pl.ds(start, size)], sems.at[k])
        for k, (source, to, start, size) in enumerate(pieces)
    ]


def pack(modes, design, out, sems):
    planes, rows = modes.shape[1], modes.shape[3]
    pieces = [(modes.at[0, c, 0], out, c * rows, rows) for c in range(planes)]
    pieces += [(design.at[l], out, planes * rows + l * SUB, SUB) for l in (0, 1)]
    copies = fetch(pieces, sems)
    for copy in copies:
        copy.start()
    for copy in copies:
        copy.wait()


def tail_rows(packed, k):
    start = packed.shape[0] - (2 - k) * SUB
    return packed[start : start + SUB]


def plane_rows(packed, c, rows):
    return packed[c * rows : (c + 1) * rows]


def first_layer(modes, packed, eigen, out, upper, pairs, sems):
    planes, rows = modes.shape[1], modes.shape[3]
    copies = fetch([(modes.at[0, c, 1], upper, c * rows, rows) for c in range(planes)], sems)
    for copy in copies:
        copy.start()
    for copy in copies:
        copy.wait()

    def store(r, stiff, mass):
        out[r, 0] = stiff
        out[r, 1] = mass

    tiles = out.shape[0]
    span = tiles * SUB

    def load(c, a):
        return plane_rows(upper if a else packed, c, span)

    forms(load, eigen[0], store, pairs, tiles)


def shifted_rows(v, o):
    rows = iota(v.shape, 0)
    moved = pltpu.roll(v, (-o) % SUB, 0)
    return jnp.where((rows + o >= 0) & (rows + o < SUB), moved, 0.0)


def edge_rows(first, second):
    up, down = [], []
    for f in (first, second):
        up += [2.0 * f[7:8] + f[6:7], f[7:8]]
        down += [f[0:1], 2.0 * f[0:1] + f[1:2]]
    return jnp.concatenate(up, 0), jnp.concatenate(down, 0)


def second_layer(packed, upper, eigen, got, before, _, out, rows, pairs, *, mode):
    def store(r, stiff, mass):
        out[r, 2] = stiff
        out[r, 3] = mass

    tiles = out.shape[0]
    span = tiles * SUB

    def load(c, a):
        return plane_rows(got if a else upper, c, span)

    m = lax.axis_index(mode)
    own = tail_rows(packed, 0), tail_rows(packed, 1)
    after = tail_rows(got, 0), tail_rows(got, 1)
    pair = across_x(own, before, after)
    up, down = edge_rows(*pair)
    for l in (0, 1):
        rows[l] = pair[l]
    weight = forms(load, eigen[0], store, pairs, tiles)
    half = SUB // 2
    for r in range(tiles):
        out[r, 4, :half] = jnp.where(m + 1 == r, up, weight[:half])
        out[r, 4, half:] = jnp.where(m - 1 == r, down, weight[half:])


def across_x(own, before, after):
    first = before[0] + 2.0 * before[1] + 3.0 * own[0] + 2.0 * own[1] + after[0]
    second = before[1] + 2.0 * own[0] + 3.0 * own[1] + 2.0 * after[0] + after[1]
    return first, second


def over_modes(got, at):
    total = got[0, at]
    for r in range(1, got.shape[0]):
        total = total + got[r, at]
    return total


def own_gradient(got, rows, out, *, slab, mode, sizes):
    total_x, total_y, total_z = sizes
    s, m = lax.axis_index(slab), lax.axis_index(mode)
    stiff = (over_modes(got, 0), over_modes(got, 2))
    mass = (over_modes(got, 1), over_modes(got, 3))
    tiles = got.shape[0]
    half = SUB // 2
    weight = None
    for r in range(tiles):
        w = jnp.where(m - 1 == r, got[r, 4, half : half + 1], got[r, 4, :1])
        weight = w if weight is None else weight + w
    inverse_weight = 1.0 / jnp.broadcast_to(weight, (SUB, LANE))
    from_last = jnp.where(m > 0, got[jnp.maximum(m - 1, 0), 4, :half], 0.0)
    from_next = jnp.where(m < tiles - 1, got[jnp.minimum(m + 1, tiles - 1), 4, half:], 0.0)
    inverse_yz = along(m * SUB + iota((SUB, LANE), 0), total_y, edge_tables(total_y)[0]) * along(
        iota((SUB, LANE), 1), total_z, edge_tables(total_z)[0]
    )
    for l in (0, 1):
        own = rows[l]
        near = jnp.concatenate(
            [from_last[2 * l : 2 * l + 2], jnp.zeros((4, LANE), F32), from_next[2 * l : 2 * l + 2]], 0
        )
        filtered = near
        for o in range(1 - FR, FR):
            filtered = filtered + float(FR - abs(o)) * (shifted_rows(own, o) if o else own)
        x = jnp.full((SUB, LANE), 2 * s + l, jnp.int32)
        inverse = inverse_yz * along(x, total_x, edge_tables(total_x)[0])
        density = tent_lanes(filtered) * inverse
        slope = (PENALTY * (1.0 - FLOOR_MODULUS)) * density * density
        out[l] = tent_lanes((slope * stiff[l] - mass[l]) * inverse_weight * inverse)


def gradient_copies(own, even, odd, packed, out, *, slab):
    is_even = lax.rem(lax.axis_index(slab), 2) == 0
    before = [jnp.where(is_even, odd[l], even[l]) for l in (0, 1)]
    after = [jnp.where(is_even, even[l], odd[l]) for l in (0, 1)]
    pair = across_x(own, before, after)
    for r in range(out.shape[0]):
        out[r, 0] = pair[0]
        out[r, 1] = pair[1]
        out[r, 2] = tail_rows(packed, 0)
        out[r, 3] = tail_rows(packed, 1)


def measure_xz(slab, total_x, total_z):
    s = lax.axis_index(slab)
    z = along(iota((SUB, LANE), 1), total_z, edge_tables(total_z)[1])
    return [
        z * along(jnp.full((SUB, LANE), 2 * s + l, jnp.int32), total_x, edge_tables(total_x)[1])
        for l in (0, 1)
    ]


def volumes(levels, gain, least, most, parts):
    count = gain.shape[0]
    for start in range(0, len(levels), 8):
        chunk = levels[start : start + 8]

        def body(v, totals):
            g, lo, hi = gain[v], least[v], most[v]
            return tuple(
                t + jnp.minimum(jnp.maximum(g * q, lo), hi) for t, q in zip(totals, chunk)
            )

        zeros = tuple(jnp.zeros((SUB, LANE), F32) for _ in chunk)
        totals = lax.fori_loop(0, count, body, zeros, unroll=16)
        for i, t in enumerate(totals):
            parts[start + i : start + i + 1] = jnp.sum(t, axis=0, keepdims=True)


def lane_totals(parts):
    column = jnp.sum(parts[...], axis=1, keepdims=True)
    shape = (FAN, LANE)
    mine = iota(shape, 0) == jnp.minimum(iota(shape, 1), FAN - 1)
    spread = jnp.where(mine, jnp.broadcast_to(column, shape), 0.0)
    return jnp.sum(spread, axis=0, keepdims=True)


def bounds(early, least, most, goals, measures, *, slab, sizes):
    total_x, total_y, total_z = sizes
    tiles = early.shape[0]
    xz = measure_xz(slab, total_x, total_z)
    goal = jnp.zeros((SUB, LANE), F32)
    for r in range(tiles):
        y = along(r * SUB + iota((SUB, LANE), 0), total_y, edge_tables(total_y)[1])
        for l in (0, 1):
            measure = xz[l] * y
            design = early[r, 2 + l]
            at = l * tiles + r
            least[at] = jnp.maximum(design - MOVE_LIMIT, 0.0) * measure
            most[at] = jnp.minimum(design + MOVE_LIMIT, 1.0) * measure
            measures[at] = measure
            goal = goal + design * measure
    goals[0:1] = jnp.sum(goal, axis=0, keepdims=True)


def first_round(got, least, most, goals, measures, gain, own, out, padded, parts, *, mode):
    tiles = got.shape[0]
    m = lax.axis_index(mode)
    for l in (0, 1):
        padded[l, :SUB] = jnp.zeros((SUB, LANE), F32)
        padded[l, (tiles + 1) * SUB :] = jnp.zeros((SUB, LANE), F32)
        for r in range(tiles):
            padded[l, (r + 1) * SUB : (r + 2) * SUB] = got[r, l]
    for l in (0, 1):
        for r in range(tiles):
            total = None
            for o in range(1 - FR, FR):
                start = (r + 1) * SUB + o
                t = float(FR - abs(o)) * padded[l, start : start + SUB]
                total = t if total is None else total + t
            at = l * tiles + r
            gain[at] = got[r, 2 + l] * jnp.sqrt(jnp.maximum(total, 0.0) * measures[at])
        total = None
        for o in range(1 - FR, FR):
            t = float(FR - abs(o)) * padded[l, pl.ds(m * SUB + SUB + o, SUB)]
            total = t if total is None else total + t
        own[l] = total
    levels = [float(np.exp(-0.5 * (LEVEL_LOW + COARSE * (i + 1)))) for i in range(FAN - 1)]
    volumes(levels, gain, least, most, parts)
    parts[FAN - 1 : FAN] = goals[0:1]
    row = lane_totals(parts)
    for k in range(out.shape[0]):
        out[k] = row


def added(got):
    rows = [got[k] for k in range(got.shape[0])]
    while len(rows) > 1:
        rows = [a + b for a, b in zip(rows[::2], rows[1::2])] + rows[len(rows) & ~1 :]
    return rows[0]


def cells_above(row, goal):
    above = (row > goal) & (iota(row.shape, 1) < FAN - 1)
    return jnp.sum(jnp.where(above, 1.0, 0.0), axis=1, keepdims=True)


def second_round(got, gain, least, most, out, state, parts):
    row = added(got)
    goal = pltpu.roll(row, LANE - FAN, 1)
    low = LEVEL_LOW + COARSE * cells_above(row, goal)
    state[0:1] = jnp.broadcast_to(low, (1, LANE))
    state[1:2] = goal
    scale = jnp.exp(-0.5 * jnp.broadcast_to(low, (SUB, LANE)))
    levels = [scale * float(np.exp(-0.5 * FINE * (i + 1))) for i in range(FAN - 1)]
    volumes(levels, gain, least, most, parts)
    parts[FAN - 1 : FAN] = jnp.zeros((1, LANE), F32)
    row = lane_totals(parts)
    for k in range(out.shape[0]):
        out[k] = row


def last_update(got, state, own, design, sens_out, out, *, slab, mode, sizes):
    total_x, total_y, total_z = sizes
    m = lax.axis_index(mode)
    row = added(got)
    goal = state[1:2]
    level = state[0:1, 0:1] + FINE * (cells_above(row, goal) + 0.5)
    scale = jnp.exp(jnp.broadcast_to(level, (SUB, LANE)))
    y = along(m * SUB + iota((SUB, LANE), 0), total_y, edge_tables(total_y)[1])
    xz = measure_xz(slab, total_x, total_z)
    for l in (0, 1):
        d, s = design[l], own[l]
        factor = jnp.sqrt(jnp.maximum(s, 0.0) / (scale * (xz[l] * y)))
        least = jnp.maximum(d - MOVE_LIMIT, 0.0)
        most = jnp.minimum(d + MOVE_LIMIT, 1.0)
        out[l] = jnp.minimum(jnp.maximum(d * factor, least), most)
        sens_out[l] = s


def call(kernel, outs, operands, specs=None, scratch=(), flops=1000, alias=None):
    outs = [jax.ShapeDtypeStruct(o, F32) for o in outs]
    size = sum(4 * int(np.prod(o.shape)) for o in (*outs, *operands))
    single = len(outs) == 1
    return pl.pallas_call(
        kernel,
        out_shape=outs[0] if single else outs,
        in_specs=specs or [VMEM] * len(operands),
        out_specs=VMEM if single else [VMEM] * len(outs),
        scratch_shapes=[pltpu.VMEM(s, F32) for s in scratch],
        cost_estimate=pl.CostEstimate(flops=flops, bytes_accessed=size, transcendentals=0),
        input_output_aliases=alias or {},
        compiler_params=pltpu.CompilerParams(vmem_limit_bytes=GRANT),
    )(*operands)


def from_before(value, axis):
    count = lax.axis_size(axis)
    return lax.ppermute(value, axis, [(i, i + 1) for i in range(count - 1)])


def from_after(value, axis):
    count = lax.axis_size(axis)
    return lax.ppermute(value, axis, [(i + 1, i) for i in range(count - 1)])


def swapped(value, axis, first):
    pairs = []
    for i in range(first, lax.axis_size(axis) - 1, 2):
        pairs += [(i, i + 1), (i + 1, i)]
    return lax.ppermute(value, axis, pairs)


def exchange(value, axis):
    return lax.all_to_all(value, axis, 0, 0, tiled=True)


def local(design, mode_shapes, eigenvalues):
    slab, mode = "slab", "mode"
    slabs, modes = lax.axis_size(slab), lax.axis_size(mode)
    _, _, _, total_y, total_z = mode_shapes.shape
    sizes = (2 * slabs, total_y, total_z)
    pairs = (3, 2, 2, total_y + SUB, LANE)
    block = (2, SUB, LANE)
    padded = (2, total_y + 2 * SUB, LANE)
    place = dict(slab=slab, mode=mode, sizes=sizes)

    held = pltpu.with_memory_space_constraint(mode_shapes, pltpu.HBM)
    params = pltpu.CompilerParams(vmem_limit_bytes=GRANT)
    hbm = pl.BlockSpec(memory_space=pltpu.HBM)
    packed = pl.pallas_call(
        pack,
        out_shape=jax.ShapeDtypeStruct((3 * total_y + 2 * SUB, LANE), F32),
        in_specs=[hbm, hbm],
        out_specs=VMEM,
        scratch_shapes=[pltpu.SemaphoreType.DMA((5,))],
        compiler_params=params,
        name="pack",
    )(held, pltpu.with_memory_space_constraint(design, pltpu.HBM))
    got = from_after(packed, slab)
    before = from_before(design, slab)
    sent, upper = pl.pallas_call(
        first_layer,
        out_shape=[
            jax.ShapeDtypeStruct((modes, 5, SUB, LANE), F32),
            jax.ShapeDtypeStruct((3 * total_y, LANE), F32),
        ],
        in_specs=[hbm, VMEM, SMEM],
        out_specs=[VMEM, VMEM],
        scratch_shapes=[pltpu.VMEM(pairs, F32), pltpu.SemaphoreType.DMA((3,))],
        cost_estimate=pl.CostEstimate(flops=5_000_000, bytes_accessed=600_000, transcendentals=0),
        compiler_params=params,
        name="first_layer",
    )(held, packed, eigenvalues)
    sent, rows = call(
        functools.partial(second_layer, mode=mode),
        [(modes, 5, SUB, LANE), block],
        [packed, upper, eigenvalues, got, before, sent],
        specs=[VMEM, VMEM, SMEM, VMEM, VMEM, VMEM],
        scratch=[pairs],
        flops=5_000_000,
        alias={5: 0},
    )
    early = exchange(sent, mode)
    gradient = call(functools.partial(own_gradient, **place), [block], [early, rows])
    even = swapped(gradient, slab, 0)
    odd = swapped(gradient, slab, 1)
    copies = call(
        functools.partial(gradient_copies, slab=slab),
        [(modes, 4, SUB, LANE)],
        [gradient, even, odd, packed],
    )
    whole = exchange(copies, mode)
    vectors = (2 * modes, SUB, LANE)
    least, most, goals, measures = call(
        functools.partial(bounds, slab=slab, sizes=sizes),
        [vectors, vectors, (SUB, LANE), vectors],
        [whole],
        flops=100_000,
    )
    gain, own, sent = call(
        functools.partial(first_round, mode=mode),
        [vectors, block, (slabs, 1, LANE)],
        [whole, least, most, goals, measures],
        scratch=[padded, (FAN, LANE)],
    )
    got = exchange(sent, slab)
    sent, state = call(
        second_round,
        [(slabs, 1, LANE), (SUB, LANE)],
        [got, gain, least, most],
        scratch=[(FAN, LANE)],
    )
    got = exchange(sent, slab)
    return call(functools.partial(last_update, **place), [block, block], [got, state, own, design])


def solution(mesh):
    in_specs = (P("slab", "mode", None), P("mode", None, "slab", None, None), P("mode"))
    out_specs = (P("slab", "mode", None), P("slab", "mode", None))

    def step(design, mode_shapes, eigenvalues):
        return tuple(local(design, mode_shapes, eigenvalues))

    return jax.shard_map(step, mesh=mesh, in_specs=in_specs, out_specs=out_specs, check_vma=False)
```

```python
import functools

import jax
import jax.numpy as jnp
import numpy as np
from jax import lax
from jax.experimental import pallas as pl
from jax.experimental.pallas import tpu as pltpu
from jax.sharding import Mesh
from jax.sharding import PartitionSpec as P


FR = 3
KS_SHARP = 2.0
PENALTY = 3.0
FLOOR_MODULUS = 0.001
MOVE_LIMIT = 0.2
POISSON = 0.3
LEVEL_LOW = -14.0
LEVEL_HIGH = 14.0
FAN = 64
COARSE = (LEVEL_HIGH - LEVEL_LOW) / FAN
FINE = COARSE / FAN
SUB, LANE = 8, 128
GRANT = 8 * 1024 * 1024
F32 = jnp.float32
VMEM = pl.BlockSpec(memory_space=pltpu.VMEM)
SMEM = pl.BlockSpec(memory_space=pltpu.SMEM)


def tent_1d(values):
    padded = np.pad(values, FR - 1)
    n = len(values)
    return sum((FR - abs(o)) * padded[FR - 1 + o : FR - 1 + o + n] for o in range(1 - FR, FR))


def edge_tables(n):
    span = tent_1d(np.ones(n))
    return 1.0 / span, tent_1d(1.0 / span)


def along(position, n, table):
    middle = float(table[n // 2])
    value = jnp.where(position >= 0, F32(middle), F32(0.0))
    for k in range(2 * (FR - 1)):
        if abs(table[k] - middle) > 1e-12:
            value = jnp.where((position == k) | (position == n - 1 - k), F32(table[k]), value)
    return value


def mode_index():
    return 2 * lax.axis_index("row") + lax.axis_index("core")


def iota(shape, axis):
    return lax.broadcasted_iota(jnp.int32, shape, axis)


def tent_lanes(v):
    lanes = iota(v.shape, v.ndim - 1)
    axis = v.ndim - 1
    total = 3.0 * v
    for o in (1, 2):
        above = jnp.where(lanes < LANE - o, pltpu.roll(v, LANE - o, axis), 0.0)
        below = jnp.where(lanes >= o, pltpu.roll(v, o, axis), 0.0)
        total = total + float(FR - o) * (above + below)
    return total


def forms(load, eigen, store, pairs, tiles):
    lame = POISSON / ((1.0 + POISSON) * (1.0 - 2.0 * POISSON))
    shear = 0.5 / (1.0 + POISSON)
    rows = tiles * SUB
    lanes = iota((rows, LANE), 1)
    for c in range(3):
        for a in (0, 1):
            u = load(c, a)
            up = jnp.where(lanes < LANE - 1, pltpu.roll(u, LANE - 1, 1), 0.0)
            pairs[c, a, 0, :rows] = up + u
            pairs[c, a, 1, :rows] = up - u
            pairs[c, a, :, rows:] = jnp.zeros((2, SUB, LANE), F32)
    eigen_v = jnp.full((SUB, LANE), eigen, F32)
    weight = jnp.exp(-KS_SHARP * eigen_v)
    eigen_weight = weight * eigen_v
    normal = lame + 2.0 * shear
    ms, md = 0.25, 1.0 / 12.0
    m0, m1, m2, m3 = ms**3, ms * ms * md, ms * md * md, md**3

    def tile(r, _):
        base = pl.multiple_of(r * SUB, SUB)
        coef = {}
        for c in range(3):
            planes = []
            for a in (0, 1):
                here = {}
                for z in (0, 1):
                    p0 = pairs[c, a, z, pl.ds(base, SUB)]
                    p1 = pairs[c, a, z, pl.ds(base + 1, SUB)]
                    here[0, z] = p1 + p0
                    here[1, z] = p1 - p0
                planes.append(here)
            for y in (0, 1):
                for z in (0, 1):
                    coef[c, 0, y, z] = planes[1][y, z] + planes[0][y, z]
                    coef[c, 1, y, z] = planes[1][y, z] - planes[0][y, z]
        groups = [None] * 6
        for c in range(3):
            for x in (0, 1):
                for y in (0, 1):
                    for z in (0, 1):
                        d = (x, y, z)
                        n = x + y + z
                        g = {0: 0, 1: 1 if d[c] else 2, 2: 3 if d[c] else 4, 3: 5}[n]
                        v = coef[c, x, y, z]
                        groups[g] = v * v if groups[g] is None else groups[g] + v * v
        mass = m0 * groups[0] + m1 * (groups[1] + groups[2]) + m2 * (groups[3] + groups[4]) + m3 * groups[5]
        stiff = (
            (12.0 * m1 * normal) * groups[1]
            + (12.0 * m1 * shear) * groups[2]
            + (12.0 * m2 * (normal + shear)) * groups[3]
            + (12.0 * m2 * 2.0 * shear) * groups[4]
            + (12.0 * m3 * (normal + 2.0 * shear)) * groups[5]
        )
        for third in (0, 1):
            along_sum = across_sum = None
            for i, j, k in ((0, 1, 2), (0, 2, 1), (1, 2, 0)):

                def at(c, di, dj):
                    d = [0, 0, 0]
                    d[i], d[j], d[k] = di, dj, third
                    return coef[c, d[0], d[1], d[2]]

                t = at(i, 1, 0) * at(j, 0, 1)
                s = at(i, 0, 1) * at(j, 1, 0)
                along_sum = t if along_sum is None else along_sum + t
                across_sum = s if across_sum is None else across_sum + s
            m = (ms, md)[third] * 0.25
            stiff = stiff + (2.0 * lame * m) * along_sum + (2.0 * shear * m) * across_sum
        store(r, weight * stiff, eigen_weight * mass)
        return 0

    lax.fori_loop(0, tiles, tile, 0, unroll=2)
    return weight


def fetch(pieces, sems):
    return [
        pltpu.make_async_copy(source, to.at[pl.ds(start, size)], sems.at[k])
        for k, (source, to, start, size) in enumerate(pieces)
    ]


def pack(modes, design, out, sems):
    planes, rows = modes.shape[1], modes.shape[3]
    pieces = [(modes.at[0, c, 0], out, c * rows, rows) for c in range(planes)]
    pieces += [(design.at[l], out, planes * rows + l * SUB, SUB) for l in (0, 1)]
    copies = fetch(pieces, sems)
    for copy in copies:
        copy.start()
    for copy in copies:
        copy.wait()


def tail_rows(packed, k):
    start = packed.shape[0] - (2 - k) * SUB
    return packed[start : start + SUB]


def plane_rows(packed, c, rows):
    return packed[c * rows : (c + 1) * rows]


def first_layer(modes, packed, eigen, out, upper, pairs, sems):
    planes, rows = modes.shape[1], modes.shape[3]
    copies = fetch([(modes.at[0, c, 1], upper, c * rows, rows) for c in range(planes)], sems)
    for copy in copies:
        copy.start()
    for copy in copies:
        copy.wait()

    def store(r, stiff, mass):
        out[r, 0] = stiff
        out[r, 1] = mass

    tiles = out.shape[0]
    span = tiles * SUB

    def load(c, a):
        return plane_rows(upper if a else packed, c, span)

    forms(load, eigen[0], store, pairs, tiles)


def shifted_rows(v, o):
    rows = iota(v.shape, 0)
    moved = pltpu.roll(v, (-o) % SUB, 0)
    return jnp.where((rows + o >= 0) & (rows + o < SUB), moved, 0.0)


def edge_rows(first, second):
    up, down = [], []
    for f in (first, second):
        up += [2.0 * f[7:8] + f[6:7], f[7:8]]
        down += [f[0:1], 2.0 * f[0:1] + f[1:2]]
    return jnp.concatenate(up, 0), jnp.concatenate(down, 0)


def second_layer(packed, upper, eigen, got, before, _, out, rows, pairs, *, mode):
    def store(r, stiff, mass):
        out[r, 2] = stiff
        out[r, 3] = mass

    tiles = out.shape[0]
    span = tiles * SUB

    def load(c, a):
        return plane_rows(got if a else upper, c, span)

    m = mode_index()
    own = tail_rows(packed, 0), tail_rows(packed, 1)
    after = tail_rows(got, 0), tail_rows(got, 1)
    pair = across_x(own, before, after)
    up, down = edge_rows(*pair)
    for l in (0, 1):
        rows[l] = pair[l]
    weight = forms(load, eigen[0], store, pairs, tiles)
    half = SUB // 2
    for r in range(tiles):
        out[r, 4, :half] = jnp.where(m + 1 == r, up, weight[:half])
        out[r, 4, half:] = jnp.where(m - 1 == r, down, weight[half:])


def across_x(own, before, after):
    first = before[0] + 2.0 * before[1] + 3.0 * own[0] + 2.0 * own[1] + after[0]
    second = before[1] + 2.0 * own[0] + 3.0 * own[1] + 2.0 * after[0] + after[1]
    return first, second


def over_modes(got, at):
    total = got[0, at]
    for r in range(1, got.shape[0]):
        total = total + got[r, at]
    return total


def own_gradient(got, rows, out, *, slab, mode, sizes):
    total_x, total_y, total_z = sizes
    s, m = lax.axis_index(slab), mode_index()
    stiff = (over_modes(got, 0), over_modes(got, 2))
    mass = (over_modes(got, 1), over_modes(got, 3))
    tiles = got.shape[0]
    half = SUB // 2
    weight = None
    for r in range(tiles):
        w = jnp.where(m - 1 == r, got[r, 4, half : half + 1], got[r, 4, :1])
        weight = w if weight is None else weight + w
    inverse_weight = 1.0 / jnp.broadcast_to(weight, (SUB, LANE))
    from_last = jnp.where(m > 0, got[jnp.maximum(m - 1, 0), 4, :half], 0.0)
    from_next = jnp.where(m < tiles - 1, got[jnp.minimum(m + 1, tiles - 1), 4, half:], 0.0)
    inverse_yz = along(m * SUB + iota((SUB, LANE), 0), total_y, edge_tables(total_y)[0]) * along(
        iota((SUB, LANE), 1), total_z, edge_tables(total_z)[0]
    )
    for l in (0, 1):
        own = rows[l]
        near = jnp.concatenate(
            [from_last[2 * l : 2 * l + 2], jnp.zeros((4, LANE), F32), from_next[2 * l : 2 * l + 2]], 0
        )
        filtered = near
        for o in range(1 - FR, FR):
            filtered = filtered + float(FR - abs(o)) * (shifted_rows(own, o) if o else own)
        x = jnp.full((SUB, LANE), 2 * s + l, jnp.int32)
        inverse = inverse_yz * along(x, total_x, edge_tables(total_x)[0])
        density = tent_lanes(filtered) * inverse
        slope = (PENALTY * (1.0 - FLOOR_MODULUS)) * density * density
        out[l] = tent_lanes((slope * stiff[l] - mass[l]) * inverse_weight * inverse)


def gradient_copies(own, even, odd, packed, out, *, slab):
    is_even = lax.rem(lax.axis_index(slab), 2) == 0
    before = [jnp.where(is_even, odd[l], even[l]) for l in (0, 1)]
    after = [jnp.where(is_even, even[l], odd[l]) for l in (0, 1)]
    pair = across_x(own, before, after)
    for r in range(out.shape[0]):
        out[r, 0] = pair[r % 2]
        out[r, 1] = tail_rows(packed, r % 2)


def measure_xz(slab, total_x, total_z):
    s = lax.axis_index(slab)
    z = along(iota((SUB, LANE), 1), total_z, edge_tables(total_z)[1])
    return [
        z * along(jnp.full((SUB, LANE), 2 * s + l, jnp.int32), total_x, edge_tables(total_x)[1])
        for l in (0, 1)
    ]


def volumes(levels, gain, least, most, parts):
    count = gain.shape[0]
    for start in range(0, len(levels), 8):
        chunk = levels[start : start + 8]

        def body(v, totals):
            g, lo, hi = gain[v], least[v], most[v]
            return tuple(
                t + jnp.minimum(jnp.maximum(g * q, lo), hi) for t, q in zip(totals, chunk)
            )

        zeros = tuple(jnp.zeros((SUB, LANE), F32) for _ in chunk)
        totals = lax.fori_loop(0, count, body, zeros, unroll=16)
        for i, t in enumerate(totals):
            parts[start + i : start + i + 1] = jnp.sum(t, axis=0, keepdims=True)


def lane_totals(parts):
    column = jnp.sum(parts[...], axis=1, keepdims=True)
    shape = (FAN, LANE)
    mine = iota(shape, 0) == jnp.minimum(iota(shape, 1), FAN - 1)
    spread = jnp.where(mine, jnp.broadcast_to(column, shape), 0.0)
    return jnp.sum(spread, axis=0, keepdims=True)


def bounds(whole, least, most, goals, measures, *, sizes):
    total_x, total_y, total_z = sizes
    x = 2 * lax.axis_index("slab") + lax.axis_index("core")
    xz = along(jnp.full((SUB, LANE), x, jnp.int32), total_x, edge_tables(total_x)[1])
    xz = xz * along(iota((SUB, LANE), 1), total_z, edge_tables(total_z)[1])
    goal = jnp.zeros((SUB, LANE), F32)
    for r in range(whole.shape[0]):
        y = along(r * SUB + iota((SUB, LANE), 0), total_y, edge_tables(total_y)[1])
        measure = xz * y
        design = whole[r, 1]
        least[r] = jnp.maximum(design - MOVE_LIMIT, 0.0) * measure
        most[r] = jnp.minimum(design + MOVE_LIMIT, 1.0) * measure
        measures[r] = measure
        goal = goal + design * measure
    goals[0:1] = jnp.sum(goal, axis=0, keepdims=True)


def across_y(padded, start):
    total = None
    for o in range(1 - FR, FR):
        t = float(FR - abs(o)) * padded[pl.ds(start + o, SUB)]
        total = t if total is None else total + t
    return total


def first_round(got, least, most, goals, measures, gain, own, other, out, padded, parts):
    tiles = got.shape[0]
    padded[:SUB] = jnp.zeros((SUB, LANE), F32)
    padded[(tiles + 1) * SUB :] = jnp.zeros((SUB, LANE), F32)
    for r in range(tiles):
        padded[(r + 1) * SUB : (r + 2) * SUB] = got[r, 0]
    for r in range(tiles):
        total = across_y(padded, (r + 1) * SUB)
        gain[r] = got[r, 1] * jnp.sqrt(jnp.maximum(total, 0.0) * measures[r])
    m = mode_index()
    own[...] = across_y(padded, (m + 1) * SUB)
    other[...] = across_y(padded, (m + 2 - 2 * lax.axis_index("core")) * SUB)
    levels = [float(np.exp(-0.5 * (LEVEL_LOW + COARSE * (i + 1)))) for i in range(FAN - 1)]
    volumes(levels, gain, least, most, parts)
    parts[FAN - 1 : FAN] = goals[0:1]
    row = lane_totals(parts)
    for k in range(out.shape[0]):
        out[k] = row


def added(got):
    rows = [got[k] for k in range(got.shape[0])]
    while len(rows) > 1:
        rows = [a + b for a, b in zip(rows[::2], rows[1::2])] + rows[len(rows) & ~1 :]
    return rows[0]


def cells_above(row, goal):
    above = (row > goal) & (iota(row.shape, 1) < FAN - 1)
    return jnp.sum(jnp.where(above, 1.0, 0.0), axis=1, keepdims=True)


def second_round(got, gain, least, most, out, state, parts):
    row = added(got)
    goal = pltpu.roll(row, LANE - FAN, 1)
    low = LEVEL_LOW + COARSE * cells_above(row, goal)
    state[0:1] = jnp.broadcast_to(low, (1, LANE))
    state[1:2] = goal
    scale = jnp.exp(-0.5 * jnp.broadcast_to(low, (SUB, LANE)))
    levels = [scale * float(np.exp(-0.5 * FINE * (i + 1))) for i in range(FAN - 1)]
    volumes(levels, gain, least, most, parts)
    parts[FAN - 1 : FAN] = jnp.zeros((1, LANE), F32)
    row = lane_totals(parts)
    for k in range(out.shape[0]):
        out[k] = row


def last_update(got, state, own, other, design, sens_out, out, *, slab, mode, sizes):
    total_x, total_y, total_z = sizes
    m = mode_index()
    row = added(got)
    goal = state[1:2]
    level = state[0:1, 0:1] + FINE * (cells_above(row, goal) + 0.5)
    scale = jnp.exp(jnp.broadcast_to(level, (SUB, LANE)))
    y = along(m * SUB + iota((SUB, LANE), 0), total_y, edge_tables(total_y)[1])
    xz = measure_xz(slab, total_x, total_z)
    for l in (0, 1):
        d = design[l]
        s = jnp.where(lax.axis_index("core") == l, own[...], other[...])
        factor = jnp.sqrt(jnp.maximum(s, 0.0) / (scale * (xz[l] * y)))
        least = jnp.maximum(d - MOVE_LIMIT, 0.0)
        most = jnp.minimum(d + MOVE_LIMIT, 1.0)
        out[l] = jnp.minimum(jnp.maximum(d * factor, least), most)
        sens_out[l] = s


def call(kernel, outs, operands, specs=None, scratch=(), flops=1000, alias=None):
    outs = [jax.ShapeDtypeStruct(o, F32) for o in outs]
    size = sum(4 * int(np.prod(o.shape)) for o in (*outs, *operands))
    single = len(outs) == 1
    return pl.pallas_call(
        kernel,
        out_shape=outs[0] if single else outs,
        in_specs=specs or [VMEM] * len(operands),
        out_specs=VMEM if single else [VMEM] * len(outs),
        scratch_shapes=[pltpu.VMEM(s, F32) for s in scratch],
        cost_estimate=pl.CostEstimate(flops=flops, bytes_accessed=size, transcendentals=0),
        input_output_aliases=alias or {},
        compiler_params=pltpu.CompilerParams(vmem_limit_bytes=GRANT),
    )(*operands)


def from_before(value, axis):
    count = lax.axis_size(axis)
    return lax.ppermute(value, axis, [(i, i + 1) for i in range(count - 1)])


def from_after(value, axis):
    count = lax.axis_size(axis)
    return lax.ppermute(value, axis, [(i + 1, i) for i in range(count - 1)])


def swapped(value, axis, first):
    pairs = []
    for i in range(first, lax.axis_size(axis) - 1, 2):
        pairs += [(i, i + 1), (i + 1, i)]
    return lax.ppermute(value, axis, pairs)


def exchange(value, axis):
    return lax.all_to_all(value, axis, 0, 0, tiled=True)


def local(design, mode_shapes, eigenvalues):
    slab, mode = "slab", ("row", "core")
    slabs, modes = lax.axis_size(slab), lax.axis_size(mode)
    _, _, _, total_y, total_z = mode_shapes.shape
    sizes = (2 * slabs, total_y, total_z)
    pairs = (3, 2, 2, total_y + SUB, LANE)
    block = (2, SUB, LANE)
    padded = (total_y + 2 * SUB, LANE)
    place = dict(slab=slab, mode=mode, sizes=sizes)

    held = pltpu.with_memory_space_constraint(mode_shapes, pltpu.HBM)
    params = pltpu.CompilerParams(vmem_limit_bytes=GRANT)
    hbm = pl.BlockSpec(memory_space=pltpu.HBM)
    packed = pl.pallas_call(
        pack,
        out_shape=jax.ShapeDtypeStruct((3 * total_y + 2 * SUB, LANE), F32),
        in_specs=[hbm, hbm],
        out_specs=VMEM,
        scratch_shapes=[pltpu.SemaphoreType.DMA((5,))],
        compiler_params=params,
        name="pack",
    )(held, pltpu.with_memory_space_constraint(design, pltpu.HBM))
    got = from_after(packed, slab)
    before = from_before(design, slab)
    sent, upper = pl.pallas_call(
        first_layer,
        out_shape=[
            jax.ShapeDtypeStruct((modes, 5, SUB, LANE), F32),
            jax.ShapeDtypeStruct((3 * total_y, LANE), F32),
        ],
        in_specs=[hbm, VMEM, SMEM],
        out_specs=[VMEM, VMEM],
        scratch_shapes=[pltpu.VMEM(pairs, F32), pltpu.SemaphoreType.DMA((3,))],
        cost_estimate=pl.CostEstimate(flops=5_000_000, bytes_accessed=600_000, transcendentals=0),
        compiler_params=params,
        name="first_layer",
    )(held, packed, eigenvalues)
    sent, rows = call(
        functools.partial(second_layer, mode=mode),
        [(modes, 5, SUB, LANE), block],
        [packed, upper, eigenvalues, got, before, sent],
        specs=[VMEM, VMEM, SMEM, VMEM, VMEM, VMEM],
        scratch=[pairs],
        flops=5_000_000,
        alias={5: 0},
    )
    early = exchange(sent, mode)
    gradient = call(functools.partial(own_gradient, **place), [block], [early, rows])
    even = swapped(gradient, slab, 0)
    odd = swapped(gradient, slab, 1)
    copies = call(
        functools.partial(gradient_copies, slab=slab),
        [(modes, 2, SUB, LANE)],
        [gradient, even, odd, packed],
    )
    whole = exchange(copies, mode)
    vectors = (modes, SUB, LANE)
    peers = (2 * slabs, 1, LANE)
    least, most, goals, measures = call(
        functools.partial(bounds, sizes=sizes),
        [vectors, vectors, (SUB, LANE), vectors],
        [whole],
        flops=100_000,
    )
    gain, own, other, sent = call(
        first_round,
        [vectors, (SUB, LANE), (SUB, LANE), peers],
        [whole, least, most, goals, measures],
        scratch=[padded, (FAN, LANE)],
    )
    other = lax.ppermute(other, "core", [(0, 1), (1, 0)])
    got = exchange(sent, (slab, "core"))
    sent, state = call(
        second_round, [peers, (SUB, LANE)], [got, gain, least, most], scratch=[(FAN, LANE)]
    )
    got = exchange(sent, (slab, "core"))
    return call(
        functools.partial(last_update, **place), [block, block], [got, state, own, other, design]
    )


def solution(mesh):
    slabs, modes = mesh.devices.shape
    split = Mesh(mesh.devices.reshape(slabs, modes // 2, 2), ("slab", "row", "core"))
    mode = ("row", "core")
    in_specs = (P("slab", mode, None), P(mode, None, "slab", None, None), P(mode))
    out_specs = (P("slab", mode, None), P("slab", mode, None))

    def step(design, mode_shapes, eigenvalues):
        return tuple(local(design, mode_shapes, eigenvalues))

    return jax.shard_map(step, mesh=split, in_specs=in_specs, out_specs=out_specs, check_vma=False)
```

```python
import functools

import jax
import jax.numpy as jnp
import numpy as np
from jax import lax
from jax.experimental import pallas as pl
from jax.experimental.pallas import tpu as pltpu
from jax.sharding import PartitionSpec as P


FR = 3
KS_SHARP = 2.0
PENALTY = 3.0
FLOOR_MODULUS = 0.001
MOVE_LIMIT = 0.2
POISSON = 0.3
LEVEL_LOW = -14.0
LEVEL_HIGH = 14.0
FAN = 64
COARSE = (LEVEL_HIGH - LEVEL_LOW) / FAN
FINE = COARSE / FAN
SUB, LANE = 8, 128
GRANT = 8 * 1024 * 1024
F32 = jnp.float32
VMEM = pl.BlockSpec(memory_space=pltpu.VMEM)
SMEM = pl.BlockSpec(memory_space=pltpu.SMEM)


def tent_1d(values):
    padded = np.pad(values, FR - 1)
    n = len(values)
    return sum((FR - abs(o)) * padded[FR - 1 + o : FR - 1 + o + n] for o in range(1 - FR, FR))


def edge_tables(n):
    span = tent_1d(np.ones(n))
    return 1.0 / span, tent_1d(1.0 / span)


def along(position, n, table):
    middle = float(table[n // 2])
    value = jnp.where(position >= 0, F32(middle), F32(0.0))
    for k in range(2 * (FR - 1)):
        if abs(table[k] - middle) > 1e-12:
            value = jnp.where((position == k) | (position == n - 1 - k), F32(table[k]), value)
    return value


def iota(shape, axis):
    return lax.broadcasted_iota(jnp.int32, shape, axis)


def tent_lanes(v):
    lanes = iota(v.shape, v.ndim - 1)
    axis = v.ndim - 1
    total = 3.0 * v
    for o in (1, 2):
        above = jnp.where(lanes < LANE - o, pltpu.roll(v, LANE - o, axis), 0.0)
        below = jnp.where(lanes >= o, pltpu.roll(v, o, axis), 0.0)
        total = total + float(FR - o) * (above + below)
    return total


def forms(load, eigen, store, pairs, tiles):
    lame = POISSON / ((1.0 + POISSON) * (1.0 - 2.0 * POISSON))
    shear = 0.5 / (1.0 + POISSON)
    rows = tiles * SUB
    lanes = iota((rows, LANE), 1)
    for c in range(3):
        for a in (0, 1):
            u = load(c, a)
            up = jnp.where(lanes < LANE - 1, pltpu.roll(u, LANE - 1, 1), 0.0)
            pairs[c, a, 0, :rows] = up + u
            pairs[c, a, 1, :rows] = up - u
            pairs[c, a, :, rows:] = jnp.zeros((2, SUB, LANE), F32)
    eigen_v = jnp.full((SUB, LANE), eigen, F32)
    weight = jnp.exp(-KS_SHARP * eigen_v)
    eigen_weight = weight * eigen_v
    normal = lame + 2.0 * shear
    ms, md = 0.25, 1.0 / 12.0
    m0, m1, m2, m3 = ms**3, ms * ms * md, ms * md * md, md**3

    def tile(r, _):
        base = pl.multiple_of(r * SUB, SUB)
        coef = {}
        for c in range(3):
            planes = []
            for a in (0, 1):
                here = {}
                for z in (0, 1):
                    p0 = pairs[c, a, z, pl.ds(base, SUB)]
                    p1 = pairs[c, a, z, pl.ds(base + 1, SUB)]
                    here[0, z] = p1 + p0
                    here[1, z] = p1 - p0
                planes.append(here)
            for y in (0, 1):
                for z in (0, 1):
                    coef[c, 0, y, z] = planes[1][y, z] + planes[0][y, z]
                    coef[c, 1, y, z] = planes[1][y, z] - planes[0][y, z]
        groups = [None] * 6
        for c in range(3):
            for x in (0, 1):
                for y in (0, 1):
                    for z in (0, 1):
                        d = (x, y, z)
                        n = x + y + z
                        g = {0: 0, 1: 1 if d[c] else 2, 2: 3 if d[c] else 4, 3: 5}[n]
                        v = coef[c, x, y, z]
                        groups[g] = v * v if groups[g] is None else groups[g] + v * v
        mass = m0 * groups[0] + m1 * (groups[1] + groups[2]) + m2 * (groups[3] + groups[4]) + m3 * groups[5]
        stiff = (
            (12.0 * m1 * normal) * groups[1]
            + (12.0 * m1 * shear) * groups[2]
            + (12.0 * m2 * (normal + shear)) * groups[3]
            + (12.0 * m2 * 2.0 * shear) * groups[4]
            + (12.0 * m3 * (normal + 2.0 * shear)) * groups[5]
        )
        for third in (0, 1):
            along_sum = across_sum = None
            for i, j, k in ((0, 1, 2), (0, 2, 1), (1, 2, 0)):

                def at(c, di, dj):
                    d = [0, 0, 0]
                    d[i], d[j], d[k] = di, dj, third
                    return coef[c, d[0], d[1], d[2]]

                t = at(i, 1, 0) * at(j, 0, 1)
                s = at(i, 0, 1) * at(j, 1, 0)
                along_sum = t if along_sum is None else along_sum + t
                across_sum = s if across_sum is None else across_sum + s
            m = (ms, md)[third] * 0.25
            stiff = stiff + (2.0 * lame * m) * along_sum + (2.0 * shear * m) * across_sum
        store(r, weight * stiff, eigen_weight * mass)
        return 0

    lax.fori_loop(0, tiles, tile, 0, unroll=2)
    return weight


def fetch(pieces, sems):
    return [
        pltpu.make_async_copy(source, to.at[pl.ds(start, size)], sems.at[k])
        for k, (source, to, start, size) in enumerate(pieces)
    ]


def pack(modes, design, out, sems):
    planes, rows = modes.shape[1], modes.shape[3]
    pieces = [(modes.at[0, c, 0], out, c * rows, rows) for c in range(planes)]
    pieces += [(design.at[l], out, planes * rows + l * SUB, SUB) for l in (0, 1)]
    copies = fetch(pieces, sems)
    for copy in copies:
        copy.start()
    for copy in copies:
        copy.wait()


def tail_rows(packed, k):
    start = packed.shape[0] - (2 - k) * SUB
    return packed[start : start + SUB]


def plane_rows(packed, c, rows):
    return packed[c * rows : (c + 1) * rows]


def first_layer(modes, packed, eigen, out, upper, pairs, sems):
    planes, rows = modes.shape[1], modes.shape[3]
    copies = fetch([(modes.at[0, c, 1], upper, c * rows, rows) for c in range(planes)], sems)
    for copy in copies:
        copy.start()
    for copy in copies:
        copy.wait()

    def store(r, stiff, mass):
        out[r, 0] = stiff
        out[r, 1] = mass

    tiles = out.shape[0]
    span = tiles * SUB

    def load(c, a):
        return plane_rows(upper if a else packed, c, span)

    forms(load, eigen[0], store, pairs, tiles)


def shifted_rows(v, o):
    rows = iota(v.shape, 0)
    moved = pltpu.roll(v, (-o) % SUB, 0)
    return jnp.where((rows + o >= 0) & (rows + o < SUB), moved, 0.0)


def edge_rows(first, second):
    up, down = [], []
    for f in (first, second):
        up += [2.0 * f[7:8] + f[6:7], f[7:8]]
        down += [f[0:1], 2.0 * f[0:1] + f[1:2]]
    return jnp.concatenate(up, 0), jnp.concatenate(down, 0)


def second_layer(packed, upper, eigen, got, before, _, out, rows, pairs, *, mode):
    def store(r, stiff, mass):
        out[r, 2] = stiff
        out[r, 3] = mass

    tiles = out.shape[0]
    span = tiles * SUB

    def load(c, a):
        return plane_rows(got if a else upper, c, span)

    m = lax.axis_index(mode)
    own = tail_rows(packed, 0), tail_rows(packed, 1)
    after = tail_rows(got, 0), tail_rows(got, 1)
    pair = across_x(own, before, after)
    up, down = edge_rows(*pair)
    for l in (0, 1):
        rows[l] = pair[l]
    weight = forms(load, eigen[0], store, pairs, tiles)
    half = SUB // 2
    for r in range(tiles):
        out[r, 4, :half] = jnp.where(m + 1 == r, up, weight[:half])
        out[r, 4, half:] = jnp.where(m - 1 == r, down, weight[half:])


def across_x(own, before, after):
    first = before[0] + 2.0 * before[1] + 3.0 * own[0] + 2.0 * own[1] + after[0]
    second = before[1] + 2.0 * own[0] + 3.0 * own[1] + 2.0 * after[0] + after[1]
    return first, second


def over_modes(got, at):
    total = got[0, at]
    for r in range(1, got.shape[0]):
        total = total + got[r, at]
    return total


def own_gradient(got, rows, out, *, slab, mode, sizes):
    total_x, total_y, total_z = sizes
    s, m = lax.axis_index(slab), lax.axis_index(mode)
    stiff = (over_modes(got, 0), over_modes(got, 2))
    mass = (over_modes(got, 1), over_modes(got, 3))
    tiles = got.shape[0]
    half = SUB // 2
    weight = None
    for r in range(tiles):
        w = jnp.where(m - 1 == r, got[r, 4, half : half + 1], got[r, 4, :1])
        weight = w if weight is None else weight + w
    inverse_weight = 1.0 / jnp.broadcast_to(weight, (SUB, LANE))
    from_last = jnp.where(m > 0, got[jnp.maximum(m - 1, 0), 4, :half], 0.0)
    from_next = jnp.where(m < tiles - 1, got[jnp.minimum(m + 1, tiles - 1), 4, half:], 0.0)
    inverse_yz = along(m * SUB + iota((SUB, LANE), 0), total_y, edge_tables(total_y)[0]) * along(
        iota((SUB, LANE), 1), total_z, edge_tables(total_z)[0]
    )
    for l in (0, 1):
        own = rows[l]
        near = jnp.concatenate(
            [from_last[2 * l : 2 * l + 2], jnp.zeros((4, LANE), F32), from_next[2 * l : 2 * l + 2]], 0
        )
        filtered = near
        for o in range(1 - FR, FR):
            filtered = filtered + float(FR - abs(o)) * (shifted_rows(own, o) if o else own)
        x = jnp.full((SUB, LANE), 2 * s + l, jnp.int32)
        inverse = inverse_yz * along(x, total_x, edge_tables(total_x)[0])
        density = tent_lanes(filtered) * inverse
        slope = (PENALTY * (1.0 - FLOOR_MODULUS)) * density * density
        out[l] = tent_lanes((slope * stiff[l] - mass[l]) * inverse_weight * inverse)


def gradient_copies(own, even, odd, packed, out, *, slab):
    is_even = lax.rem(lax.axis_index(slab), 2) == 0
    before = [jnp.where(is_even, odd[l], even[l]) for l in (0, 1)]
    after = [jnp.where(is_even, even[l], odd[l]) for l in (0, 1)]
    pair = across_x(own, before, after)
    for r in range(out.shape[0]):
        out[r, 0] = pair[0]
        out[r, 1] = pair[1]
        out[r, 2] = tail_rows(packed, 0)
        out[r, 3] = tail_rows(packed, 1)


def measure_xz(slab, total_x, total_z):
    s = lax.axis_index(slab)
    z = along(iota((SUB, LANE), 1), total_z, edge_tables(total_z)[1])
    return [
        z * along(jnp.full((SUB, LANE), 2 * s + l, jnp.int32), total_x, edge_tables(total_x)[1])
        for l in (0, 1)
    ]


def volumes(levels, gain, least, most, parts):
    count = gain.shape[0]
    for start in range(0, len(levels), 8):
        chunk = levels[start : start + 8]

        def body(v, totals):
            g, lo, hi = gain[v], least[v], most[v]
            return tuple(
                t + jnp.minimum(jnp.maximum(g * q, lo), hi) for t, q in zip(totals, chunk)
            )

        zeros = tuple(jnp.zeros((SUB, LANE), F32) for _ in chunk)
        totals = lax.fori_loop(0, count, body, zeros, unroll=32)
        for i, t in enumerate(totals):
            parts[start + i : start + i + 1] = jnp.sum(t, axis=0, keepdims=True)


def lane_totals(parts):
    column = jnp.sum(parts[...], axis=1, keepdims=True)
    shape = (FAN, LANE)
    mine = iota(shape, 0) == jnp.minimum(iota(shape, 1), FAN - 1)
    spread = jnp.where(mine, jnp.broadcast_to(column, shape), 0.0)
    return jnp.sum(spread, axis=0, keepdims=True)


def first_round(got, gain, least, most, own, out, padded, parts, *, slab, mode, sizes):
    total_x, total_y, total_z = sizes
    tiles = got.shape[0]
    m = lax.axis_index(mode)
    xz = measure_xz(slab, total_x, total_z)
    goal = jnp.zeros((SUB, LANE), F32)
    for l in (0, 1):
        padded[l, :SUB] = jnp.zeros((SUB, LANE), F32)
        padded[l, (tiles + 1) * SUB :] = jnp.zeros((SUB, LANE), F32)
        for r in range(tiles):
            padded[l, (r + 1) * SUB : (r + 2) * SUB] = got[r, l]
    for l in (0, 1):
        for r in range(tiles):
            total = None
            for o in range(1 - FR, FR):
                start = (r + 1) * SUB + o
                t = float(FR - abs(o)) * padded[l, start : start + SUB]
                total = t if total is None else total + t
            y = along(r * SUB + iota((SUB, LANE), 0), total_y, edge_tables(total_y)[1])
            measure = xz[l] * y
            design = got[r, 2 + l]
            at = l * tiles + r
            gain[at] = design * jnp.sqrt(jnp.maximum(total, 0.0) * measure)
            least[at] = jnp.maximum(design - MOVE_LIMIT, 0.0) * measure
            most[at] = jnp.minimum(design + MOVE_LIMIT, 1.0) * measure
            goal = goal + design * measure
        total = None
        for o in range(1 - FR, FR):
            t = float(FR - abs(o)) * padded[l, pl.ds(m * SUB + SUB + o, SUB)]
            total = t if total is None else total + t
        own[l] = total
    levels = [float(np.exp(-0.5 * (LEVEL_LOW + COARSE * (i + 1)))) for i in range(FAN - 1)]
    volumes(levels, gain, least, most, parts)
    parts[FAN - 1 : FAN] = jnp.sum(goal, axis=0, keepdims=True)
    row = lane_totals(parts)
    for k in range(out.shape[0]):
        out[k] = row


def added(got):
    rows = [got[k] for k in range(got.shape[0])]
    while len(rows) > 1:
        rows = [a + b for a, b in zip(rows[::2], rows[1::2])] + rows[len(rows) & ~1 :]
    return rows[0]


def cells_above(row, goal):
    above = (row > goal) & (iota(row.shape, 1) < FAN - 1)
    return jnp.sum(jnp.where(above, 1.0, 0.0), axis=1, keepdims=True)


def second_round(got, gain, least, most, out, state, parts):
    row = added(got)
    goal = pltpu.roll(row, LANE - FAN, 1)
    low = LEVEL_LOW + COARSE * cells_above(row, goal)
    state[0:1] = jnp.broadcast_to(low, (1, LANE))
    state[1:2] = goal
    scale = jnp.exp(-0.5 * jnp.broadcast_to(low, (SUB, LANE)))
    levels = [scale * float(np.exp(-0.5 * FINE * (i + 1))) for i in range(FAN - 1)]
    volumes(levels, gain, least, most, parts)
    parts[FAN - 1 : FAN] = jnp.zeros((1, LANE), F32)
    row = lane_totals(parts)
    for k in range(out.shape[0]):
        out[k] = row


def last_update(got, state, own, design, sens_out, out, *, slab, mode, sizes):
    total_x, total_y, total_z = sizes
    m = lax.axis_index(mode)
    row = added(got)
    goal = state[1:2]
    level = state[0:1, 0:1] + FINE * (cells_above(row, goal) + 0.5)
    scale = jnp.exp(jnp.broadcast_to(level, (SUB, LANE)))
    y = along(m * SUB + iota((SUB, LANE), 0), total_y, edge_tables(total_y)[1])
    xz = measure_xz(slab, total_x, total_z)
    for l in (0, 1):
        d, s = design[l], own[l]
        factor = jnp.sqrt(jnp.maximum(s, 0.0) / (scale * (xz[l] * y)))
        least = jnp.maximum(d - MOVE_LIMIT, 0.0)
        most = jnp.minimum(d + MOVE_LIMIT, 1.0)
        out[l] = jnp.minimum(jnp.maximum(d * factor, least), most)
        sens_out[l] = s


def call(kernel, outs, operands, specs=None, scratch=(), flops=1000, alias=None):
    outs = [jax.ShapeDtypeStruct(o, F32) for o in outs]
    size = sum(4 * int(np.prod(o.shape)) for o in (*outs, *operands))
    single = len(outs) == 1
    return pl.pallas_call(
        kernel,
        out_shape=outs[0] if single else outs,
        in_specs=specs or [VMEM] * len(operands),
        out_specs=VMEM if single else [VMEM] * len(outs),
        scratch_shapes=[pltpu.VMEM(s, F32) for s in scratch],
        cost_estimate=pl.CostEstimate(flops=flops, bytes_accessed=size, transcendentals=0),
        input_output_aliases=alias or {},
        compiler_params=pltpu.CompilerParams(vmem_limit_bytes=GRANT),
    )(*operands)


def from_before(value, axis):
    count = lax.axis_size(axis)
    return lax.ppermute(value, axis, [(i, i + 1) for i in range(count - 1)])


def from_after(value, axis):
    count = lax.axis_size(axis)
    return lax.ppermute(value, axis, [(i + 1, i) for i in range(count - 1)])


def swapped(value, axis, first):
    pairs = []
    for i in range(first, lax.axis_size(axis) - 1, 2):
        pairs += [(i, i + 1), (i + 1, i)]
    return lax.ppermute(value, axis, pairs)


def exchange(value, axis):
    return lax.all_to_all(value, axis, 0, 0, tiled=True)


def local(design, mode_shapes, eigenvalues):
    slab, mode = "slab", "mode"
    slabs, modes = lax.axis_size(slab), lax.axis_size(mode)
    _, _, _, total_y, total_z = mode_shapes.shape
    sizes = (2 * slabs, total_y, total_z)
    pairs = (3, 2, 2, total_y + SUB, LANE)
    block = (2, SUB, LANE)
    padded = (2, total_y + 2 * SUB, LANE)
    place = dict(slab=slab, mode=mode, sizes=sizes)

    held = pltpu.with_memory_space_constraint(mode_shapes, pltpu.HBM)
    params = pltpu.CompilerParams(vmem_limit_bytes=GRANT)
    hbm = pl.BlockSpec(memory_space=pltpu.HBM)
    packed = pl.pallas_call(
        pack,
        out_shape=jax.ShapeDtypeStruct((3 * total_y + 2 * SUB, LANE), F32),
        in_specs=[hbm, hbm],
        out_specs=VMEM,
        scratch_shapes=[pltpu.SemaphoreType.DMA((5,))],
        compiler_params=params,
        name="pack",
    )(held, pltpu.with_memory_space_constraint(design, pltpu.HBM))
    got = from_after(packed, slab)
    before = from_before(design, slab)
    sent, upper = pl.pallas_call(
        first_layer,
        out_shape=[
            jax.ShapeDtypeStruct((modes, 5, SUB, LANE), F32),
            jax.ShapeDtypeStruct((3 * total_y, LANE), F32),
        ],
        in_specs=[hbm, VMEM, SMEM],
        out_specs=[VMEM, VMEM],
        scratch_shapes=[pltpu.VMEM(pairs, F32), pltpu.SemaphoreType.DMA((3,))],
        cost_estimate=pl.CostEstimate(flops=5_000_000, bytes_accessed=600_000, transcendentals=0),
        compiler_params=params,
        name="first_layer",
    )(held, packed, eigenvalues)
    sent, rows = call(
        functools.partial(second_layer, mode=mode),
        [(modes, 5, SUB, LANE), block],
        [packed, upper, eigenvalues, got, before, sent],
        specs=[VMEM, VMEM, SMEM, VMEM, VMEM, VMEM],
        scratch=[pairs],
        flops=5_000_000,
        alias={5: 0},
    )
    early = exchange(sent, mode)
    gradient = call(functools.partial(own_gradient, **place), [block], [early, rows])
    even = swapped(gradient, slab, 0)
    odd = swapped(gradient, slab, 1)
    copies = call(
        functools.partial(gradient_copies, slab=slab),
        [(modes, 4, SUB, LANE)],
        [gradient, even, odd, packed],
    )
    whole = exchange(copies, mode)
    vectors = (2 * modes, SUB, LANE)
    gain, least, most, own, sent = call(
        functools.partial(first_round, **place),
        [vectors, vectors, vectors, block, (slabs, 1, LANE)],
        [whole],
        scratch=[padded, (FAN, LANE)],
    )
    got = exchange(sent, slab)
    sent, state = call(
        second_round,
        [(slabs, 1, LANE), (SUB, LANE)],
        [got, gain, least, most],
        scratch=[(FAN, LANE)],
    )
    got = exchange(sent, slab)
    return call(functools.partial(last_update, **place), [block, block], [got, state, own, design])


def solution(mesh):
    in_specs = (P("slab", "mode", None), P("mode", None, "slab", None, None), P("mode"))
    out_specs = (P("slab", "mode", None), P("slab", "mode", None))

    def step(design, mode_shapes, eigenvalues):
        return tuple(local(design, mode_shapes, eigenvalues))

    return jax.shard_map(step, mesh=mesh, in_specs=in_specs, out_specs=out_specs, check_vma=False)
```

```python
import functools

import jax
import jax.numpy as jnp
import numpy as np
from jax import lax
from jax.experimental import pallas as pl
from jax.experimental.pallas import tpu as pltpu
from jax.sharding import PartitionSpec as P


FR = 3
KS_SHARP = 2.0
PENALTY = 3.0
FLOOR_MODULUS = 0.001
MOVE_LIMIT = 0.2
POISSON = 0.3
LEVEL_LOW = -14.0
LEVEL_HIGH = 14.0
FAN = 64
COARSE = (LEVEL_HIGH - LEVEL_LOW) / FAN
FINE = COARSE / FAN
SUB, LANE = 8, 128
GRANT = 8 * 1024 * 1024
F32 = jnp.float32
VMEM = pl.BlockSpec(memory_space=pltpu.VMEM)
SMEM = pl.BlockSpec(memory_space=pltpu.SMEM)


def tent_1d(values):
    padded = np.pad(values, FR - 1)
    n = len(values)
    return sum((FR - abs(o)) * padded[FR - 1 + o : FR - 1 + o + n] for o in range(1 - FR, FR))


def edge_tables(n):
    span = tent_1d(np.ones(n))
    return 1.0 / span, tent_1d(1.0 / span)


def along(position, n, table):
    middle = float(table[n // 2])
    value = jnp.where(position >= 0, F32(middle), F32(0.0))
    for k in range(2 * (FR - 1)):
        if abs(table[k] - middle) > 1e-12:
            value = jnp.where((position == k) | (position == n - 1 - k), F32(table[k]), value)
    return value


def iota(shape, axis):
    return lax.broadcasted_iota(jnp.int32, shape, axis)


def tent_lanes(v):
    lanes = iota(v.shape, v.ndim - 1)
    axis = v.ndim - 1
    total = 3.0 * v
    for o in (1, 2):
        above = jnp.where(lanes < LANE - o, pltpu.roll(v, LANE - o, axis), 0.0)
        below = jnp.where(lanes >= o, pltpu.roll(v, o, axis), 0.0)
        total = total + float(FR - o) * (above + below)
    return total


def forms(load, eigen, store, pairs, tiles):
    lame = POISSON / ((1.0 + POISSON) * (1.0 - 2.0 * POISSON))
    shear = 0.5 / (1.0 + POISSON)
    rows = tiles * SUB
    lanes = iota((rows, LANE), 1)
    for c in range(3):
        for a in (0, 1):
            u = load(c, a)
            up = jnp.where(lanes < LANE - 1, pltpu.roll(u, LANE - 1, 1), 0.0)
            pairs[c, a, 0, :rows] = up + u
            pairs[c, a, 1, :rows] = up - u
            pairs[c, a, :, rows:] = jnp.zeros((2, SUB, LANE), F32)
    eigen_v = jnp.full((SUB, LANE), eigen, F32)
    weight = jnp.exp(-KS_SHARP * eigen_v)
    eigen_weight = weight * eigen_v
    normal = lame + 2.0 * shear
    ms, md = 0.25, 1.0 / 12.0
    m0, m1, m2, m3 = ms**3, ms * ms * md, ms * md * md, md**3

    def tile(r, _):
        base = pl.multiple_of(r * SUB, SUB)
        coef = {}
        for c in range(3):
            planes = []
            for a in (0, 1):
                here = {}
                for z in (0, 1):
                    p0 = pairs[c, a, z, pl.ds(base, SUB)]
                    p1 = pairs[c, a, z, pl.ds(base + 1, SUB)]
                    here[0, z] = p1 + p0
                    here[1, z] = p1 - p0
                planes.append(here)
            for y in (0, 1):
                for z in (0, 1):
                    coef[c, 0, y, z] = planes[1][y, z] + planes[0][y, z]
                    coef[c, 1, y, z] = planes[1][y, z] - planes[0][y, z]
        groups = [None] * 6
        for c in range(3):
            for x in (0, 1):
                for y in (0, 1):
                    for z in (0, 1):
                        d = (x, y, z)
                        n = x + y + z
                        g = {0: 0, 1: 1 if d[c] else 2, 2: 3 if d[c] else 4, 3: 5}[n]
                        v = coef[c, x, y, z]
                        groups[g] = v * v if groups[g] is None else groups[g] + v * v
        mass = m0 * groups[0] + m1 * (groups[1] + groups[2]) + m2 * (groups[3] + groups[4]) + m3 * groups[5]
        stiff = (
            (12.0 * m1 * normal) * groups[1]
            + (12.0 * m1 * shear) * groups[2]
            + (12.0 * m2 * (normal + shear)) * groups[3]
            + (12.0 * m2 * 2.0 * shear) * groups[4]
            + (12.0 * m3 * (normal + 2.0 * shear)) * groups[5]
        )
        for third in (0, 1):
            along_sum = across_sum = None
            for i, j, k in ((0, 1, 2), (0, 2, 1), (1, 2, 0)):

                def at(c, di, dj):
                    d = [0, 0, 0]
                    d[i], d[j], d[k] = di, dj, third
                    return coef[c, d[0], d[1], d[2]]

                t = at(i, 1, 0) * at(j, 0, 1)
                s = at(i, 0, 1) * at(j, 1, 0)
                along_sum = t if along_sum is None else along_sum + t
                across_sum = s if across_sum is None else across_sum + s
            m = (ms, md)[third] * 0.25
            stiff = stiff + (2.0 * lame * m) * along_sum + (2.0 * shear * m) * across_sum
        store(r, weight * stiff, eigen_weight * mass)
        return 0

    lax.fori_loop(0, tiles, tile, 0, unroll=2)
    return weight


def pack(modes, design, out, sems):
    planes, rows = modes.shape[1], modes.shape[3]
    first = out.at[pl.ds(0, planes * rows)].reshape(planes, rows, LANE)
    last = out.at[pl.ds(planes * rows, 2 * SUB)].reshape(2, SUB, LANE)
    copies = [
        pltpu.make_async_copy(modes.at[0, :, 0], first, sems.at[0]),
        pltpu.make_async_copy(design, last, sems.at[1]),
    ]
    for copy in copies:
        copy.start()
    for copy in copies:
        copy.wait()


def tail_rows(packed, k):
    start = packed.shape[0] - (2 - k) * SUB
    return packed[start : start + SUB]


def plane_rows(packed, c, rows):
    return packed[c * rows : (c + 1) * rows]


def first_layer(modes, packed, eigen, out, upper, pairs, sems):
    planes, rows = modes.shape[1], modes.shape[3]
    first = upper.at[pl.ds(0, planes * rows)].reshape(planes, rows, LANE)
    copies = [pltpu.make_async_copy(modes.at[0, :, 1], first, sems.at[0])]
    for copy in copies:
        copy.start()
    for copy in copies:
        copy.wait()

    def store(r, stiff, mass):
        out[r, 0] = stiff
        out[r, 1] = mass

    tiles = out.shape[0]
    span = tiles * SUB

    def load(c, a):
        return plane_rows(upper if a else packed, c, span)

    forms(load, eigen[0], store, pairs, tiles)


def shifted_rows(v, o):
    rows = iota(v.shape, 0)
    moved = pltpu.roll(v, (-o) % SUB, 0)
    return jnp.where((rows + o >= 0) & (rows + o < SUB), moved, 0.0)


def edge_rows(first, second):
    up, down = [], []
    for f in (first, second):
        up += [2.0 * f[7:8] + f[6:7], f[7:8]]
        down += [f[0:1], 2.0 * f[0:1] + f[1:2]]
    return jnp.concatenate(up, 0), jnp.concatenate(down, 0)


def second_layer(packed, upper, eigen, got, before, _, out, rows, pairs, *, mode):
    def store(r, stiff, mass):
        out[r, 2] = stiff
        out[r, 3] = mass

    tiles = out.shape[0]
    span = tiles * SUB

    def load(c, a):
        return plane_rows(got if a else upper, c, span)

    m = lax.axis_index(mode)
    own = tail_rows(packed, 0), tail_rows(packed, 1)
    after = tail_rows(got, 0), tail_rows(got, 1)
    pair = across_x(own, before, after)
    up, down = edge_rows(*pair)
    for l in (0, 1):
        rows[l] = pair[l]
    weight = forms(load, eigen[0], store, pairs, tiles)
    half = SUB // 2
    for r in range(tiles):
        out[r, 4, :half] = jnp.where(m + 1 == r, up, weight[:half])
        out[r, 4, half:] = jnp.where(m - 1 == r, down, weight[half:])


def across_x(own, before, after):
    first = before[0] + 2.0 * before[1] + 3.0 * own[0] + 2.0 * own[1] + after[0]
    second = before[1] + 2.0 * own[0] + 3.0 * own[1] + 2.0 * after[0] + after[1]
    return first, second


def over_modes(got, at):
    total = got[0, at]
    for r in range(1, got.shape[0]):
        total = total + got[r, at]
    return total


def own_gradient(got, rows, out, *, slab, mode, sizes):
    total_x, total_y, total_z = sizes
    s, m = lax.axis_index(slab), lax.axis_index(mode)
    stiff = (over_modes(got, 0), over_modes(got, 2))
    mass = (over_modes(got, 1), over_modes(got, 3))
    tiles = got.shape[0]
    half = SUB // 2
    weight = None
    for r in range(tiles):
        w = jnp.where(m - 1 == r, got[r, 4, half : half + 1], got[r, 4, :1])
        weight = w if weight is None else weight + w
    inverse_weight = 1.0 / jnp.broadcast_to(weight, (SUB, LANE))
    from_last = jnp.where(m > 0, got[jnp.maximum(m - 1, 0), 4, :half], 0.0)
    from_next = jnp.where(m < tiles - 1, got[jnp.minimum(m + 1, tiles - 1), 4, half:], 0.0)
    inverse_yz = along(m * SUB + iota((SUB, LANE), 0), total_y, edge_tables(total_y)[0]) * along(
        iota((SUB, LANE), 1), total_z, edge_tables(total_z)[0]
    )
    for l in (0, 1):
        own = rows[l]
        near = jnp.concatenate(
            [from_last[2 * l : 2 * l + 2], jnp.zeros((4, LANE), F32), from_next[2 * l : 2 * l + 2]], 0
        )
        filtered = near
        for o in range(1 - FR, FR):
            filtered = filtered + float(FR - abs(o)) * (shifted_rows(own, o) if o else own)
        x = jnp.full((SUB, LANE), 2 * s + l, jnp.int32)
        inverse = inverse_yz * along(x, total_x, edge_tables(total_x)[0])
        density = tent_lanes(filtered) * inverse
        slope = (PENALTY * (1.0 - FLOOR_MODULUS)) * density * density
        out[l] = tent_lanes((slope * stiff[l] - mass[l]) * inverse_weight * inverse)


def gradient_copies(own, even, odd, packed, out, *, slab):
    is_even = lax.rem(lax.axis_index(slab), 2) == 0
    before = [jnp.where(is_even, odd[l], even[l]) for l in (0, 1)]
    after = [jnp.where(is_even, even[l], odd[l]) for l in (0, 1)]
    pair = across_x(own, before, after)
    for r in range(out.shape[0]):
        out[r, 0] = pair[0]
        out[r, 1] = pair[1]
        out[r, 2] = tail_rows(packed, 0)
        out[r, 3] = tail_rows(packed, 1)


def measure_xz(slab, total_x, total_z):
    s = lax.axis_index(slab)
    z = along(iota((SUB, LANE), 1), total_z, edge_tables(total_z)[1])
    return [
        z * along(jnp.full((SUB, LANE), 2 * s + l, jnp.int32), total_x, edge_tables(total_x)[1])
        for l in (0, 1)
    ]


def volumes(levels, gain, least, most, parts):
    count = gain.shape[0]
    for start in range(0, len(levels), 8):
        chunk = levels[start : start + 8]

        def body(v, totals):
            g, lo, hi = gain[v], least[v], most[v]
            return tuple(
                t + jnp.minimum(jnp.maximum(g * q, lo), hi) for t, q in zip(totals, chunk)
            )

        zeros = tuple(jnp.zeros((SUB, LANE), F32) for _ in chunk)
        totals = lax.fori_loop(0, count, body, zeros, unroll=32)
        for i, t in enumerate(totals):
            parts[start + i : start + i + 1] = jnp.sum(t, axis=0, keepdims=True)


def lane_totals(parts):
    column = jnp.sum(parts[...], axis=1, keepdims=True)
    shape = (FAN, LANE)
    mine = iota(shape, 0) == jnp.minimum(iota(shape, 1), FAN - 1)
    spread = jnp.where(mine, jnp.broadcast_to(column, shape), 0.0)
    return jnp.sum(spread, axis=0, keepdims=True)


def first_round(got, gain, least, most, own, out, padded, parts, *, slab, mode, sizes):
    total_x, total_y, total_z = sizes
    tiles = got.shape[0]
    m = lax.axis_index(mode)
    xz = measure_xz(slab, total_x, total_z)
    goal = jnp.zeros((SUB, LANE), F32)
    for l in (0, 1):
        padded[l, :SUB] = jnp.zeros((SUB, LANE), F32)
        padded[l, (tiles + 1) * SUB :] = jnp.zeros((SUB, LANE), F32)
        for r in range(tiles):
            padded[l, (r + 1) * SUB : (r + 2) * SUB] = got[r, l]
    for l in (0, 1):
        for r in range(tiles):
            total = None
            for o in range(1 - FR, FR):
                start = (r + 1) * SUB + o
                t = float(FR - abs(o)) * padded[l, start : start + SUB]
                total = t if total is None else total + t
            y = along(r * SUB + iota((SUB, LANE), 0), total_y, edge_tables(total_y)[1])
            measure = xz[l] * y
            design = got[r, 2 + l]
            at = l * tiles + r
            gain[at] = design * jnp.sqrt(jnp.maximum(total, 0.0) * measure)
            least[at] = jnp.maximum(design - MOVE_LIMIT, 0.0) * measure
            most[at] = jnp.minimum(design + MOVE_LIMIT, 1.0) * measure
            goal = goal + design * measure
        total = None
        for o in range(1 - FR, FR):
            t = float(FR - abs(o)) * padded[l, pl.ds(m * SUB + SUB + o, SUB)]
            total = t if total is None else total + t
        own[l] = total
    levels = [float(np.exp(-0.5 * (LEVEL_LOW + COARSE * (i + 1)))) for i in range(FAN - 1)]
    volumes(levels, gain, least, most, parts)
    parts[FAN - 1 : FAN] = jnp.sum(goal, axis=0, keepdims=True)
    row = lane_totals(parts)
    for k in range(out.shape[0]):
        out[k] = row


def added(got):
    rows = [got[k] for k in range(got.shape[0])]
    while len(rows) > 1:
        rows = [a + b for a, b in zip(rows[::2], rows[1::2])] + rows[len(rows) & ~1 :]
    return rows[0]


def cells_above(row, goal):
    above = (row > goal) & (iota(row.shape, 1) < FAN - 1)
    return jnp.sum(jnp.where(above, 1.0, 0.0), axis=1, keepdims=True)


def second_round(got, gain, least, most, out, state, parts):
    row = added(got)
    goal = pltpu.roll(row, LANE - FAN, 1)
    low = LEVEL_LOW + COARSE * cells_above(row, goal)
    state[0:1] = jnp.broadcast_to(low, (1, LANE))
    state[1:2] = goal
    scale = jnp.exp(-0.5 * jnp.broadcast_to(low, (SUB, LANE)))
    levels = [scale * float(np.exp(-0.5 * FINE * (i + 1))) for i in range(FAN - 1)]
    volumes(levels, gain, least, most, parts)
    parts[FAN - 1 : FAN] = jnp.zeros((1, LANE), F32)
    row = lane_totals(parts)
    for k in range(out.shape[0]):
        out[k] = row


def last_update(got, state, own, design, sens_out, out, *, slab, mode, sizes):
    total_x, total_y, total_z = sizes
    m = lax.axis_index(mode)
    row = added(got)
    goal = state[1:2]
    level = state[0:1, 0:1] + FINE * (cells_above(row, goal) + 0.5)
    scale = jnp.exp(jnp.broadcast_to(level, (SUB, LANE)))
    y = along(m * SUB + iota((SUB, LANE), 0), total_y, edge_tables(total_y)[1])
    xz = measure_xz(slab, total_x, total_z)
    for l in (0, 1):
        d, s = design[l], own[l]
        factor = jnp.sqrt(jnp.maximum(s, 0.0) / (scale * (xz[l] * y)))
        least = jnp.maximum(d - MOVE_LIMIT, 0.0)
        most = jnp.minimum(d + MOVE_LIMIT, 1.0)
        out[l] = jnp.minimum(jnp.maximum(d * factor, least), most)
        sens_out[l] = s


def call(kernel, outs, operands, specs=None, scratch=(), flops=1000, alias=None):
    outs = [jax.ShapeDtypeStruct(o, F32) for o in outs]
    size = sum(4 * int(np.prod(o.shape)) for o in (*outs, *operands))
    single = len(outs) == 1
    return pl.pallas_call(
        kernel,
        out_shape=outs[0] if single else outs,
        in_specs=specs or [VMEM] * len(operands),
        out_specs=VMEM if single else [VMEM] * len(outs),
        scratch_shapes=[pltpu.VMEM(s, F32) for s in scratch],
        cost_estimate=pl.CostEstimate(flops=flops, bytes_accessed=size, transcendentals=0),
        input_output_aliases=alias or {},
        compiler_params=pltpu.CompilerParams(vmem_limit_bytes=GRANT),
    )(*operands)


def from_before(value, axis):
    count = lax.axis_size(axis)
    return lax.ppermute(value, axis, [(i, i + 1) for i in range(count - 1)])


def from_after(value, axis):
    count = lax.axis_size(axis)
    return lax.ppermute(value, axis, [(i + 1, i) for i in range(count - 1)])


def swapped(value, axis, first):
    pairs = []
    for i in range(first, lax.axis_size(axis) - 1, 2):
        pairs += [(i, i + 1), (i + 1, i)]
    return lax.ppermute(value, axis, pairs)


def exchange(value, axis):
    return lax.all_to_all(value, axis, 0, 0, tiled=True)


def local(design, mode_shapes, eigenvalues):
    slab, mode = "slab", "mode"
    slabs, modes = lax.axis_size(slab), lax.axis_size(mode)
    _, _, _, total_y, total_z = mode_shapes.shape
    sizes = (2 * slabs, total_y, total_z)
    pairs = (3, 2, 2, total_y + SUB, LANE)
    block = (2, SUB, LANE)
    padded = (2, total_y + 2 * SUB, LANE)
    place = dict(slab=slab, mode=mode, sizes=sizes)

    held = pltpu.with_memory_space_constraint(mode_shapes, pltpu.HBM)
    params = pltpu.CompilerParams(vmem_limit_bytes=GRANT)
    hbm = pl.BlockSpec(memory_space=pltpu.HBM)
    packed = pl.pallas_call(
        pack,
        out_shape=jax.ShapeDtypeStruct((3 * total_y + 2 * SUB, LANE), F32),
        in_specs=[hbm, hbm],
        out_specs=VMEM,
        scratch_shapes=[pltpu.SemaphoreType.DMA((2,))],
        compiler_params=params,
        name="pack",
    )(held, pltpu.with_memory_space_constraint(design, pltpu.HBM))
    got = from_after(packed, slab)
    before = from_before(design, slab)
    sent, upper = pl.pallas_call(
        first_layer,
        out_shape=[
            jax.ShapeDtypeStruct((modes, 5, SUB, LANE), F32),
            jax.ShapeDtypeStruct((3 * total_y, LANE), F32),
        ],
        in_specs=[hbm, VMEM, SMEM],
        out_specs=[VMEM, VMEM],
        scratch_shapes=[pltpu.VMEM(pairs, F32), pltpu.SemaphoreType.DMA((1,))],
        cost_estimate=pl.CostEstimate(flops=5_000_000, bytes_accessed=600_000, transcendentals=0),
        compiler_params=params,
        name="first_layer",
    )(held, packed, eigenvalues)
    sent, rows = call(
        functools.partial(second_layer, mode=mode),
        [(modes, 5, SUB, LANE), block],
        [packed, upper, eigenvalues, got, before, sent],
        specs=[VMEM, VMEM, SMEM, VMEM, VMEM, VMEM],
        scratch=[pairs],
        flops=5_000_000,
        alias={5: 0},
    )
    early = exchange(sent, mode)
    gradient = call(functools.partial(own_gradient, **place), [block], [early, rows])
    even = swapped(gradient, slab, 0)
    odd = swapped(gradient, slab, 1)
    copies = call(
        functools.partial(gradient_copies, slab=slab),
        [(modes, 4, SUB, LANE)],
        [gradient, even, odd, packed],
    )
    whole = exchange(copies, mode)
    vectors = (2 * modes, SUB, LANE)
    gain, least, most, own, sent = call(
        functools.partial(first_round, **place),
        [vectors, vectors, vectors, block, (slabs, 1, LANE)],
        [whole],
        scratch=[padded, (FAN, LANE)],
    )
    got = exchange(sent, slab)
    sent, state = call(
        second_round,
        [(slabs, 1, LANE), (SUB, LANE)],
        [got, gain, least, most],
        scratch=[(FAN, LANE)],
    )
    got = exchange(sent, slab)
    return call(functools.partial(last_update, **place), [block, block], [got, state, own, design])


def solution(mesh):
    in_specs = (P("slab", "mode", None), P("mode", None, "slab", None, None), P("mode"))
    out_specs = (P("slab", "mode", None), P("slab", "mode", None))

    def step(design, mode_shapes, eigenvalues):
        return tuple(local(design, mode_shapes, eigenvalues))

    return jax.shard_map(step, mesh=mesh, in_specs=in_specs, out_specs=out_specs, check_vma=False)
```

```python
import functools

import jax
import jax.numpy as jnp
import numpy as np
from jax import lax
from jax.experimental import pallas as pl
from jax.experimental.pallas import tpu as pltpu
from jax.sharding import PartitionSpec as P


FR = 3
KS_SHARP = 2.0
PENALTY = 3.0
FLOOR_MODULUS = 0.001
MOVE_LIMIT = 0.2
POISSON = 0.3
LEVEL_LOW = -14.0
LEVEL_HIGH = 14.0
FAN = 64
COARSE = (LEVEL_HIGH - LEVEL_LOW) / FAN
FINE = COARSE / FAN
SUB, LANE = 8, 128
GRANT = 8 * 1024 * 1024
F32 = jnp.float32
VMEM = pl.BlockSpec(memory_space=pltpu.VMEM)
SMEM = pl.BlockSpec(memory_space=pltpu.SMEM)


def tent_1d(values):
    padded = np.pad(values, FR - 1)
    n = len(values)
    return sum((FR - abs(o)) * padded[FR - 1 + o : FR - 1 + o + n] for o in range(1 - FR, FR))


def edge_tables(n):
    span = tent_1d(np.ones(n))
    return 1.0 / span, tent_1d(1.0 / span)


def along(position, n, table):
    middle = float(table[n // 2])
    value = jnp.where(position >= 0, F32(middle), F32(0.0))
    for k in range(2 * (FR - 1)):
        if abs(table[k] - middle) > 1e-12:
            value = jnp.where((position == k) | (position == n - 1 - k), F32(table[k]), value)
    return value


def iota(shape, axis):
    return lax.broadcasted_iota(jnp.int32, shape, axis)


def tent_lanes(v):
    lanes = iota(v.shape, v.ndim - 1)
    axis = v.ndim - 1
    total = 3.0 * v
    for o in (1, 2):
        above = jnp.where(lanes < LANE - o, pltpu.roll(v, LANE - o, axis), 0.0)
        below = jnp.where(lanes >= o, pltpu.roll(v, o, axis), 0.0)
        total = total + float(FR - o) * (above + below)
    return total


def forms(load, eigen, store, pairs, tiles):
    lame = POISSON / ((1.0 + POISSON) * (1.0 - 2.0 * POISSON))
    shear = 0.5 / (1.0 + POISSON)
    rows = tiles * SUB
    lanes = iota((rows, LANE), 1)
    for c in range(3):
        for a in (0, 1):
            u = load(c, a)
            up = jnp.where(lanes < LANE - 1, pltpu.roll(u, LANE - 1, 1), 0.0)
            pairs[c, a, 0, :rows] = up + u
            pairs[c, a, 1, :rows] = up - u
            pairs[c, a, :, rows:] = jnp.zeros((2, SUB, LANE), F32)
    eigen_v = jnp.full((SUB, LANE), eigen, F32)
    weight = jnp.exp(-KS_SHARP * eigen_v)
    eigen_weight = weight * eigen_v
    normal = lame + 2.0 * shear
    ms, md = 0.25, 1.0 / 12.0
    m0, m1, m2, m3 = ms**3, ms * ms * md, ms * md * md, md**3

    def tile(r, _):
        base = pl.multiple_of(r * SUB, SUB)
        coef = {}
        for c in range(3):
            planes = []
            for a in (0, 1):
                here = {}
                for z in (0, 1):
                    p0 = pairs[c, a, z, pl.ds(base, SUB)]
                    p1 = pairs[c, a, z, pl.ds(base + 1, SUB)]
                    here[0, z] = p1 + p0
                    here[1, z] = p1 - p0
                planes.append(here)
            for y in (0, 1):
                for z in (0, 1):
                    coef[c, 0, y, z] = planes[1][y, z] + planes[0][y, z]
                    coef[c, 1, y, z] = planes[1][y, z] - planes[0][y, z]
        groups = [None] * 6
        for c in range(3):
            for x in (0, 1):
                for y in (0, 1):
                    for z in (0, 1):
                        d = (x, y, z)
                        n = x + y + z
                        g = {0: 0, 1: 1 if d[c] else 2, 2: 3 if d[c] else 4, 3: 5}[n]
                        v = coef[c, x, y, z]
                        groups[g] = v * v if groups[g] is None else groups[g] + v * v
        mass = m0 * groups[0] + m1 * (groups[1] + groups[2]) + m2 * (groups[3] + groups[4]) + m3 * groups[5]
        stiff = (
            (12.0 * m1 * normal) * groups[1]
            + (12.0 * m1 * shear) * groups[2]
            + (12.0 * m2 * (normal + shear)) * groups[3]
            + (12.0 * m2 * 2.0 * shear) * groups[4]
            + (12.0 * m3 * (normal + 2.0 * shear)) * groups[5]
        )
        for third in (0, 1):
            along_sum = across_sum = None
            for i, j, k in ((0, 1, 2), (0, 2, 1), (1, 2, 0)):

                def at(c, di, dj):
                    d = [0, 0, 0]
                    d[i], d[j], d[k] = di, dj, third
                    return coef[c, d[0], d[1], d[2]]

                t = at(i, 1, 0) * at(j, 0, 1)
                s = at(i, 0, 1) * at(j, 1, 0)
                along_sum = t if along_sum is None else along_sum + t
                across_sum = s if across_sum is None else across_sum + s
            m = (ms, md)[third] * 0.25
            stiff = stiff + (2.0 * lame * m) * along_sum + (2.0 * shear * m) * across_sum
        store(r, weight * stiff, eigen_weight * mass)
        return 0

    lax.fori_loop(0, tiles, tile, 0, unroll=16)
    return weight


def pack(modes, design, out, sems):
    planes, rows = modes.shape[1], modes.shape[3]
    first = out.at[pl.ds(0, planes * rows)].reshape(planes, rows, LANE)
    last = out.at[pl.ds(planes * rows, 2 * SUB)].reshape(2, SUB, LANE)
    copies = [
        pltpu.make_async_copy(modes.at[0, :, 0], first, sems.at[0]),
        pltpu.make_async_copy(design, last, sems.at[1]),
    ]
    for copy in copies:
        copy.start()
    for copy in copies:
        copy.wait()


def tail_rows(packed, k):
    start = packed.shape[0] - (2 - k) * SUB
    return packed[start : start + SUB]


def plane_rows(packed, c, rows):
    return packed[c * rows : (c + 1) * rows]


def first_layer(modes, packed, eigen, out, upper, pairs, sems):
    planes, rows = modes.shape[1], modes.shape[3]
    first = upper.at[pl.ds(0, planes * rows)].reshape(planes, rows, LANE)
    copies = [pltpu.make_async_copy(modes.at[0, :, 1], first, sems.at[0])]
    for copy in copies:
        copy.start()
    for copy in copies:
        copy.wait()

    def store(r, stiff, mass):
        out[r, 0] = stiff
        out[r, 1] = mass

    tiles = out.shape[0]
    span = tiles * SUB

    def load(c, a):
        return plane_rows(upper if a else packed, c, span)

    forms(load, eigen[0], store, pairs, tiles)


def shifted_rows(v, o):
    rows = iota(v.shape, 0)
    moved = pltpu.roll(v, (-o) % SUB, 0)
    return jnp.where((rows + o >= 0) & (rows + o < SUB), moved, 0.0)


def edge_rows(first, second):
    up, down = [], []
    for f in (first, second):
        up += [2.0 * f[7:8] + f[6:7], f[7:8]]
        down += [f[0:1], 2.0 * f[0:1] + f[1:2]]
    return jnp.concatenate(up, 0), jnp.concatenate(down, 0)


def second_layer(packed, upper, eigen, got, before, _, out, rows, pairs, *, mode):
    def store(r, stiff, mass):
        out[r, 2] = stiff
        out[r, 3] = mass

    tiles = out.shape[0]
    span = tiles * SUB

    def load(c, a):
        return plane_rows(got if a else upper, c, span)

    m = lax.axis_index(mode)
    own = tail_rows(packed, 0), tail_rows(packed, 1)
    after = tail_rows(got, 0), tail_rows(got, 1)
    pair = across_x(own, before, after)
    up, down = edge_rows(*pair)
    for l in (0, 1):
        rows[l] = pair[l]
    weight = forms(load, eigen[0], store, pairs, tiles)
    half = SUB // 2
    for r in range(tiles):
        out[r, 4, :half] = jnp.where(m + 1 == r, up, weight[:half])
        out[r, 4, half:] = jnp.where(m - 1 == r, down, weight[half:])


def across_x(own, before, after):
    first = before[0] + 2.0 * before[1] + 3.0 * own[0] + 2.0 * own[1] + after[0]
    second = before[1] + 2.0 * own[0] + 3.0 * own[1] + 2.0 * after[0] + after[1]
    return first, second


def over_modes(got, at):
    total = got[0, at]
    for r in range(1, got.shape[0]):
        total = total + got[r, at]
    return total


def own_gradient(got, rows, out, *, slab, mode, sizes):
    total_x, total_y, total_z = sizes
    s, m = lax.axis_index(slab), lax.axis_index(mode)
    stiff = (over_modes(got, 0), over_modes(got, 2))
    mass = (over_modes(got, 1), over_modes(got, 3))
    tiles = got.shape[0]
    half = SUB // 2
    weight = None
    for r in range(tiles):
        w = jnp.where(m - 1 == r, got[r, 4, half : half + 1], got[r, 4, :1])
        weight = w if weight is None else weight + w
    inverse_weight = 1.0 / jnp.broadcast_to(weight, (SUB, LANE))
    from_last = jnp.where(m > 0, got[jnp.maximum(m - 1, 0), 4, :half], 0.0)
    from_next = jnp.where(m < tiles - 1, got[jnp.minimum(m + 1, tiles - 1), 4, half:], 0.0)
    inverse_yz = along(m * SUB + iota((SUB, LANE), 0), total_y, edge_tables(total_y)[0]) * along(
        iota((SUB, LANE), 1), total_z, edge_tables(total_z)[0]
    )
    for l in (0, 1):
        own = rows[l]
        near = jnp.concatenate(
            [from_last[2 * l : 2 * l + 2], jnp.zeros((4, LANE), F32), from_next[2 * l : 2 * l + 2]], 0
        )
        filtered = near
        for o in range(1 - FR, FR):
            filtered = filtered + float(FR - abs(o)) * (shifted_rows(own, o) if o else own)
        x = jnp.full((SUB, LANE), 2 * s + l, jnp.int32)
        inverse = inverse_yz * along(x, total_x, edge_tables(total_x)[0])
        density = tent_lanes(filtered) * inverse
        slope = (PENALTY * (1.0 - FLOOR_MODULUS)) * density * density
        out[l] = tent_lanes((slope * stiff[l] - mass[l]) * inverse_weight * inverse)


def gradient_copies(own, even, odd, packed, out, *, slab):
    is_even = lax.rem(lax.axis_index(slab), 2) == 0
    before = [jnp.where(is_even, odd[l], even[l]) for l in (0, 1)]
    after = [jnp.where(is_even, even[l], odd[l]) for l in (0, 1)]
    pair = across_x(own, before, after)
    for r in range(out.shape[0]):
        out[r, 0] = pair[0]
        out[r, 1] = pair[1]
        out[r, 2] = tail_rows(packed, 0)
        out[r, 3] = tail_rows(packed, 1)


def measure_xz(slab, total_x, total_z):
    s = lax.axis_index(slab)
    z = along(iota((SUB, LANE), 1), total_z, edge_tables(total_z)[1])
    return [
        z * along(jnp.full((SUB, LANE), 2 * s + l, jnp.int32), total_x, edge_tables(total_x)[1])
        for l in (0, 1)
    ]


def volumes(levels, gain, least, most, parts):
    count = gain.shape[0]
    for start in range(0, len(levels), 9):
        chunk = levels[start : start + 9]

        def body(v, totals):
            g, lo, hi = gain[v], least[v], most[v]
            return tuple(
                t + jnp.minimum(jnp.maximum(g * q, lo), hi) for t, q in zip(totals, chunk)
            )

        zeros = tuple(jnp.zeros((SUB, LANE), F32) for _ in chunk)
        totals = lax.fori_loop(0, count, body, zeros, unroll=32)
        for i, t in enumerate(totals):
            parts[start + i : start + i + 1] = jnp.sum(t, axis=0, keepdims=True)


def lane_totals(parts):
    column = jnp.sum(parts[...], axis=1, keepdims=True)
    shape = (FAN, LANE)
    mine = iota(shape, 0) == jnp.minimum(iota(shape, 1), FAN - 1)
    spread = jnp.where(mine, jnp.broadcast_to(column, shape), 0.0)
    return jnp.sum(spread, axis=0, keepdims=True)


def first_round(got, gain, least, most, own, out, padded, parts, *, slab, mode, sizes):
    total_x, total_y, total_z = sizes
    tiles = got.shape[0]
    m = lax.axis_index(mode)
    xz = measure_xz(slab, total_x, total_z)
    goal = jnp.zeros((SUB, LANE), F32)
    for l in (0, 1):
        padded[l, :SUB] = jnp.zeros((SUB, LANE), F32)
        padded[l, (tiles + 1) * SUB :] = jnp.zeros((SUB, LANE), F32)
        for r in range(tiles):
            padded[l, (r + 1) * SUB : (r + 2) * SUB] = got[r, l]
    for l in (0, 1):
        for r in range(tiles):
            total = None
            for o in range(1 - FR, FR):
                start = (r + 1) * SUB + o
                t = float(FR - abs(o)) * padded[l, start : start + SUB]
                total = t if total is None else total + t
            y = along(r * SUB + iota((SUB, LANE), 0), total_y, edge_tables(total_y)[1])
            measure = xz[l] * y
            design = got[r, 2 + l]
            at = l * tiles + r
            gain[at] = design * jnp.sqrt(jnp.maximum(total, 0.0) * measure)
            least[at] = jnp.maximum(design - MOVE_LIMIT, 0.0) * measure
            most[at] = jnp.minimum(design + MOVE_LIMIT, 1.0) * measure
            goal = goal + design * measure
        total = None
        for o in range(1 - FR, FR):
            t = float(FR - abs(o)) * padded[l, pl.ds(m * SUB + SUB + o, SUB)]
            total = t if total is None else total + t
        own[l] = total
    levels = [float(np.exp(-0.5 * (LEVEL_LOW + COARSE * (i + 1)))) for i in range(FAN - 1)]
    volumes(levels, gain, least, most, parts)
    parts[FAN - 1 : FAN] = jnp.sum(goal, axis=0, keepdims=True)
    row = lane_totals(parts)
    for k in range(out.shape[0]):
        out[k] = row


def added(got):
    rows = [got[k] for k in range(got.shape[0])]
    while len(rows) > 1:
        rows = [a + b for a, b in zip(rows[::2], rows[1::2])] + rows[len(rows) & ~1 :]
    return rows[0]


def cells_above(row, goal):
    above = (row > goal) & (iota(row.shape, 1) < FAN - 1)
    return jnp.sum(jnp.where(above, 1.0, 0.0), axis=1, keepdims=True)


def second_round(got, gain, least, most, out, state, parts):
    row = added(got)
    goal = pltpu.roll(row, LANE - FAN, 1)
    low = LEVEL_LOW + COARSE * cells_above(row, goal)
    state[0:1] = jnp.broadcast_to(low, (1, LANE))
    state[1:2] = goal
    scale = jnp.exp(-0.5 * jnp.broadcast_to(low, (SUB, LANE)))
    levels = [scale * float(np.exp(-0.5 * FINE * (i + 1))) for i in range(FAN - 1)]
    volumes(levels, gain, least, most, parts)
    parts[FAN - 1 : FAN] = jnp.zeros((1, LANE), F32)
    row = lane_totals(parts)
    for k in range(out.shape[0]):
        out[k] = row


def last_update(got, state, own, design, sens_out, out, *, slab, mode, sizes):
    total_x, total_y, total_z = sizes
    m = lax.axis_index(mode)
    row = added(got)
    goal = state[1:2]
    level = state[0:1, 0:1] + FINE * (cells_above(row, goal) + 0.5)
    scale = jnp.exp(jnp.broadcast_to(level, (SUB, LANE)))
    y = along(m * SUB + iota((SUB, LANE), 0), total_y, edge_tables(total_y)[1])
    xz = measure_xz(slab, total_x, total_z)
    for l in (0, 1):
        d, s = design[l], own[l]
        factor = jnp.sqrt(jnp.maximum(s, 0.0) / (scale * (xz[l] * y)))
        least = jnp.maximum(d - MOVE_LIMIT, 0.0)
        most = jnp.minimum(d + MOVE_LIMIT, 1.0)
        out[l] = jnp.minimum(jnp.maximum(d * factor, least), most)
        sens_out[l] = s


def call(kernel, outs, operands, specs=None, scratch=(), flops=1000, alias=None):
    outs = [jax.ShapeDtypeStruct(o, F32) for o in outs]
    size = sum(4 * int(np.prod(o.shape)) for o in (*outs, *operands))
    single = len(outs) == 1
    return pl.pallas_call(
        kernel,
        out_shape=outs[0] if single else outs,
        in_specs=specs or [VMEM] * len(operands),
        out_specs=VMEM if single else [VMEM] * len(outs),
        scratch_shapes=[pltpu.VMEM(s, F32) for s in scratch],
        cost_estimate=pl.CostEstimate(flops=flops, bytes_accessed=size, transcendentals=0),
        input_output_aliases=alias or {},
        compiler_params=pltpu.CompilerParams(vmem_limit_bytes=GRANT),
    )(*operands)


def from_before(value, axis):
    count = lax.axis_size(axis)
    return lax.ppermute(value, axis, [(i, i + 1) for i in range(count - 1)])


def from_after(value, axis):
    count = lax.axis_size(axis)
    return lax.ppermute(value, axis, [(i + 1, i) for i in range(count - 1)])


def swapped(value, axis, first):
    pairs = []
    for i in range(first, lax.axis_size(axis) - 1, 2):
        pairs += [(i, i + 1), (i + 1, i)]
    return lax.ppermute(value, axis, pairs)


def exchange(value, axis):
    return lax.all_to_all(value, axis, 0, 0, tiled=True)


def local(design, mode_shapes, eigenvalues):
    slab, mode = "slab", "mode"
    slabs, modes = lax.axis_size(slab), lax.axis_size(mode)
    _, _, _, total_y, total_z = mode_shapes.shape
    sizes = (2 * slabs, total_y, total_z)
    pairs = (3, 2, 2, total_y + SUB, LANE)
    block = (2, SUB, LANE)
    padded = (2, total_y + 2 * SUB, LANE)
    place = dict(slab=slab, mode=mode, sizes=sizes)

    held = pltpu.with_memory_space_constraint(mode_shapes, pltpu.HBM)
    params = pltpu.CompilerParams(vmem_limit_bytes=GRANT)
    hbm = pl.BlockSpec(memory_space=pltpu.HBM)
    packed = pl.pallas_call(
        pack,
        out_shape=jax.ShapeDtypeStruct((3 * total_y + 2 * SUB, LANE), F32),
        in_specs=[hbm, hbm],
        out_specs=VMEM,
        scratch_shapes=[pltpu.SemaphoreType.DMA((2,))],
        compiler_params=params,
        name="pack",
    )(held, pltpu.with_memory_space_constraint(design, pltpu.HBM))
    got = from_after(packed, slab)
    before = from_before(design, slab)
    sent, upper = pl.pallas_call(
        first_layer,
        out_shape=[
            jax.ShapeDtypeStruct((modes, 5, SUB, LANE), F32),
            jax.ShapeDtypeStruct((3 * total_y, LANE), F32),
        ],
        in_specs=[hbm, VMEM, SMEM],
        out_specs=[VMEM, VMEM],
        scratch_shapes=[pltpu.VMEM(pairs, F32), pltpu.SemaphoreType.DMA((1,))],
        cost_estimate=pl.CostEstimate(flops=5_000_000, bytes_accessed=600_000, transcendentals=0),
        compiler_params=params,
        name="first_layer",
    )(held, packed, eigenvalues)
    sent, rows = call(
        functools.partial(second_layer, mode=mode),
        [(modes, 5, SUB, LANE), block],
        [packed, upper, eigenvalues, got, before, sent],
        specs=[VMEM, VMEM, SMEM, VMEM, VMEM, VMEM],
        scratch=[pairs],
        flops=5_000_000,
        alias={5: 0},
    )
    early = exchange(sent, mode)
    gradient = call(functools.partial(own_gradient, **place), [block], [early, rows])
    even = swapped(gradient, slab, 0)
    odd = swapped(gradient, slab, 1)
    copies = call(
        functools.partial(gradient_copies, slab=slab),
        [(modes, 4, SUB, LANE)],
        [gradient, even, odd, packed],
    )
    whole = exchange(copies, mode)
    vectors = (2 * modes, SUB, LANE)
    gain, least, most, own, sent = call(
        functools.partial(first_round, **place),
        [vectors, vectors, vectors, block, (slabs, 1, LANE)],
        [whole],
        scratch=[padded, (FAN, LANE)],
    )
    got = exchange(sent, slab)
    sent, state = call(
        second_round,
        [(slabs, 1, LANE), (SUB, LANE)],
        [got, gain, least, most],
        scratch=[(FAN, LANE)],
    )
    got = exchange(sent, slab)
    return call(functools.partial(last_update, **place), [block, block], [got, state, own, design])


def solution(mesh):
    in_specs = (P("slab", "mode", None), P("mode", None, "slab", None, None), P("mode"))
    out_specs = (P("slab", "mode", None), P("slab", "mode", None))

    def step(design, mode_shapes, eigenvalues):
        return tuple(local(design, mode_shapes, eigenvalues))

    return jax.shard_map(step, mesh=mesh, in_specs=in_specs, out_specs=out_specs, check_vma=False)
```
